32 devices in a mesh: pairs: 2 (over y), col: 4 (over z), row: 4 (over x, core).
Axes of the slice: x: 2, y: 2, z: 4, core: 2. Of those that a mesh axis runs over, the one named last changes fastest.
Arguments:
- images: float32 [4, 8, 64, 512], P('pairs', None, 'row', 'col'), parts along dimension 0, may hold values from -12 to 12
- conv_weight: bfloat16 [32, 72], replicated, may hold values from -0.75 to 0.75
- conv_bias: float32 [32], replicated, may hold values from -2.5 to 2.5
- agg_weight: float32 [8, 27], replicated, may hold values from -3.2 to 3.2
Outputs:
- disparity: float32 [128, 512], P(('pairs', 'row'), 'col'), parts along dimension 0
The draws below stay inside these ranges and needn't reach their ends.
There are 2 independent parts, one for each index of `pairs`. The reference program is written for one: setup_inputs(seed, part) draws one part's arguments, and reference() takes and returns one part's arrays. A program takes and returns all parts, laid end to end along the dimension named above; an argument that names none is the same for every part. Nothing has to cross between parts.
All inputs are finite; a program needn't handle non-finite values.
Results may differ from the reference program's by a relative error of at most 0.012.
The reference program's roundings to bfloat16 on the way count: a program that leaves them out, or rounds other values in their place, can miss the bound.
Values may be sent and summed in bfloat16 or wider, within the bound.
A program may use at most 64 MiB of HBM per device.

```python
import jax
import jax.numpy as jnp
from jax import lax

CIN = 8
F = 32
G = 8
D = 64
DB = 16
H = 64
W = 512


def draw_images(key, part):
    values = jax.random.normal(key, (2, CIN, H, W), jnp.float32)
    return jnp.clip(values, -12.0, 12.0)


def centred(key, shape, deviation, most, kind=jnp.bfloat16):
    array = jax.random.normal(key, shape, jnp.float32) * deviation
    return jnp.minimum(jnp.maximum(array, -most), most).astype(kind)


def setup_inputs(seed: int = 0, part: int = 0) -> dict:
    seeds = jax.random.split(jax.random.key(seed), 5)
    own_keys = jax.random.split(jax.random.fold_in(seeds[4], part), 5)
    images = draw_images(jax.random.fold_in(jax.random.fold_in(seeds[4], part), 71), part)
    conv_weight = centred(seeds[1], (F, 9 * CIN), (9 * CIN) ** -0.5, 0.75)
    conv_bias = centred(seeds[2], (F,), 0.5, 2.5, jnp.float32)
    agg_weight = centred(seeds[3], (G, 27), 0.8, 3.2, jnp.float32)
    return {"images": images, "conv_weight": conv_weight, "conv_bias": conv_bias, "agg_weight": agg_weight}


def conv_valid(picture, conv_weight, conv_bias):
    height = picture.shape[1] - 2
    width_out = picture.shape[2] - 2
    patches = jnp.concatenate([picture[:, step_y:step_y + height, step_x:step_x + width_out] for step_y in range(3) for step_x in range(3)], axis=0)
    flattened = patches.reshape(patches.shape[0], height * width_out)
    summed = jnp.dot(conv_weight, flattened, preferred_element_type=jnp.float32) + conv_bias[:, None]
    return jax.nn.leaky_relu(summed, 0.1).reshape(conv_weight.shape[0], height, width_out)


def block_costs(left_feat, right_full, start_d, search, block_depth, groups):
    channels, height, width_out = left_feat.shape
    window = lax.dynamic_slice_in_dim(right_full, search - start_d - block_depth, width_out + block_depth + 1, 2)
    left_grouped = left_feat.reshape(groups, channels // groups, height, width_out)
    layers = []
    for offset in range(block_depth + 2):
        shifted = window[:, :, block_depth + 1 - offset:block_depth + 1 - offset + width_out]
        product = jnp.einsum("gcyx,gcyx->gyx", left_grouped, shifted.reshape(groups, channels // groups, height, width_out), preferred_element_type=jnp.float32) * (groups / channels)
        disparity = start_d - 1 + offset
        usable = jnp.logical_and(disparity >= 0, disparity < search).astype(jnp.float32)
        layers.append((product * usable).astype(jnp.bfloat16))
    return jnp.stack(layers, axis=1)


def aggregate(cost_block, agg_weight, block_depth, height, width_out):
    tapped = jnp.einsum("gdyx,gk->kdyx", cost_block.astype(jnp.float32), agg_weight, precision=lax.Precision.HIGHEST)
    summed = jnp.zeros((block_depth, height, width_out), jnp.float32)
    for step_d in range(3):
        for step_y in range(3):
            for step_x in range(3):
                summed = summed + tapped[9 * step_d + 3 * step_y + step_x, step_d:step_d + block_depth, step_y:step_y + height, step_x:step_x + width_out]
    return summed


def softmax_update(running, scores, start_d):
    running_max, running_sum, running_moment = running
    values = (start_d + lax.iota(jnp.int32, scores.shape[0])).astype(jnp.float32)
    new_max = jnp.maximum(running_max, jnp.max(scores, axis=0))
    rescale = jnp.exp(running_max - new_max)
    weights = jnp.exp(scores - new_max[None])
    return (new_max, running_sum * rescale + jnp.sum(weights, axis=0), running_moment * rescale + jnp.sum(weights * values[:, None, None], axis=0))


def reference(images, conv_weight, conv_bias, agg_weight):
    pictures = images.astype(jnp.bfloat16)
    padded = jnp.pad(pictures, ((0, 0), (0, 0), (1, 1), (1, 1)))
    left_feat = conv_valid(padded[0], conv_weight, conv_bias).astype(jnp.bfloat16)
    right_feat = conv_valid(padded[1], conv_weight, conv_bias).astype(jnp.bfloat16)
    channels = left_feat.shape[0]
    right_full = jnp.concatenate([jnp.zeros((channels, H, D), jnp.bfloat16), right_feat, jnp.zeros((channels, H, 1), jnp.bfloat16)], axis=2)

    def advance(running, block_index):
        start_d = block_index * DB
        cost_block = block_costs(left_feat, right_full, start_d, D, DB, G)
        cost_block = jnp.pad(cost_block, ((0, 0), (0, 0), (1, 1), (1, 1)))
        scores = aggregate(cost_block, agg_weight, DB, H, W)
        return softmax_update(running, scores, start_d), None

    initial = (jnp.full((H, W), -1e30, jnp.float32), jnp.zeros((H, W), jnp.float32), jnp.zeros((H, W), jnp.float32))
    running, unused = lax.scan(advance, initial, jnp.arange(D // DB, dtype=jnp.int32))
    return running[2] / running[1] / D
```

```python
import functools

import jax
import jax.numpy as jnp
from jax import lax
from jax.experimental import pallas as pl
from jax.experimental.pallas import tpu as pltpu
from jax.sharding import PartitionSpec as P

D = 64


MESH = pl.DeviceIdType.MESH
STEPS = ((0, 1), (0, -1), (1, 0), (-1, 0), (1, 1), (1, -1), (-1, 1), (-1, -1))


def body(
    shape, images_hbm, weight_hbm, bias_hbm, agg_hbm, out_ref,
    images_ref, weight_ref, bias_in, agg_in, load_sem, pt, wc, amat, lf, rf, raw, cost, acc, score, tr_ref, edge_ref, near0, near1, far, lines, send_sem, recv_sem,
):
    rows, cols, groups, per, cin = shape
    lanes = wc.shape[2] // per
    lead = D + 8
    span = rf.shape[1]
    tiles = lanes // 128
    rows_axis, cols_axis = lax.axis_size("row"), lax.axis_size("col")
    my_row, my_col = lax.axis_index("row"), lax.axis_index("col")
    total_rows = rows * rows_axis
    total_cols = cols * cols_axis
    top = my_row * rows - 1
    left = my_col * cols
    reach = near1.shape[0]
    skew = 128 // (2 * groups)

    def row_of(lane):
        beside = jnp.where((lane // groups) % 2 == 0, 0, rows + 1)
        return jnp.where(lane < rows * groups, lane // groups + 1, beside)

    def skew_of(lane):
        return (lane - rows * groups) // (2 * groups)


    def exists(step):
        r, c = my_row + step[0], my_col + step[1]
        return (r >= 0) & (r < rows_axis) & (c >= 0) & (c < cols_axis)

    def device(step):
        return {"row": my_row + step[0], "col": my_col + step[1]}

    barrier = pltpu.get_barrier_semaphore()
    for step in STEPS:

        @pl.when(exists(step))
        def _(step=step):
            pl.semaphore_signal(barrier, inc=1, device_id=device(step), device_id_type=MESH)

    loads = [
        pltpu.make_async_copy(source, target, load_sem.at[k])
        for k, (source, target) in enumerate(
            ((images_hbm, images_ref), (weight_hbm, weight_ref), (bias_hbm, bias_in), (agg_hbm, agg_in))
        )
    ]
    for load in loads:
        load.start()
    for load in loads:
        load.wait()

    main = rows * cin
    for image in range(2):
        flat = images_ref[image].reshape(main, cols)
        tr_ref[image] = flat.T.astype(jnp.bfloat16)
        for side, first in ((0, 0), (1, rows - 2)):
            pair = [images_ref[image, :, first + y, :] for y in range(2)]
            edge_ref[side, image * 2 * cin : (image + 1) * 2 * cin, :] = jnp.concatenate(
                pair, axis=0
            ).astype(jnp.bfloat16)

    spread_at = lax.broadcasted_iota(jnp.int32, (groups * per, lanes), 1) % groups * per
    spread_from = lax.broadcasted_iota(jnp.int32, (groups * per, lanes), 0)
    tn = (((0,), (0,)), ((), ()))
    weight = weight_ref[...].astype(jnp.float32)
    q, bias = [], []
    for ch in range(per):
        spread = (spread_from == spread_at + ch).astype(jnp.float32)
        q.append(
            lax.dot_general(weight, spread, tn, preferred_element_type=jnp.float32)
        )
        bias.append(
            jnp.dot(
                bias_in[...], spread,
                precision=lax.Precision.HIGHEST, preferred_element_type=jnp.float32,
            )
        )
    one = (
        lax.broadcasted_iota(jnp.int32, (groups, lanes), 0)
        == lax.broadcasted_iota(jnp.int32, (groups, lanes), 1) % groups
    ).astype(jnp.float32)
    agg = lax.dot_general(
        agg_in[...], one, tn,
        precision=lax.Precision.HIGHEST, preferred_element_type=jnp.float32,
    )

    lane = lax.broadcasted_iota(jnp.int32, (rows, lanes), 1)
    off = row_of(lane) - lax.broadcasted_iota(jnp.int32, (rows, lanes), 0)
    group_main = rows * groups
    part_of = skew_of(lane)
    for step_d in range(3):
        for step_x in range(3):
            value = jnp.zeros((rows, lanes), jnp.float32)
            for step_y in range(3):
                k = 9 * step_d + 3 * step_y + step_x
                value = jnp.where(off == step_y, agg[k : k + 1, :], value)
            high = value.astype(jnp.bfloat16)
            low = (value - high.astype(jnp.float32)).astype(jnp.bfloat16)
            at = (step_d * 3 + step_x) * 2 * rows
            for v, value in enumerate((high, low)):
                begin = at + v * rows
                amat[0, begin : begin + rows, :] = value[:, :group_main]
                for ds in range(skew):
                    own = jnp.where(part_of == ds, value.astype(jnp.float32), 0.0)
                    amat[1 + ds, begin : begin + rows, :] = own[:, group_main:].astype(jnp.bfloat16)

    tall = 1 + (my_row > 0).astype(jnp.int32) + (my_row < rows_axis - 1).astype(jnp.int32)
    wide = 1 + (my_col > 0).astype(jnp.int32) + (my_col < cols_axis - 1).astype(jnp.int32)
    pl.semaphore_wait(barrier, tall * wide - 1)

    plan = [
        ((0, 1), tr_ref.at[1, pl.ds(cols - reach, reach), :], near1),
        ((0, 1), tr_ref.at[0, pl.ds(cols - 16, 16), :], near0),
        ((0, -1), tr_ref.at[:, pl.ds(0, 16), :], far),
    ]
    for r in (1, -1):
        side = 0 if r == 1 else 1
        for c in (0, 1, -1):
            plan.append(((r, c), edge_ref.at[1 - side], lines.at[side, 1 - c]))
    copies = []
    for k, (step, source, target) in enumerate(plan):
        copy = pltpu.make_async_remote_copy(
            src_ref=source,
            dst_ref=target,
            send_sem=send_sem.at[k],
            recv_sem=recv_sem.at[k],
            device_id=device(step),
            device_id_type=MESH,
        )
        copies.append((step, copy))

        @pl.when(exists(step))
        def _(copy=copy):
            copy.start()

        @pl.when(jnp.logical_not(exists((-step[0], -step[1]))))
        def _(target=target):
            target[...] = jnp.zeros(target.shape, target.dtype)

    lane_row = row_of(lax.broadcasted_iota(jnp.int32, (rows, lanes), 1))
    line_off = lane_row - lax.broadcasted_iota(jnp.int32, (rows, lanes), 0)
    near_row = lane_row[:cin]
    for step_x in range(3):
        for ch in range(per):
            columns = slice(ch * lanes, (ch + 1) * lanes)
            taps = []
            for step_y in range(3):
                base = (step_y * 3 + step_x) * cin
                taps.append(q[ch][base : base + cin, :])
            for c in range(cin):
                value = jnp.zeros((rows, lanes), jnp.float32)
                for step_y in range(3):
                    value = jnp.where(line_off == 2 - step_y, taps[step_y][c : c + 1, :], value)
                wc[step_x, c * rows : (c + 1) * rows, columns] = value.astype(jnp.bfloat16)
            for pair in range(2):
                halves = []
                for line in ((0, 1), (rows + 2, rows + 3))[pair]:
                    value = jnp.zeros((cin, lanes), jnp.float32)
                    for step_y in range(3):
                        value = jnp.where(near_row == line - step_y, taps[step_y], value)
                    halves.append(value)
                begin = main + pair * 2 * cin
                wc[step_x, begin : begin + 2 * cin, columns] = (
                    jnp.concatenate(halves, axis=0).astype(jnp.bfloat16)
                )
    used = (rows + 4) * cin
    if used < lanes:
        wc[:, used:, :] = jnp.zeros((3, lanes - used, per * lanes), jnp.bfloat16)

    acc[...] = jnp.zeros_like(acc)
    base = 16 + D
    pt[:, base : base + cols, 0:main] = tr_ref[...].astype(jnp.float32)

    for step, copy in copies:

        @pl.when(exists((-step[0], -step[1])))
        def _(copy=copy):
            copy.wait_recv()

    base = 16 + D
    pt[1, base - reach : base, 0:main] = near1[...].astype(jnp.float32)
    pt[0, base - 16 : base, 0:main] = near0[...].astype(jnp.float32)
    pt[:, base + cols : base + cols + 16, 0:main] = far[...].astype(jnp.float32)
    half = 2 * cin
    for image in range(2):
        for place in range(3):
            block = jnp.concatenate(
                [
                    lines[side, place, image * half : (image + 1) * half, :].astype(jnp.float32)
                    for side in range(2)
                ]
                + [jnp.zeros((lanes - main - 2 * half, cols), jnp.float32)],
                axis=0,
            )
            block = block.T
            if place == 0:
                pt[image, base - reach : base, main:] = block[cols - reach :, :]
            elif place == 1:
                pt[image, base : base + cols, main:] = block
            else:
                pt[image, base + cols : base + cols + 16, main:] = block[:16, :]

    def features(image, first, count, store, scale):
        row_ids = left + first - lead + lax.broadcasted_iota(jnp.int32, (count, lanes), 0)
        line = top + row_of(lax.broadcasted_iota(jnp.int32, (count, lanes), 1))
        keep = (row_ids >= 0) & (row_ids < total_cols) & (line >= 0) & (line < total_rows)
        parts = [
            pt[image, 7 + step_x + first : 7 + step_x + first + count, :].astype(jnp.bfloat16)
            for step_x in range(3)
        ]
        for ch in range(per):
            summed = jnp.broadcast_to(bias[ch], (count, lanes))
            total = None
            for step_x in range(3):
                term = jnp.dot(
                    parts[step_x],
                    wc[step_x, :, ch * lanes : (ch + 1) * lanes],
                    preferred_element_type=jnp.float32,
                )
                total = term if total is None else total + term
            summed = total + summed
            feat = jnp.where(summed >= 0, summed, summed * 0.1)
            feat = feat.astype(jnp.bfloat16).astype(jnp.float32)
            feat = jnp.where(keep, feat * scale, 0.0)
            for tile in range(tiles):
                store[ch * tiles + tile, :, :] = feat[:, tile * 128 : (tile + 1) * 128]

    features(0, lead - 8, cols + 16, lf, 1.0 / per)
    features(1, 0, span, rf, 1.0)

    apart = skew_of(lax.broadcasted_iota(jnp.int32, (span, 128), 1) + group_main)
    for ch in range(per):
        raw[ch, 0:8, :] = jnp.zeros((8, 128), jnp.float32)
        value = rf[ch * tiles + 1, :, :]
        raw[ch, 8 : 8 + span, :] = value
        for ds in range(1, skew):
            value = jnp.where(apart == ds, raw[ch, 8 - ds : 8 - ds + span, :], value)
        rf[ch * tiles + 1, :, :] = value

    edges = []
    for at, begin in ((7, lead - D), (8 + cols, lead + cols - D + 1)):
        parts = []
        for tile in range(tiles):
            total = None
            for ch in range(per):
                k = ch * tiles + tile
                term = lf[k, at : at + 1, :] * rf[k, begin : begin + D, :]
                total = term if total is None else total + term
            parts.append(total.astype(jnp.bfloat16))
        edges.append(jnp.concatenate(parts, axis=1))
    edge = jnp.concatenate(edges, axis=0)
    nt = (((1,), (1,)), ((), ()))
    main_a = amat[0]
    side = lax.dot_general(
        jnp.concatenate([main_a, amat[1]], axis=1), edge, nt, preferred_element_type=jnp.float32
    )
    place = lax.broadcasted_iota(jnp.int32, (rows, 2 * D), 1)
    within = jnp.where(place >= D, place - D, place)
    border = None
    for step_d in range(3):
        pick = []
        for step_x in (0, 2):
            at = (step_d * 3 + step_x) * 2 * rows
            pick.append(side[at : at + rows, :] + side[at + rows : at + 2 * rows, :])
        value = jnp.where(place < D, pick[0], pick[1])
        if step_d == 0:
            value = jnp.where(within == D - 1, 0.0, pltpu.roll(value, 2 * D - 1, 1))
        elif step_d == 2:
            value = jnp.where(within == 0, 0.0, pltpu.roll(value, 1, 1))
        border = value if border is None else border + value

    def product(tile, chunk, d):
        total = None
        for ch in range(per):
            k = ch * tiles + tile
            term = (
                lf[k, 8 + chunk * 16 : 24 + chunk * 16, :]
                * rf[k, pl.ds(lead + chunk * 16 - d, 16), :]
            )
            total = term if total is None else total + term
        return total.astype(jnp.bfloat16)

    def band(block, carry):
        d0 = block * 2 * skew
        beside = []
        for p in range(2):
            for chunk in range(cols // 16):
                beside.append(product(1, chunk, d0 + p * skew))
        cost[0, :, group_main:] = jnp.concatenate(beside, axis=0)
        held = {}
        for ds in range(skew):
            for p in range(2):
                for chunk in range(cols // 16):
                    at = p * cols + chunk * 16
                    cost[ds, at : at + 16, :group_main] = product(0, chunk, d0 + p * skew + ds)
            stack = jnp.concatenate([cost[ds, :, :group_main], cost[0, :, group_main:]], axis=1)
            weights = jnp.concatenate([amat[0], amat[1 + ds]], axis=1)
            got = lax.dot_general(weights, stack, nt, preferred_element_type=jnp.float32)
            for step_x in range(3):
                for p in range(2):
                    for step_d in range(3):
                        at = (step_d * 3 + step_x) * 2 * rows
                        columns = slice(p * cols, (p + 1) * cols)
                        value = got[at : at + rows, columns] + got[at + rows : at + 2 * rows, columns]
                        key = (step_x, p, ds + 2 - step_d)
                        held[key] = held[key] + value if key in held else value
                    done = [ds] if ds < skew - 1 else [ds, ds + 1, ds + 2]
                    for o in done:
                        acc[step_x, d0 + p * skew + o, :, :] += held.pop((step_x, p, o))
        return carry

    lax.fori_loop(0, D // (2 * skew), band, 0, unroll=2)

    lane = lax.broadcasted_iota(jnp.int32, (rows, cols), 1)

    def finish(d, best):
        before = jnp.where(
            lane == 0,
            pltpu.roll(border, lax.rem(d + D + 1, 2 * D), 1),
            pltpu.roll(acc[0, d + 1, :, :], 1, 1),
        )
        after = jnp.where(
            lane == cols - 1, pltpu.roll(border, d, 1), pltpu.roll(acc[2, d + 1, :, :], cols - 1, 1)
        )
        value = acc[1, d + 1, :, :] + before + after
        score[d, :, :] = value
        return jnp.maximum(best, value)

    best = lax.fori_loop(0, D, finish, jnp.full((rows, cols), -jnp.inf, jnp.float32), unroll=16)

    def weigh(d, carry):
        total, moment = carry
        weight = jnp.exp(score[d, :, :] - best)
        return total + weight, moment + weight * d.astype(jnp.float32)

    zero = jnp.zeros((rows, cols), jnp.float32)
    total, moment = lax.fori_loop(0, D, weigh, (zero, zero), unroll=16)
    out_ref[...] = moment / total / D

    for step, copy in copies:

        @pl.when(exists(step))
        def _(copy=copy):
            copy.wait_send()


def on_device(images, conv_weight, conv_bias, agg_weight):
    cin, rows, cols = images.shape[1:]
    groups = agg_weight.shape[0]
    per = conv_weight.shape[0] // groups
    main = rows * cin
    lanes = main + 128
    span = cols + D + 16
    reach = -(-(D + 2) // 16) * 16
    return pl.pallas_call(
        functools.partial(body, (rows, cols, groups, per, cin)),
        out_shape=pltpu.VMEM((rows, cols), jnp.float32),
        in_specs=[pl.BlockSpec(memory_space=pl.ANY)] * 4,
        out_specs=pl.BlockSpec(memory_space=pltpu.VMEM),
        scratch_shapes=[
            pltpu.VMEM(images.shape, images.dtype),
            pltpu.VMEM(conv_weight.shape, conv_weight.dtype),
            pltpu.VMEM((1,) + conv_bias.shape, conv_bias.dtype),
            pltpu.VMEM(agg_weight.shape, agg_weight.dtype),
            pltpu.SemaphoreType.DMA((4,)),
            pltpu.VMEM((2, span + 16, lanes), jnp.float32),
            pltpu.VMEM((3, lanes, per * lanes), jnp.bfloat16),
            pltpu.VMEM((1 + 64 // groups, 18 * rows, 128), jnp.bfloat16),
            pltpu.VMEM((per * (lanes // 128), cols + 16, 128), jnp.float32),
            pltpu.VMEM((per * (lanes // 128), span, 128), jnp.float32),
            pltpu.VMEM((per, span + 8, 128), jnp.float32),
            pltpu.VMEM((64 // groups, 2 * cols, lanes), jnp.bfloat16),
            pltpu.VMEM((3, D + 2, rows, cols), jnp.float32),
            pltpu.VMEM((D, rows, cols), jnp.float32),
            pltpu.VMEM((2, cols, main), jnp.bfloat16),
            pltpu.VMEM((2, 4 * cin, cols), jnp.bfloat16),
            pltpu.VMEM((16, main), jnp.bfloat16),
            pltpu.VMEM((reach, main), jnp.bfloat16),
            pltpu.VMEM((2, 16, main), jnp.bfloat16),
            pltpu.VMEM((2, 3, 4 * cin, cols), jnp.bfloat16),
            pltpu.SemaphoreType.DMA((9,)),
            pltpu.SemaphoreType.DMA((9,)),
        ],
        compiler_params=pltpu.CompilerParams(collective_id=0, has_side_effects=True),
    )(images, conv_weight, conv_bias[None], agg_weight)


def solution(mesh):
    in_specs = (P("pairs", None, "row", "col"), P(), P(), P())
    out_specs = P(("pairs", "row"), "col")
    return jax.shard_map(
        on_device, mesh=mesh, in_specs=in_specs, out_specs=out_specs, check_vma=False
    )
```

```python
import functools

import jax
import jax.numpy as jnp
from jax import lax
from jax.experimental import pallas as pl
from jax.experimental.pallas import tpu as pltpu
from jax.sharding import PartitionSpec as P

D = 64
LOG2E = 1.4426950408889634


MESH = pl.DeviceIdType.MESH
STEPS = ((0, 1), (0, -1), (1, 0), (-1, 0), (1, 1), (1, -1), (-1, 1), (-1, -1))


def body(
    shape, images_hbm, weight_hbm, bias_hbm, agg_hbm, out_ref,
    images_ref, weight_ref, bias_in, agg_in, load_sem,
    pt, ext, lhs, wc, amat, taps_ref, band_w, mask, lf, rf, left_m, right_m, part,
    tr_ref, edge_ref, near0, near1, far, lines, send_sem, recv_sem,
):
    rows, cols, groups, per, cin = shape
    feats = groups * per
    pairs = rows // 2
    lead = D + 8
    span = rf.shape[1]
    wide_l = lf.shape[1]
    rows_axis, cols_axis = lax.axis_size("row"), lax.axis_size("col")
    my_row, my_col = lax.axis_index("row"), lax.axis_index("col")
    reach = near1.shape[0]

    def exists(step):
        r, c = my_row + step[0], my_col + step[1]
        return (r >= 0) & (r < rows_axis) & (c >= 0) & (c < cols_axis)

    def device(step):
        return {"row": my_row + step[0], "col": my_col + step[1]}

    barrier = pltpu.get_barrier_semaphore()
    for step in STEPS:

        @pl.when(exists(step))
        def _(step=step):
            pl.semaphore_signal(barrier, inc=1, device_id=device(step), device_id_type=MESH)

    loads = [
        pltpu.make_async_copy(source, target, load_sem.at[k])
        for k, (source, target) in enumerate(
            ((images_hbm, images_ref), (weight_hbm, weight_ref), (bias_hbm, bias_in), (agg_hbm, agg_in))
        )
    ]
    for load in loads:
        load.start()
    for load in loads:
        load.wait()

    main = rows * cin
    for image in range(2):
        flat = images_ref[image].reshape(main, cols)
        tr_ref[image] = flat.T.astype(jnp.bfloat16)
        for side, first in ((0, 0), (1, rows - 2)):
            pair = [images_ref[image, :, first + y, :] for y in range(2)]
            edge_ref[side, image * 2 * cin : (image + 1) * 2 * cin, :] = jnp.concatenate(
                pair, axis=0
            ).astype(jnp.bfloat16)

    tall = 1 + (my_row > 0).astype(jnp.int32) + (my_row < rows_axis - 1).astype(jnp.int32)
    wide = 1 + (my_col > 0).astype(jnp.int32) + (my_col < cols_axis - 1).astype(jnp.int32)
    pl.semaphore_wait(barrier, tall * wide - 1)

    plan = [
        ((0, 1), tr_ref.at[1, pl.ds(cols - reach, reach), :], near1),
        ((0, 1), tr_ref.at[0, pl.ds(cols - 16, 16), :], near0),
        ((0, -1), tr_ref.at[:, pl.ds(0, 16), :], far),
    ]
    for r in (1, -1):
        side = 0 if r == 1 else 1
        for c in (0, 1, -1):
            plan.append(((r, c), edge_ref.at[1 - side], lines.at[side, 1 - c]))
    copies = []
    for k, (step, source, target) in enumerate(plan):
        copy = pltpu.make_async_remote_copy(
            src_ref=source,
            dst_ref=target,
            send_sem=send_sem.at[k],
            recv_sem=recv_sem.at[k],
            device_id=device(step),
            device_id_type=MESH,
        )
        copies.append((step, copy))

        @pl.when(exists(step))
        def _(copy=copy):
            copy.start()

        @pl.when(jnp.logical_not(exists((-step[0], -step[1]))))
        def _(target=target):
            target[...] = jnp.zeros(target.shape, target.dtype)

    tn = (((0,), (0,)), ((), ()))
    nt = (((1,), (1,)), ((), ()))
    tile = (rows, 128)
    lane = lax.broadcasted_iota(jnp.int32, tile, 1)
    line = lane // feats
    spread = (
        lax.broadcasted_iota(jnp.int32, (feats, 128), 1) % feats
        == lax.broadcasted_iota(jnp.int32, (feats, 128), 0)
    ).astype(jnp.float32)
    one = (
        lax.broadcasted_iota(jnp.int32, (groups, 128), 1) % feats // per
        == lax.broadcasted_iota(jnp.int32, (groups, 128), 0)
    ).astype(jnp.float32)
    exact = dict(precision=lax.Precision.HIGHEST, preferred_element_type=jnp.float32)
    bias = jnp.dot(bias_in[...], spread, **exact)
    taps_ref[...] = lax.dot_general(
        weight_ref[...].astype(jnp.float32), spread, tn, preferred_element_type=jnp.float32
    )
    agg = lax.dot_general(agg_in[...], one, tn, **exact) * (LOG2E / per)

    above = lax.broadcasted_iota(jnp.int32, tile, 0) - line + 2
    near_line = line[:cin]
    for k in range(pairs):
        columns = slice(k * 128, (k + 1) * 128)
        hit = [above == step_y + 2 * k for step_y in range(3)]
        for step_x in range(3):
            for c in range(cin):
                value = jnp.zeros(tile, jnp.float32)
                for step_y in range(3):
                    at = (step_y * 3 + step_x) * cin + c
                    value = jnp.where(hit[step_y], taps_ref[at : at + 1, :], value)
                begin = step_x * main + c * rows
                wc[begin : begin + rows, columns] = value.astype(jnp.bfloat16)
        if k in (0, 1, pairs - 2, pairs - 1):
            for step_x in range(3):
                for side in range(2):
                    halves = []
                    for y in range(2):
                        row = y - 2 if side == 0 else rows + y
                        value = jnp.zeros((cin, 128), jnp.float32)
                        for step_y in range(3):
                            at = (step_y * 3 + step_x) * cin
                            value = jnp.where(
                                near_line == row - 2 * k + 2 - step_y, taps_ref[at : at + cin, :], value
                            )
                        halves.append(value)
                    begin = 3 * main + (step_x * 2 + side) * 2 * cin
                    wc[begin : begin + 2 * cin, columns] = (
                        jnp.concatenate(halves, axis=0).astype(jnp.bfloat16)
                    )
            begin = 3 * main + 12 * cin
            wc[begin:, columns] = jnp.zeros((wc.shape[0] - begin, 128), jnp.bfloat16)

    for step_d in range(3):
        for step_x in range(3):
            for odd in range(2):
                value = jnp.zeros((8, 128), jnp.float32)
                for step_y in range(3):
                    at = 9 * step_d + 3 * step_y + step_x
                    value = jnp.where(line[:8] == step_y + odd, agg[at : at + 1, :], value)
                band_w[(step_d * 3 + step_x) * 2 + odd] = value

    behind = line - lax.broadcasted_iota(jnp.int32, tile, 0)
    once = [k for k in range(0, pairs, 2)] + [pairs - 1]
    for step_d in range(3):
        for step_x in range(3):
            for t, k in enumerate(once):
                value = jnp.zeros(tile, jnp.float32)
                for step_y in range(3):
                    at = 9 * step_d + 3 * step_y + step_x
                    value = jnp.where(behind == step_y - 2 * k, agg[at : at + 1, :], value)
                if k % 2:
                    value = jnp.where(line >= 2, value, 0.0)
                amat[step_d, step_x * rows : (step_x + 1) * rows, t * 128 : (t + 1) * 128] = (
                    value.astype(jnp.bfloat16)
                )

    at_x = lax.broadcasted_iota(jnp.int32, (D, cols), 1)
    at_i = lax.broadcasted_iota(jnp.int32, (D, cols), 0)
    low = at_x < D
    for j, apart in enumerate((jnp.where(low, at_x - at_i + D, at_x - at_i - D), at_x - at_i)):
        mask[j] = jnp.where((apart >= 1) & (apart <= D - 2), 0.0, -jnp.inf)

    base = 16 + D
    pt[:, base : base + cols, :] = tr_ref[...].astype(jnp.float32)

    for step, copy in copies:

        @pl.when(exists((-step[0], -step[1])))
        def _(copy=copy):
            copy.wait_recv()

    pt[1, base - reach : base, :] = near1[...].astype(jnp.float32)
    pt[0, base - 16 : base, :] = near0[...].astype(jnp.float32)
    pt[:, base + cols : base + cols + 16, :] = far[...].astype(jnp.float32)
    half = 2 * cin
    for image in range(2):
        blocks = []
        for place in range(3):
            block = jnp.concatenate(
                [
                    lines[side, place, image * half : (image + 1) * half, :].astype(jnp.float32)
                    for side in range(2)
                ]
                * 3
                + [jnp.zeros((128 - 6 * half, cols), jnp.float32)],
                axis=0,
            ).T
            if place == 0:
                keep = reach if image else 16
                blocks.append((8 + base - keep, block[cols - keep :, :]))
            elif place == 1:
                blocks.append((8 + base, block))
            else:
                blocks.append((8 + base + cols, block[:16, :]))
        for at, block in blocks:
            ext[image, at : at + block.shape[0], :] = block
        wide_part = 2 * half
        for at, block in blocks:
            size = block.shape[0]
            ext[image, at + 1 : at + 1 + size, :wide_part] = block[:, :wide_part]
            ext[image, at - 1 : at - 1 + size, 2 * wide_part : 3 * wide_part] = (
                block[:, 2 * wide_part : 3 * wide_part]
            )

    top_ok = (my_row > 0) | (line[:1] > 0)
    end_ok = (my_row < rows_axis - 1) | (line[:1] < 3)

    def features(image, first, count, store):
        for step_x in range(3):
            lhs[image, :count, step_x * main : (step_x + 1) * main] = (
                pt[image, 7 + step_x + first : 7 + step_x + first + count, :].astype(jnp.bfloat16)
            )
        lhs[image, :count, 3 * main :] = ext[image, 16 + first : 16 + first + count, :].astype(jnp.bfloat16)
        for n in range(pairs // 2):
            depth = lhs.shape[2] if n in (0, pairs // 2 - 1) else 3 * main
            total = jnp.dot(
                lhs[image, :count, :depth],
                wc[:depth, n * 256 : (n + 1) * 256],
                preferred_element_type=jnp.float32,
            )
            for j in range(2):
                k = 2 * n + j
                value = total[:, j * 128 : (j + 1) * 128] + bias
                value = jnp.maximum(value, value * 0.1)
                value = value.astype(jnp.bfloat16).astype(jnp.float32)
                if image == 0 and k == 0:
                    value = jnp.where(top_ok, value, 0.0)
                if image == 0 and k == pairs - 1:
                    value = jnp.where(end_ok, value, 0.0)
                store[k, :, :] = value

    features(0, lead - 8, wide_l, lf)
    features(1, 0, span, rf)

    @pl.when(my_col == 0)
    def _():
        lf[:, 0:8, :] = jnp.zeros((pairs, 8, 128), jnp.float32)
        rf[:, 0:lead, :] = jnp.zeros((pairs, lead, 128), jnp.float32)

    @pl.when(my_col == cols_axis - 1)
    def _():
        lf[:, 8 + cols :, :] = jnp.zeros((pairs, wide_l - 8 - cols, 128), jnp.float32)

    ends = []
    for last, first_d in ((0, 0), (1, D - 2)):
        total = None
        for j in range(2):
            d = first_d + j
            parts = []
            for k in once:
                got = lf[k, :, :] * rf[k, lead - 8 - d : lead - 8 - d + wide_l, :]
                parts.append(
                    jnp.concatenate(
                        [got[8:, :], jnp.zeros((256 - wide_l, 128), jnp.float32), got[:8, :]], axis=0
                    ).astype(jnp.bfloat16)
                )
            term = lax.dot_general(
                amat[j + 1 - last], jnp.concatenate(parts, axis=1), nt, preferred_element_type=jnp.float32
            )
            total = term if total is None else total + term
        value = total[rows : 2 * rows, :]
        value = value + pltpu.roll(total[:rows, :], 1, 1) + pltpu.roll(total[2 * rows :, :], 255, 1)
        ends.append(value[:, :cols])

    for k in range(pairs):
        for delta in range(-2, 3):
            at = lead - D + delta
            right_m[k, :, (delta + 2) * 128 : (delta + 3) * 128] = (
                rf[k, at : at + D + cols, :].astype(jnp.bfloat16)
            )
        for chunk in range(cols // 16):
            at = 7 + chunk * 16
            shifted = [lf[k, at + c : at + c + 16, :].reshape(2, 8, 128) for c in range(3)]
            for odd in range(2):
                for delta in range(-2, 3):
                    value = None
                    for c in range(3):
                        a = c - delta
                        if 0 <= a < 3:
                            term = shifted[c] * band_w[(a * 3 + c) * 2 + odd]
                            value = term if value is None else value + term
                    left_m[
                        k,
                        odd * cols + chunk * 16 : odd * cols + chunk * 16 + 16,
                        (delta + 2) * 128 : (delta + 3) * 128,
                    ] = value.reshape(16, 128).astype(jnp.bfloat16)

    low_lane = lax.broadcasted_iota(jnp.int32, (D, cols), 1) < D
    lane8 = lax.broadcasted_iota(jnp.int32, (8, cols), 1)
    from_x = (lane8 - lax.broadcasted_iota(jnp.int32, (8, cols), 0)).astype(jnp.float32)
    jump = jnp.where(lane8 < D, float(D), -float(D))
    for k in range(pairs):
        score = lax.dot_general(right_m[k], left_m[k], nt, preferred_element_type=jnp.float32)
        for odd in range(2):
            mine = slice(odd * cols, (odd + 1) * cols)
            outer = jnp.where(low_lane, score[:D, mine], score[2 * D :, mine]) + mask[0]
            inner = score[D : 2 * D, mine] + mask[1]
            outer = outer.reshape(D // 8, 8, cols)
            inner = inner.reshape(D // 8, 8, cols)
            best = jnp.maximum(jnp.max(outer, axis=0), jnp.max(inner, axis=0))
            outer = jnp.exp2(outer - best)
            both = outer + jnp.exp2(inner - best)
            tail, steps = both[D // 8 - 1], None
            for j in range(D // 8 - 2, -1, -1):
                steps = tail if steps is None else steps + tail
                tail = tail + both[j]
            moment = from_x * tail - 8.0 * steps + jump * jnp.sum(outer, axis=0)
            y = 2 * k + odd
            for j, value in enumerate((best, tail, moment)):
                part[j, y * 8 : (y + 1) * 8, :] = value

    for h in range(rows // 8):
        first = ends[0][h * 8 : (h + 1) * 8, :]
        last = ends[1][h * 8 : (h + 1) * 8, :]
        tops = [part[0, pl.ds(h * 64 + j, 8, stride=8), :] for j in range(8)]
        best = jnp.maximum(first, last)
        for top in tops:
            best = jnp.maximum(best, top)
        last = jnp.exp2(last - best)
        total = jnp.exp2(first - best) + last
        moment = last * float(D - 1)
        for j in range(8):
            weight = jnp.exp2(tops[j] - best)
            total = total + weight * part[1, pl.ds(h * 64 + j, 8, stride=8), :]
            moment = moment + weight * part[2, pl.ds(h * 64 + j, 8, stride=8), :]
        out_ref[h * 8 : (h + 1) * 8, :] = moment / total / D

    for step, copy in copies:

        @pl.when(exists(step))
        def _(copy=copy):
            copy.wait_send()


def on_device(images, conv_weight, conv_bias, agg_weight):
    cin, rows, cols = images.shape[1:]
    groups = agg_weight.shape[0]
    per = conv_weight.shape[0] // groups
    main = rows * cin
    pairs = rows // 2
    span = cols + D + 16
    reach = -(-(D + 2) // 16) * 16
    return pl.pallas_call(
        functools.partial(body, (rows, cols, groups, per, cin)),
        out_shape=pltpu.VMEM((rows, cols), jnp.float32),
        in_specs=[pl.BlockSpec(memory_space=pl.ANY)] * 4,
        out_specs=pl.BlockSpec(memory_space=pltpu.VMEM),
        scratch_shapes=[
            pltpu.VMEM(images.shape, images.dtype),
            pltpu.VMEM(conv_weight.shape, conv_weight.dtype),
            pltpu.VMEM((1,) + conv_bias.shape, conv_bias.dtype),
            pltpu.VMEM(agg_weight.shape, agg_weight.dtype),
            pltpu.SemaphoreType.DMA((4,)),
            pltpu.VMEM((2, span + 16, main), jnp.float32),
            pltpu.VMEM((2, span + 32, 128), jnp.float32),
            pltpu.VMEM((2, span, 3 * main + 128), jnp.bfloat16),
            pltpu.VMEM((3 * main + 128, pairs * 128), jnp.bfloat16),
            pltpu.VMEM((3, 3 * rows, (pairs // 2 + 1) * 128), jnp.bfloat16),
            pltpu.VMEM((9 * cin, 128), jnp.float32),
            pltpu.VMEM((18, 8, 128), jnp.float32),
            pltpu.VMEM((2, D, cols), jnp.float32),
            pltpu.VMEM((pairs, cols + 16, 128), jnp.float32),
            pltpu.VMEM((pairs, span, 128), jnp.float32),
            pltpu.VMEM((pairs, 2 * cols, 640), jnp.bfloat16),
            pltpu.VMEM((pairs, D + cols, 640), jnp.bfloat16),
            pltpu.VMEM((3, rows * 8, cols), jnp.float32),
            pltpu.VMEM((2, cols, main), jnp.bfloat16),
            pltpu.VMEM((2, 4 * cin, cols), jnp.bfloat16),
            pltpu.VMEM((16, main), jnp.bfloat16),
            pltpu.VMEM((reach, main), jnp.bfloat16),
            pltpu.VMEM((2, 16, main), jnp.bfloat16),
            pltpu.VMEM((2, 3, 4 * cin, cols), jnp.bfloat16),
            pltpu.SemaphoreType.DMA((9,)),
            pltpu.SemaphoreType.DMA((9,)),
        ],
        compiler_params=pltpu.CompilerParams(collective_id=0, has_side_effects=True),
    )(images, conv_weight, conv_bias[None], agg_weight)


def solution(mesh):
    in_specs = (P("pairs", None, "row", "col"), P(), P(), P())
    out_specs = P(("pairs", "row"), "col")
    return jax.shard_map(
        on_device, mesh=mesh, in_specs=in_specs, out_specs=out_specs, check_vma=False
    )
```

```python
import functools

import jax
import jax.numpy as jnp
from jax import lax
from jax.experimental import pallas as pl
from jax.experimental.pallas import tpu as pltpu
from jax.sharding import PartitionSpec as P

D = 64
LOG2E = 1.4426950408889634


MESH = pl.DeviceIdType.MESH
STEPS = ((0, 1), (0, -1), (1, 0), (-1, 0), (1, 1), (1, -1), (-1, 1), (-1, -1))


def body(
    shape, images_hbm, weight_hbm, bias_hbm, agg_hbm, out_ref,
    images_ref, weight_ref, bias_in, agg_in, load_sem,
    pt, ext, lhs, wc, amat, taps_ref, band_w, mask, lf, rf, left_m, right_m, part,
    tr_ref, edge_ref, near0, near1, far, lines, send_sem, recv_sem, ready,
):
    rows, cols, groups, per, cin = shape
    feats = groups * per
    pairs = rows // 2
    lead = D + 8
    span = rf.shape[1]
    wide_l = lf.shape[1]
    rows_axis, cols_axis = lax.axis_size("row"), lax.axis_size("col")
    my_row, my_col = lax.axis_index("row"), lax.axis_index("col")
    reach = near1.shape[0]

    def exists(step):
        r, c = my_row + step[0], my_col + step[1]
        return (r >= 0) & (r < rows_axis) & (c >= 0) & (c < cols_axis)

    def device(step):
        return {"row": my_row + step[0], "col": my_col + step[1]}

    barrier = pltpu.get_barrier_semaphore()
    for step in STEPS:
        if step[1] >= 0:

            @pl.when(exists(step))
            def _(step=step):
                pl.semaphore_signal(barrier, inc=1, device_id=device(step), device_id_type=MESH)

    loads = [
        pltpu.make_async_copy(source, target, load_sem.at[k])
        for k, (source, target) in enumerate(
            ((images_hbm, images_ref), (weight_hbm, weight_ref), (bias_hbm, bias_in), (agg_hbm, agg_in))
        )
    ]
    for load in loads:
        load.start()
    tall = 1 + (my_row > 0).astype(jnp.int32) + (my_row < rows_axis - 1).astype(jnp.int32)
    pl.semaphore_wait(barrier, tall - 1 + jnp.where(my_col > 0, tall, 0))
    for step in STEPS:
        if step[1] < 0:

            @pl.when(exists(step))
            def _(step=step):
                pl.semaphore_signal(ready, inc=1, device_id=device(step), device_id_type=MESH)

    for load in loads:
        load.wait()

    main = rows * cin
    for image in range(2):
        flat = images_ref[image].reshape(main, cols)
        tr_ref[image] = flat.T.astype(jnp.bfloat16)
        for side, first in ((0, 0), (1, rows - 2)):
            pair = [images_ref[image, :, first + y, :] for y in range(2)]
            edge_ref[side, image * 2 * cin : (image + 1) * 2 * cin, :] = jnp.concatenate(
                pair, axis=0
            ).astype(jnp.bfloat16)

    plan = [
        ((0, 1), tr_ref.at[1, pl.ds(cols - reach, reach), :], near1),
        ((0, 1), tr_ref.at[0, pl.ds(cols - 16, 16), :], near0),
        ((0, -1), tr_ref.at[:, pl.ds(0, 16), :], far),
    ]
    for r in (1, -1):
        side = 0 if r == 1 else 1
        for c in (0, 1, -1):
            plan.append(((r, c), edge_ref.at[1 - side], lines.at[side, 1 - c]))
    copies = []
    for k, (step, source, target) in enumerate(plan):
        copy = pltpu.make_async_remote_copy(
            src_ref=source,
            dst_ref=target,
            send_sem=send_sem.at[k],
            recv_sem=recv_sem.at[k],
            device_id=device(step),
            device_id_type=MESH,
        )
        copies.append((step, copy))

        @pl.when(jnp.logical_not(exists((-step[0], -step[1]))))
        def _(target=target):
            target[...] = jnp.zeros(target.shape, target.dtype)

    def send(chosen):
        for step, copy in copies:
            if chosen(step):

                @pl.when(exists(step))
                def _(copy=copy):
                    copy.start()

    def receive(chosen):
        for step, copy in copies:
            if chosen(step):

                @pl.when(exists((-step[0], -step[1])))
                def _(copy=copy):
                    copy.wait_recv()

    send(lambda step: step[1] <= 0)

    tn = (((0,), (0,)), ((), ()))
    nt = (((1,), (1,)), ((), ()))
    tile = (rows, 128)
    lane = lax.broadcasted_iota(jnp.int32, tile, 1)
    line = lane // feats
    spread = (
        lax.broadcasted_iota(jnp.int32, (feats, 128), 1) % feats
        == lax.broadcasted_iota(jnp.int32, (feats, 128), 0)
    ).astype(jnp.float32)
    one = (
        lax.broadcasted_iota(jnp.int32, (groups, 128), 1) % feats // per
        == lax.broadcasted_iota(jnp.int32, (groups, 128), 0)
    ).astype(jnp.float32)
    exact = dict(precision=lax.Precision.HIGHEST, preferred_element_type=jnp.float32)
    bias = jnp.dot(bias_in[...], spread, **exact)
    taps_ref[...] = lax.dot_general(
        weight_ref[...].astype(jnp.float32), spread, tn, preferred_element_type=jnp.float32
    )
    agg = lax.dot_general(agg_in[...], one, tn, **exact) * (LOG2E / per)

    above = lax.broadcasted_iota(jnp.int32, tile, 0) - line + 2
    near_line = line[:cin]
    inner_pairs, outer_pairs = list(range(1, pairs - 1)), [0, pairs - 1]
    for n, k in enumerate(inner_pairs + outer_pairs):
        columns = slice(n * 128, (n + 1) * 128)
        hit = [above == step_y + 2 * k for step_y in range(3)]
        for step_x in range(3):
            for c in range(cin):
                value = jnp.zeros(tile, jnp.float32)
                for step_y in range(3):
                    at = (step_y * 3 + step_x) * cin + c
                    value = jnp.where(hit[step_y], taps_ref[at : at + 1, :], value)
                begin = step_x * main + c * rows
                wc[begin : begin + rows, columns] = value.astype(jnp.bfloat16)
        if k in outer_pairs:
            for step_x in range(3):
                for side in range(2):
                    halves = []
                    for y in range(2):
                        row = y - 2 if side == 0 else rows + y
                        value = jnp.zeros((cin, 128), jnp.float32)
                        for step_y in range(3):
                            at = (step_y * 3 + step_x) * cin
                            value = jnp.where(
                                near_line == row - 2 * k + 2 - step_y, taps_ref[at : at + cin, :], value
                            )
                        halves.append(value)
                    begin = 3 * main + (step_x * 2 + side) * 2 * cin
                    wc[begin : begin + 2 * cin, columns] = (
                        jnp.concatenate(halves, axis=0).astype(jnp.bfloat16)
                    )
            begin = 3 * main + 12 * cin
            wc[begin:, columns] = jnp.zeros((wc.shape[0] - begin, 128), jnp.bfloat16)

    for step_d in range(3):
        for step_x in range(3):
            for odd in range(2):
                value = jnp.zeros((8, 128), jnp.float32)
                for step_y in range(3):
                    at = 9 * step_d + 3 * step_y + step_x
                    value = jnp.where(line[:8] == step_y + odd, agg[at : at + 1, :], value)
                band_w[(step_d * 3 + step_x) * 2 + odd] = value

    behind = line - lax.broadcasted_iota(jnp.int32, tile, 0)
    once = inner_pairs[::2] + outer_pairs
    for step_d in range(3):
        for step_x in range(3):
            for t, k in enumerate(once):
                value = jnp.zeros(tile, jnp.float32)
                for step_y in range(3):
                    at = 9 * step_d + 3 * step_y + step_x
                    value = jnp.where(behind == step_y - 2 * k, agg[at : at + 1, :], value)
                if k == 0:
                    value = jnp.where(line < 2, value, 0.0)
                amat[step_d, step_x * rows : (step_x + 1) * rows, t * 128 : (t + 1) * 128] = (
                    value.astype(jnp.bfloat16)
                )

    at_x = lax.broadcasted_iota(jnp.int32, (D, cols), 1)
    at_i = lax.broadcasted_iota(jnp.int32, (D, cols), 0)
    low = at_x < D
    for j, apart in enumerate((jnp.where(low, at_x - at_i + D, at_x - at_i - D), at_x - at_i)):
        mask[j] = jnp.where((apart >= 1) & (apart <= D - 2), 0.0, -jnp.inf)

    base = 16 + D
    pt[:, base : base + cols, :] = tr_ref[...].astype(jnp.float32)

    @pl.when(my_col < cols_axis - 1)
    def _():
        pl.semaphore_wait(ready, tall)

    send(lambda step: step[1] > 0)

    left_ok = (my_col > 0).astype(jnp.float32)
    right_ok = (my_col < cols_axis - 1).astype(jnp.float32)
    top_ok = (my_row > 0) | (line[:1] > 0)
    end_ok = (my_row < rows_axis - 1) | (line[:1] < 3)
    split = cols - 8

    def gather(image, first, count):
        for step_x in range(3):
            lhs[image, first : first + count, step_x * main : (step_x + 1) * main] = (
                pt[image, 7 + step_x + at0[image] + first : 7 + step_x + at0[image] + first + count, :]
            ).astype(jnp.bfloat16)

    def finish(total, j, k, image):
        value = total[:, j * 128 : (j + 1) * 128] + bias
        value = jnp.maximum(value, value * 0.1)
        value = value.astype(jnp.bfloat16).astype(jnp.float32)
        if image == 0 and k == 0:
            value = jnp.where(top_ok, value, 0.0)
        if image == 0 and k == pairs - 1:
            value = jnp.where(end_ok, value, 0.0)
        return value

    def convolve(rows_in, n, depth):
        return jnp.dot(
            rows_in, wc[:depth, n * 256 : (n + 1) * 256], preferred_element_type=jnp.float32
        )

    def put(image, k, begin, value):
        store = (lf, rf)[image]
        edge = (8, lead)[image]
        end = begin + value.shape[0]
        if begin < edge:
            store[k, begin:edge, :] = value[: edge - begin, :] * left_ok
            value, begin = value[edge - begin :, :], edge
        if image == 0 and end > 8 + cols:
            store[k, 8 + cols : end, :] = value[8 + cols - begin :, :] * right_ok
            value = value[: 8 + cols - begin, :]
        store[k, begin : begin + value.shape[0], :] = value

    def build_right(k, begin, count):
        for delta in range(-2, 3):
            at = lead - D + delta + begin
            right_m[k, begin : begin + count, (delta + 2) * 128 : (delta + 3) * 128] = (
                rf[k, at : at + count, :].astype(jnp.bfloat16)
            )

    def build_left(k, chunks):
        for chunk in chunks:
            at = 7 + chunk * 16
            shifted = [lf[k, at + c : at + c + 16, :].reshape(2, 8, 128) for c in range(3)]
            for odd in range(2):
                for delta in range(-2, 3):
                    value = None
                    for c in range(3):
                        a = c - delta
                        if 0 <= a < 3:
                            term = shifted[c] * band_w[(a * 3 + c) * 2 + odd]
                            value = term if value is None else value + term
                    left_m[
                        k,
                        odd * cols + chunk * 16 : odd * cols + chunk * 16 + 16,
                        (delta + 2) * 128 : (delta + 3) * 128,
                    ] = value.reshape(16, 128).astype(jnp.bfloat16)

    def end_costs(tiles, begin):
        sums = []
        for last, first_d in ((0, 0), (1, D - 2)):
            total = None
            for j in range(2):
                d = first_d + j
                parts = []
                for k in tiles:
                    got = lf[k, :, :] * rf[k, lead - 8 - d : lead - 8 - d + wide_l, :]
                    parts.append(
                        jnp.concatenate(
                            [got[8:, :], jnp.zeros((256 - wide_l, 128), jnp.float32), got[:8, :]], axis=0
                        ).astype(jnp.bfloat16)
                    )
                term = lax.dot_general(
                    amat[j + 1 - last, :, begin * 128 : (begin + len(tiles)) * 128],
                    jnp.concatenate(parts, axis=1),
                    nt,
                    preferred_element_type=jnp.float32,
                )
                total = term if total is None else total + term
            sums.append(total)
        return sums

    chunks = cols // 16
    counts = (wide_l, span)
    at0 = (lead - 8, 0)
    sizes = (8 + split, lead + split)

    receive(lambda step: step == (0, 1))
    base = 16 + D
    pt[1, base - reach : base, :] = near1[...].astype(jnp.float32)
    pt[0, base - 16 : base, :] = near0[...].astype(jnp.float32)
    for image in range(2):
        gather(image, 0, sizes[image])
        for n in range(len(inner_pairs) // 2):
            total = convolve(lhs[image, : sizes[image], : 3 * main], n, 3 * main)
            for j in range(2):
                k = inner_pairs[2 * n + j]
                put(image, k, 0, finish(total, j, k, image))
    for k in inner_pairs:
        build_right(k, 0, D + cols - 16)
        build_left(k, range(chunks - 1))

    receive(lambda step: step == (0, -1))
    pt[:, base + cols : base + cols + 16, :] = far[...].astype(jnp.float32)
    for image in range(2):
        gather(image, sizes[image], 16)
    ends_in = jnp.concatenate(
        [lhs[image, sizes[image] : sizes[image] + 16, : 3 * main] for image in range(2)], axis=0
    )
    for n in range(len(inner_pairs) // 2):
        total = convolve(ends_in, n, 3 * main)
        for j in range(2):
            k = inner_pairs[2 * n + j]
            for image in range(2):
                value = finish(total[image * 16 : (image + 1) * 16, :], j, k, image)
                put(image, k, sizes[image], value)
    for k in inner_pairs:
        build_right(k, D + cols - 16, 16)
        build_left(k, [chunks - 1])
    inner_tiles = len(inner_pairs[::2])
    ends_inner = end_costs(inner_pairs[::2], 0)

    low_lane = lax.broadcasted_iota(jnp.int32, (D, cols), 1) < D
    lane8 = lax.broadcasted_iota(jnp.int32, (8, cols), 1)
    from_x = (lane8 - lax.broadcasted_iota(jnp.int32, (8, cols), 0)).astype(jnp.float32)
    jump = jnp.where(lane8 < D, float(D), -float(D))

    def attend(k):
        score = lax.dot_general(right_m[k], left_m[k], nt, preferred_element_type=jnp.float32)
        for odd in range(2):
            mine = slice(odd * cols, (odd + 1) * cols)
            outer = jnp.where(low_lane, score[:D, mine], score[2 * D :, mine]) + mask[0]
            inner = score[D : 2 * D, mine] + mask[1]
            outer = outer.reshape(D // 8, 8, cols)
            inner = inner.reshape(D // 8, 8, cols)
            best = jnp.maximum(jnp.max(outer, axis=0), jnp.max(inner, axis=0))
            outer = jnp.exp2(outer - best)
            both = outer + jnp.exp2(inner - best)
            tail, steps = both[D // 8 - 1], None
            for j in range(D // 8 - 2, -1, -1):
                steps = tail if steps is None else steps + tail
                tail = tail + both[j]
            moment = from_x * tail - 8.0 * steps + jump * jnp.sum(outer, axis=0)
            y = 2 * k + odd
            for j, value in enumerate((best, tail, moment)):
                part[j, y * 8 : (y + 1) * 8, :] = value

    for k in inner_pairs:
        attend(k)

    receive(lambda step: step[0] != 0)
    half = 2 * cin
    for image in range(2):
        blocks = []
        for place in range(3):
            block = jnp.concatenate(
                [
                    lines[side, place, image * half : (image + 1) * half, :].astype(jnp.float32)
                    for side in range(2)
                ]
                * 3
                + [jnp.zeros((128 - 6 * half, cols), jnp.float32)],
                axis=0,
            ).T
            if place == 0:
                keep = reach if image else 16
                blocks.append((8 + base - keep, block[cols - keep :, :]))
            elif place == 1:
                blocks.append((8 + base, block))
            else:
                blocks.append((8 + base + cols, block[:16, :]))
        for at, block in blocks:
            ext[image, at : at + block.shape[0], :] = block
        wide_part = 2 * half
        for at, block in blocks:
            size = block.shape[0]
            ext[image, at + 1 : at + 1 + size, :wide_part] = block[:, :wide_part]
            ext[image, at - 1 : at - 1 + size, 2 * wide_part : 3 * wide_part] = (
                block[:, 2 * wide_part : 3 * wide_part]
            )
        begin = 16 + at0[image]
        lhs[image, : counts[image], 3 * main :] = (
            ext[image, begin : begin + counts[image], :].astype(jnp.bfloat16)
        )
        total = convolve(lhs[image, : counts[image], :], len(inner_pairs) // 2, lhs.shape[2])
        for j, k in enumerate(outer_pairs):
            put(image, k, 0, finish(total, j, k, image))
    for k in outer_pairs:
        build_right(k, 0, D + cols)
        build_left(k, range(chunks))
    ends = []
    for total, more in zip(ends_inner, end_costs(outer_pairs, inner_tiles)):
        total = total + more
        value = total[rows : 2 * rows, :]
        value = value + pltpu.roll(total[:rows, :], 1, 1) + pltpu.roll(total[2 * rows :, :], 255, 1)
        ends.append(value[:, :cols])
    for k in outer_pairs:
        attend(k)

    for h in range(rows // 8):
        first = ends[0][h * 8 : (h + 1) * 8, :]
        last = ends[1][h * 8 : (h + 1) * 8, :]
        tops = [part[0, pl.ds(h * 64 + j, 8, stride=8), :] for j in range(8)]
        best = jnp.maximum(first, last)
        for top in tops:
            best = jnp.maximum(best, top)
        last = jnp.exp2(last - best)
        total = jnp.exp2(first - best) + last
        moment = last * float(D - 1)
        for j in range(8):
            weight = jnp.exp2(tops[j] - best)
            total = total + weight * part[1, pl.ds(h * 64 + j, 8, stride=8), :]
            moment = moment + weight * part[2, pl.ds(h * 64 + j, 8, stride=8), :]
        out_ref[h * 8 : (h + 1) * 8, :] = moment / total / D

    for step, copy in copies:

        @pl.when(exists(step))
        def _(copy=copy):
            copy.wait_send()


def on_device(images, conv_weight, conv_bias, agg_weight):
    cin, rows, cols = images.shape[1:]
    groups = agg_weight.shape[0]
    per = conv_weight.shape[0] // groups
    main = rows * cin
    pairs = rows // 2
    span = cols + D + 16
    reach = -(-(D + 2) // 16) * 16
    return pl.pallas_call(
        functools.partial(body, (rows, cols, groups, per, cin)),
        out_shape=pltpu.VMEM((rows, cols), jnp.float32),
        in_specs=[pl.BlockSpec(memory_space=pl.ANY)] * 4,
        out_specs=pl.BlockSpec(memory_space=pltpu.VMEM),
        scratch_shapes=[
            pltpu.VMEM(images.shape, images.dtype),
            pltpu.VMEM(conv_weight.shape, conv_weight.dtype),
            pltpu.VMEM((1,) + conv_bias.shape, conv_bias.dtype),
            pltpu.VMEM(agg_weight.shape, agg_weight.dtype),
            pltpu.SemaphoreType.DMA((4,)),
            pltpu.VMEM((2, span + 16, main), jnp.float32),
            pltpu.VMEM((2, span + 32, 128), jnp.float32),
            pltpu.VMEM((2, span, 3 * main + 128), jnp.bfloat16),
            pltpu.VMEM((3 * main + 128, pairs * 128), jnp.bfloat16),
            pltpu.VMEM((3, 3 * rows, (pairs // 2 + 1) * 128), jnp.bfloat16),
            pltpu.VMEM((9 * cin, 128), jnp.float32),
            pltpu.VMEM((18, 8, 128), jnp.float32),
            pltpu.VMEM((2, D, cols), jnp.float32),
            pltpu.VMEM((pairs, cols + 16, 128), jnp.float32),
            pltpu.VMEM((pairs, span, 128), jnp.float32),
            pltpu.VMEM((pairs, 2 * cols, 640), jnp.bfloat16),
            pltpu.VMEM((pairs, D + cols, 640), jnp.bfloat16),
            pltpu.VMEM((3, rows * 8, cols), jnp.float32),
            pltpu.VMEM((2, cols, main), jnp.bfloat16),
            pltpu.VMEM((2, 4 * cin, cols), jnp.bfloat16),
            pltpu.VMEM((16, main), jnp.bfloat16),
            pltpu.VMEM((reach, main), jnp.bfloat16),
            pltpu.VMEM((2, 16, main), jnp.bfloat16),
            pltpu.VMEM((2, 3, 4 * cin, cols), jnp.bfloat16),
            pltpu.SemaphoreType.DMA((9,)),
            pltpu.SemaphoreType.DMA((9,)),
            pltpu.SemaphoreType.REGULAR,
        ],
        compiler_params=pltpu.CompilerParams(collective_id=0, has_side_effects=True),
    )(images, conv_weight, conv_bias[None], agg_weight)


def solution(mesh):
    in_specs = (P("pairs", None, "row", "col"), P(), P(), P())
    out_specs = P(("pairs", "row"), "col")
    return jax.shard_map(
        on_device, mesh=mesh, in_specs=in_specs, out_specs=out_specs, check_vma=False
    )
```

```python
import functools

import jax
import jax.numpy as jnp
from jax import lax
from jax.experimental import pallas as pl
from jax.experimental.pallas import tpu as pltpu
from jax.sharding import PartitionSpec as P

D = 64
LOG2E = 1.4426950408889634


MESH = pl.DeviceIdType.MESH
STEPS = ((0, 1), (0, -1), (1, 0), (-1, 0), (1, 1), (1, -1), (-1, 1), (-1, -1))


def body(
    shape, images_hbm, weight_hbm, bias_hbm, agg_hbm, out_ref,
    images_ref, weight_ref, bias_in, agg_in, load_sem,
    pt, ext, lhs, wc, amat, taps_ref, band_w, mask, lf, rf, left_m, right_m, part,
    tr_ref, edge_ref, near0, near1, far, lines, send_sem, recv_sem, ready,
):
    rows, cols, groups, per, cin = shape
    feats = groups * per
    pairs = rows // 2
    lead = D + 8
    span = rf.shape[1]
    wide_l = lf.shape[1]
    rows_axis, cols_axis = lax.axis_size("row"), lax.axis_size("col")
    my_row, my_col = lax.axis_index("row"), lax.axis_index("col")
    reach = near1.shape[0]

    def exists(step):
        r, c = my_row + step[0], my_col + step[1]
        return (r >= 0) & (r < rows_axis) & (c >= 0) & (c < cols_axis)

    def device(step):
        return {"row": my_row + step[0], "col": my_col + step[1]}

    barrier = pltpu.get_barrier_semaphore()
    for step in STEPS:
        if step[1] >= 0:

            @pl.when(exists(step))
            def _(step=step):
                pl.semaphore_signal(barrier, inc=1, device_id=device(step), device_id_type=MESH)

    loads = [
        pltpu.make_async_copy(source, target, load_sem.at[k])
        for k, (source, target) in enumerate(
            ((images_hbm, images_ref), (weight_hbm, weight_ref), (bias_hbm, bias_in), (agg_hbm, agg_in))
        )
    ]
    for load in loads:
        load.start()
    tall = 1 + (my_row > 0).astype(jnp.int32) + (my_row < rows_axis - 1).astype(jnp.int32)
    pl.semaphore_wait(barrier, tall - 1 + jnp.where(my_col > 0, tall, 0))
    for step in STEPS:
        if step[1] < 0:

            @pl.when(exists(step))
            def _(step=step):
                pl.semaphore_signal(ready, inc=1, device_id=device(step), device_id_type=MESH)

    for load in loads:
        load.wait()

    main = rows * cin
    for image in range(2):
        flat = images_ref[image].reshape(main, cols)
        tr_ref[image] = flat.T.astype(jnp.bfloat16)
        for side, first in ((0, 0), (1, rows - 2)):
            pair = [images_ref[image, :, first + y, :] for y in range(2)]
            edge_ref[side, image * 2 * cin : (image + 1) * 2 * cin, :] = jnp.concatenate(
                pair, axis=0
            ).astype(jnp.bfloat16)

    plan = [
        ((0, 1), tr_ref.at[1, pl.ds(cols - reach, reach), :], near1),
        ((0, 1), tr_ref.at[0, pl.ds(cols - 16, 16), :], near0),
        ((0, -1), tr_ref.at[:, pl.ds(0, 16), :], far),
    ]
    for r in (1, -1):
        side = 0 if r == 1 else 1
        for c in (0, 1, -1):
            plan.append(((r, c), edge_ref.at[1 - side], lines.at[side, 1 - c]))
    copies = []
    for k, (step, source, target) in enumerate(plan):
        copy = pltpu.make_async_remote_copy(
            src_ref=source,
            dst_ref=target,
            send_sem=send_sem.at[k],
            recv_sem=recv_sem.at[k],
            device_id=device(step),
            device_id_type=MESH,
        )
        copies.append((step, copy))

        @pl.when(jnp.logical_not(exists((-step[0], -step[1]))))
        def _(target=target):
            target[...] = jnp.zeros(target.shape, target.dtype)

    def send(chosen):
        for step, copy in copies:
            if chosen(step):

                @pl.when(exists(step))
                def _(copy=copy):
                    copy.start()

    def receive(chosen):
        for step, copy in copies:
            if chosen(step):

                @pl.when(exists((-step[0], -step[1])))
                def _(copy=copy):
                    copy.wait_recv()

    send(lambda step: step[1] <= 0)

    tn = (((0,), (0,)), ((), ()))
    nt = (((1,), (1,)), ((), ()))
    tile = (rows, 128)
    lane = lax.broadcasted_iota(jnp.int32, tile, 1)
    line = lane // feats
    spread = (
        lax.broadcasted_iota(jnp.int32, (feats, 128), 1) % feats
        == lax.broadcasted_iota(jnp.int32, (feats, 128), 0)
    ).astype(jnp.float32)
    one = (
        lax.broadcasted_iota(jnp.int32, (groups, 128), 1) % feats // per
        == lax.broadcasted_iota(jnp.int32, (groups, 128), 0)
    ).astype(jnp.float32)
    exact = dict(precision=lax.Precision.HIGHEST, preferred_element_type=jnp.float32)
    bias = jnp.dot(bias_in[...], spread, **exact)
    taps_ref[...] = lax.dot_general(
        weight_ref[...].astype(jnp.float32), spread, tn, preferred_element_type=jnp.float32
    )
    agg = lax.dot_general(agg_in[...], one, tn, **exact) * (LOG2E / per)

    above = lax.broadcasted_iota(jnp.int32, tile, 0) - line + 2
    near_line = line[:cin]
    inner_pairs, outer_pairs = list(range(1, pairs - 1)), [0, pairs - 1]
    for n, k in enumerate(inner_pairs + outer_pairs):
        columns = slice(n * 128, (n + 1) * 128)
        hit = [above == step_y + 2 * k for step_y in range(3)]
        for step_x in range(3):
            for c in range(cin):
                value = jnp.zeros(tile, jnp.float32)
                for step_y in range(3):
                    at = (step_y * 3 + step_x) * cin + c
                    value = jnp.where(hit[step_y], taps_ref[at : at + 1, :], value)
                begin = step_x * main + c * rows
                wc[begin : begin + rows, columns] = value.astype(jnp.bfloat16)
        if k in outer_pairs:
            for step_x in range(3):
                for side in range(2):
                    halves = []
                    for y in range(2):
                        row = y - 2 if side == 0 else rows + y
                        value = jnp.zeros((cin, 128), jnp.float32)
                        for step_y in range(3):
                            at = (step_y * 3 + step_x) * cin
                            value = jnp.where(
                                near_line == row - 2 * k + 2 - step_y, taps_ref[at : at + cin, :], value
                            )
                        halves.append(value)
                    begin = 3 * main + (step_x * 2 + side) * 2 * cin
                    wc[begin : begin + 2 * cin, columns] = (
                        jnp.concatenate(halves, axis=0).astype(jnp.bfloat16)
                    )
            begin = 3 * main + 12 * cin
            wc[begin:, columns] = jnp.zeros((wc.shape[0] - begin, 128), jnp.bfloat16)

    for step_d in range(3):
        for step_x in range(3):
            for odd in range(2):
                value = jnp.zeros((8, 128), jnp.float32)
                for step_y in range(3):
                    at = 9 * step_d + 3 * step_y + step_x
                    value = jnp.where(line[:8] == step_y + odd, agg[at : at + 1, :], value)
                band_w[(step_d * 3 + step_x) * 2 + odd] = value

    behind = line - lax.broadcasted_iota(jnp.int32, tile, 0)
    once = inner_pairs[::2] + outer_pairs
    for step_d in range(3):
        for step_x in range(3):
            for t, k in enumerate(once):
                value = jnp.zeros(tile, jnp.float32)
                for step_y in range(3):
                    at = 9 * step_d + 3 * step_y + step_x
                    value = jnp.where(behind == step_y - 2 * k, agg[at : at + 1, :], value)
                if k == 0:
                    value = jnp.where(line < 2, value, 0.0)
                amat[step_d, step_x * rows : (step_x + 1) * rows, t * 128 : (t + 1) * 128] = (
                    value.astype(jnp.bfloat16)
                )

    at_x = lax.broadcasted_iota(jnp.int32, (D, cols), 1)
    at_i = lax.broadcasted_iota(jnp.int32, (D, cols), 0)
    low = at_x < D
    for j, apart in enumerate((jnp.where(low, at_x - at_i + D, at_x - at_i - D), at_x - at_i)):
        mask[j] = jnp.where((apart >= 1) & (apart <= D - 2), 0.0, -jnp.inf)

    base = 16 + D
    pt[:, base : base + cols, :] = tr_ref[...].astype(jnp.float32)
    ext[:, :, 12 * cin :] = jnp.zeros((2, span + 32, 128 - 12 * cin), jnp.float32)

    @pl.when(my_col < cols_axis - 1)
    def _():
        pl.semaphore_wait(ready, tall)

    send(lambda step: step[1] > 0)

    left_ok = (my_col > 0).astype(jnp.float32)
    right_ok = (my_col < cols_axis - 1).astype(jnp.float32)
    top_ok = (my_row > 0) | (line[:1] > 0)
    end_ok = (my_row < rows_axis - 1) | (line[:1] < 3)
    base = 16 + D
    counts = (wide_l, span)
    origin = (8, lead)
    local = cols - 16

    def gather(image, first, count):
        begin = 8 + origin[1] - origin[image] + first
        for step_x in range(3):
            at = begin + step_x - 1
            lhs[image, first : first + count, step_x * main : (step_x + 1) * main] = (
                pt[image, at : at + count, :].astype(jnp.bfloat16)
            )

    def gather_lines(image, first, count):
        at = 16 + origin[1] - origin[image] + first
        lhs[image, first : first + count, 3 * main :] = ext[image, at : at + count, :].astype(jnp.bfloat16)

    def finish(total, j, k, image):
        value = total[:, j * 128 : (j + 1) * 128] + bias
        value = jnp.maximum(value, value * 0.1)
        value = value.astype(jnp.bfloat16).astype(jnp.float32)
        if image == 0 and k == 0:
            value = jnp.where(top_ok, value, 0.0)
        if image == 0 and k == pairs - 1:
            value = jnp.where(end_ok, value, 0.0)
        return value

    def convolve(rows_in, n, depth):
        return jnp.dot(
            rows_in, wc[:depth, n * 256 : (n + 1) * 256], preferred_element_type=jnp.float32
        )

    def put(image, k, begin, value):
        store = (lf, rf)[image]
        edge = origin[image]
        end = begin + value.shape[0]
        if begin < edge:
            store[k, begin:edge, :] = value[: edge - begin, :] * left_ok
            value, begin = value[edge - begin :, :], edge
        if image == 0 and end > 8 + cols:
            store[k, 8 + cols : end, :] = value[8 + cols - begin :, :] * right_ok
            value = value[: 8 + cols - begin, :]
        store[k, begin : begin + value.shape[0], :] = value

    def place_lines(image, place):
        half = 2 * cin
        block = jnp.concatenate(
            [
                lines[side, place, image * half : (image + 1) * half, :].astype(jnp.float32)
                for side in range(2)
            ]
            * 3
            + [jnp.zeros((128 - 6 * half, cols), jnp.float32)],
            axis=0,
        ).T
        at = 8 + base
        if place == 0:
            keep = reach if image else 16
            at, block = at - keep, block[cols - keep :, :]
        elif place == 2:
            at, block = at + cols, block[:16, :]
        for step_x in range(3):
            begin = at + 1 - step_x
            some = slice(step_x * 2 * half, (step_x + 1) * 2 * half)
            ext[image, begin : begin + block.shape[0], some] = block[:, some]

    def build_right(k, begin, count):
        for delta in range(-2, 3):
            at = lead - D + delta + begin
            right_m[k, begin : begin + count, (delta + 2) * 128 : (delta + 3) * 128] = (
                rf[k, at : at + count, :].astype(jnp.bfloat16)
            )

    def build_left(k, chunks):
        for chunk in chunks:
            at = 7 + chunk * 16
            shifted = [lf[k, at + c : at + c + 16, :].reshape(2, 8, 128) for c in range(3)]
            for odd in range(2):
                for delta in range(-2, 3):
                    value = None
                    for c in range(3):
                        a = c - delta
                        if 0 <= a < 3:
                            term = shifted[c] * band_w[(a * 3 + c) * 2 + odd]
                            value = term if value is None else value + term
                    left_m[
                        k,
                        odd * cols + chunk * 16 : odd * cols + chunk * 16 + 16,
                        (delta + 2) * 128 : (delta + 3) * 128,
                    ] = value.reshape(16, 128).astype(jnp.bfloat16)

    def end_costs(tiles, begin):
        sums = []
        for last, first_d in ((0, 0), (1, D - 2)):
            total = None
            for j in range(2):
                d = first_d + j
                parts = []
                for k in tiles:
                    got = lf[k, :, :] * rf[k, lead - 8 - d : lead - 8 - d + wide_l, :]
                    parts.append(
                        jnp.concatenate(
                            [got[8:, :], jnp.zeros((256 - wide_l, 128), jnp.float32), got[:8, :]], axis=0
                        ).astype(jnp.bfloat16)
                    )
                term = lax.dot_general(
                    amat[j + 1 - last, :, begin * 128 : (begin + len(tiles)) * 128],
                    jnp.concatenate(parts, axis=1),
                    nt,
                    preferred_element_type=jnp.float32,
                )
                total = term if total is None else total + term
            sums.append(total)
        return sums

    chunks = cols // 16
    inner = len(inner_pairs) // 2
    strips = ((1, 0, lead + 8), (0, 0, 16), (1, span - 16, 16), (0, wide_l - 16, 16))

    def own_columns(pairs_in, n, depth):
        for image in range(2):
            first = origin[image] + 8
            total = convolve(lhs[image, first : first + local, :depth], n, depth)
            for j, k in enumerate(pairs_in):
                put(image, k, first, finish(total, j, k, image))
        for k in pairs_in:
            build_right(k, D + 16, cols - 32)
            build_left(k, range(1, chunks - 1))

    def other_columns(pairs_in, n, depth):
        rows_in = jnp.concatenate(
            [lhs[image, first : first + count, :depth] for image, first, count in strips], axis=0
        )
        total = convolve(rows_in, n, depth)
        for j, k in enumerate(pairs_in):
            at = 0
            for image, first, count in strips:
                put(image, k, first, finish(total[at : at + count, :], j, k, image))
                at += count
        for k in pairs_in:
            build_right(k, 0, D + 16)
            build_right(k, D + cols - 16, 16)
            build_left(k, [0, chunks - 1])

    for image in range(2):
        gather(image, origin[image] + 8, local)
    for n in range(inner):
        own_columns(inner_pairs[2 * n : 2 * n + 2], n, 3 * main)

    receive(lambda step: step[1] == 0)
    for image in range(2):
        place_lines(image, 1)
        gather_lines(image, origin[image] + 8, local)
    own_columns(outer_pairs, inner, 3 * main + 128)

    receive(lambda step: step[0] == 0)
    pt[1, base - reach : base, :] = near1[...].astype(jnp.float32)
    pt[0, base - 16 : base, :] = near0[...].astype(jnp.float32)
    pt[:, base + cols : base + cols + 16, :] = far[...].astype(jnp.float32)
    for image, first, count in strips:
        gather(image, first, count)
    for n in range(inner):
        other_columns(inner_pairs[2 * n : 2 * n + 2], n, 3 * main)
    inner_tiles = len(inner_pairs[::2])
    ends_inner = end_costs(inner_pairs[::2], 0)

    low_lane = lax.broadcasted_iota(jnp.int32, (D, cols), 1) < D
    lane8 = lax.broadcasted_iota(jnp.int32, (8, cols), 1)
    from_x = (lane8 - lax.broadcasted_iota(jnp.int32, (8, cols), 0)).astype(jnp.float32)
    jump = jnp.where(lane8 < D, float(D), -float(D))

    def attend(k):
        score = lax.dot_general(right_m[k], left_m[k], nt, preferred_element_type=jnp.float32)
        for odd in range(2):
            mine = slice(odd * cols, (odd + 1) * cols)
            outer = jnp.where(low_lane, score[:D, mine], score[2 * D :, mine]) + mask[0]
            inner = score[D : 2 * D, mine] + mask[1]
            outer = outer.reshape(D // 8, 8, cols)
            inner = inner.reshape(D // 8, 8, cols)
            best = jnp.maximum(jnp.max(outer, axis=0), jnp.max(inner, axis=0))
            outer = jnp.exp2(outer - best)
            both = outer + jnp.exp2(inner - best)
            tail, steps = both[D // 8 - 1], None
            for j in range(D // 8 - 2, -1, -1):
                steps = tail if steps is None else steps + tail
                tail = tail + both[j]
            moment = from_x * tail - 8.0 * steps + jump * jnp.sum(outer, axis=0)
            y = 2 * k + odd
            for j, value in enumerate((best, tail, moment)):
                part[j, y * 8 : (y + 1) * 8, :] = value

    for k in inner_pairs:
        attend(k)

    receive(lambda step: step[0] != 0 and step[1] != 0)
    for image in range(2):
        for place in (0, 2):
            place_lines(image, place)
    for image, first, count in strips:
        gather_lines(image, first, count)
    other_columns(outer_pairs, inner, 3 * main + 128)
    ends = []
    for total, more in zip(ends_inner, end_costs(outer_pairs, inner_tiles)):
        total = total + more
        value = total[rows : 2 * rows, :]
        value = value + pltpu.roll(total[:rows, :], 1, 1) + pltpu.roll(total[2 * rows :, :], 255, 1)
        ends.append(value[:, :cols])
    for k in outer_pairs:
        attend(k)

    for h in range(rows // 8):
        first = ends[0][h * 8 : (h + 1) * 8, :]
        last = ends[1][h * 8 : (h + 1) * 8, :]
        tops = [part[0, pl.ds(h * 64 + j, 8, stride=8), :] for j in range(8)]
        best = jnp.maximum(first, last)
        for top in tops:
            best = jnp.maximum(best, top)
        last = jnp.exp2(last - best)
        total = jnp.exp2(first - best) + last
        moment = last * float(D - 1)
        for j in range(8):
            weight = jnp.exp2(tops[j] - best)
            total = total + weight * part[1, pl.ds(h * 64 + j, 8, stride=8), :]
            moment = moment + weight * part[2, pl.ds(h * 64 + j, 8, stride=8), :]
        out_ref[h * 8 : (h + 1) * 8, :] = moment / total / D

    for step, copy in copies:

        @pl.when(exists(step))
        def _(copy=copy):
            copy.wait_send()


def on_device(images, conv_weight, conv_bias, agg_weight):
    cin, rows, cols = images.shape[1:]
    groups = agg_weight.shape[0]
    per = conv_weight.shape[0] // groups
    main = rows * cin
    pairs = rows // 2
    span = cols + D + 16
    reach = -(-(D + 2) // 16) * 16
    return pl.pallas_call(
        functools.partial(body, (rows, cols, groups, per, cin)),
        out_shape=pltpu.VMEM((rows, cols), jnp.float32),
        in_specs=[pl.BlockSpec(memory_space=pl.ANY)] * 4,
        out_specs=pl.BlockSpec(memory_space=pltpu.VMEM),
        scratch_shapes=[
            pltpu.VMEM(images.shape, images.dtype),
            pltpu.VMEM(conv_weight.shape, conv_weight.dtype),
            pltpu.VMEM((1,) + conv_bias.shape, conv_bias.dtype),
            pltpu.VMEM(agg_weight.shape, agg_weight.dtype),
            pltpu.SemaphoreType.DMA((4,)),
            pltpu.VMEM((2, span + 16, main), jnp.float32),
            pltpu.VMEM((2, span + 32, 128), jnp.float32),
            pltpu.VMEM((2, span, 3 * main + 128), jnp.bfloat16),
            pltpu.VMEM((3 * main + 128, pairs * 128), jnp.bfloat16),
            pltpu.VMEM((3, 3 * rows, (pairs // 2 + 1) * 128), jnp.bfloat16),
            pltpu.VMEM((9 * cin, 128), jnp.float32),
            pltpu.VMEM((18, 8, 128), jnp.float32),
            pltpu.VMEM((2, D, cols), jnp.float32),
            pltpu.VMEM((pairs, cols + 16, 128), jnp.float32),
            pltpu.VMEM((pairs, span, 128), jnp.float32),
            pltpu.VMEM((pairs, 2 * cols, 640), jnp.bfloat16),
            pltpu.VMEM((pairs, D + cols, 640), jnp.bfloat16),
            pltpu.VMEM((3, rows * 8, cols), jnp.float32),
            pltpu.VMEM((2, cols, main), jnp.bfloat16),
            pltpu.VMEM((2, 4 * cin, cols), jnp.bfloat16),
            pltpu.VMEM((16, main), jnp.bfloat16),
            pltpu.VMEM((reach, main), jnp.bfloat16),
            pltpu.VMEM((2, 16, main), jnp.bfloat16),
            pltpu.VMEM((2, 3, 4 * cin, cols), jnp.bfloat16),
            pltpu.SemaphoreType.DMA((9,)),
            pltpu.SemaphoreType.DMA((9,)),
            pltpu.SemaphoreType.REGULAR,
        ],
        compiler_params=pltpu.CompilerParams(collective_id=0, has_side_effects=True),
    )(images, conv_weight, conv_bias[None], agg_weight)


def solution(mesh):
    in_specs = (P("pairs", None, "row", "col"), P(), P(), P())
    out_specs = P(("pairs", "row"), "col")
    return jax.shard_map(
        on_device, mesh=mesh, in_specs=in_specs, out_specs=out_specs, check_vma=False
    )
```

```python
import functools

import jax
import jax.numpy as jnp
from jax import lax
from jax.experimental import pallas as pl
from jax.experimental.pallas import tpu as pltpu
from jax.sharding import PartitionSpec as P

D = 64
LOG2E = 1.4426950408889634


MESH = pl.DeviceIdType.MESH
STEPS = ((0, 1), (0, -1), (1, 0), (-1, 0), (1, 1), (1, -1), (-1, 1), (-1, -1))


def body(
    shape, images_hbm, weight_hbm, bias_hbm, agg_hbm, out_ref,
    images_ref, weight_ref, bias_in, agg_in, load_sem,
    pt, ext, lhs, wc, end_w, end_in, end_sum, taps_ref, band_w, mask, lf, rf, left_m, right_m, part,
    tr_ref, edge_ref, near0, near1, far, lines, send_sem, recv_sem, ready,
):
    rows, cols, groups, per, cin = shape
    feats = groups * per
    pairs = rows // 2
    lead = D + 8
    span = rf.shape[1]
    wide_l = lf.shape[1]
    rows_axis, cols_axis = lax.axis_size("row"), lax.axis_size("col")
    my_row, my_col = lax.axis_index("row"), lax.axis_index("col")
    reach = near1.shape[0]

    def exists(step):
        r, c = my_row + step[0], my_col + step[1]
        return (r >= 0) & (r < rows_axis) & (c >= 0) & (c < cols_axis)

    def device(step):
        return {"row": my_row + step[0], "col": my_col + step[1]}

    barrier = pltpu.get_barrier_semaphore()
    for step in STEPS:
        if step[1] >= 0:

            @pl.when(exists(step))
            def _(step=step):
                pl.semaphore_signal(barrier, inc=1, device_id=device(step), device_id_type=MESH)

    loads = [
        pltpu.make_async_copy(source, target, load_sem.at[k])
        for k, (source, target) in enumerate(
            ((images_hbm, images_ref), (weight_hbm, weight_ref), (bias_hbm, bias_in), (agg_hbm, agg_in))
        )
    ]
    for load in loads:
        load.start()
    tall = 1 + (my_row > 0).astype(jnp.int32) + (my_row < rows_axis - 1).astype(jnp.int32)
    pl.semaphore_wait(barrier, tall - 1 + jnp.where(my_col > 0, tall, 0))
    for step in STEPS:
        if step[1] < 0:

            @pl.when(exists(step))
            def _(step=step):
                pl.semaphore_signal(ready, inc=1, device_id=device(step), device_id_type=MESH)

    for load in loads:
        load.wait()

    main = rows * cin
    for image in range(2):
        flat = images_ref[image].reshape(main, cols)
        tr_ref[image] = flat.T.astype(jnp.bfloat16)
        for side, first in ((0, 0), (1, rows - 2)):
            pair = [images_ref[image, :, first + y, :] for y in range(2)]
            edge_ref[side, image * 2 * cin : (image + 1) * 2 * cin, :] = jnp.concatenate(
                pair, axis=0
            ).astype(jnp.bfloat16)

    plan = [
        ((0, 1), tr_ref.at[1, pl.ds(cols - reach, reach), :], near1),
        ((0, 1), tr_ref.at[0, pl.ds(cols - 16, 16), :], near0),
        ((0, -1), tr_ref.at[:, pl.ds(0, 16), :], far),
    ]
    for r in (1, -1):
        side = 0 if r == 1 else 1
        for c in (0, 1, -1):
            plan.append(((r, c), edge_ref.at[1 - side], lines.at[side, 1 - c]))
    copies = []
    for k, (step, source, target) in enumerate(plan):
        copy = pltpu.make_async_remote_copy(
            src_ref=source,
            dst_ref=target,
            send_sem=send_sem.at[k],
            recv_sem=recv_sem.at[k],
            device_id=device(step),
            device_id_type=MESH,
        )
        copies.append((step, copy))

        @pl.when(jnp.logical_not(exists((-step[0], -step[1]))))
        def _(target=target):
            target[...] = jnp.zeros(target.shape, target.dtype)

    def send(chosen):
        for step, copy in copies:
            if chosen(step):

                @pl.when(exists(step))
                def _(copy=copy):
                    copy.start()

    def receive(chosen):
        for step, copy in copies:
            if chosen(step):

                @pl.when(exists((-step[0], -step[1])))
                def _(copy=copy):
                    copy.wait_recv()

    send(lambda step: step[1] <= 0)

    tn = (((0,), (0,)), ((), ()))
    nt = (((1,), (1,)), ((), ()))
    tile = (rows, 128)
    lane = lax.broadcasted_iota(jnp.int32, tile, 1)
    line = lane // feats
    spread = (
        lax.broadcasted_iota(jnp.int32, (feats, 128), 1) % feats
        == lax.broadcasted_iota(jnp.int32, (feats, 128), 0)
    ).astype(jnp.float32)
    one = (
        lax.broadcasted_iota(jnp.int32, (groups, 128), 1) % feats // per
        == lax.broadcasted_iota(jnp.int32, (groups, 128), 0)
    ).astype(jnp.float32)
    exact = dict(precision=lax.Precision.HIGHEST, preferred_element_type=jnp.float32)
    bias = jnp.dot(bias_in[...], spread, **exact)
    taps_ref[...] = lax.dot_general(
        weight_ref[...].astype(jnp.float32), spread, tn, preferred_element_type=jnp.float32
    )
    agg = lax.dot_general(agg_in[...], one, tn, **exact) * (LOG2E / per)

    above = lax.broadcasted_iota(jnp.int32, tile, 0) - line + 2
    near_line = line[:cin]
    inner_pairs, outer_pairs = list(range(1, pairs - 1)), [0, pairs - 1]
    for n, k in enumerate(inner_pairs + outer_pairs):
        columns = slice(n * 128, (n + 1) * 128)
        hit = [above == step_y + 2 * k for step_y in range(3)]
        for step_x in range(3):
            for c in range(cin):
                value = jnp.zeros(tile, jnp.float32)
                for step_y in range(3):
                    at = (step_y * 3 + step_x) * cin + c
                    value = jnp.where(hit[step_y], taps_ref[at : at + 1, :], value)
                begin = step_x * main + c * rows
                wc[begin : begin + rows, columns] = value.astype(jnp.bfloat16)
        if k in outer_pairs:
            for step_x in range(3):
                for side in range(2):
                    halves = []
                    for y in range(2):
                        row = y - 2 if side == 0 else rows + y
                        value = jnp.zeros((cin, 128), jnp.float32)
                        for step_y in range(3):
                            at = (step_y * 3 + step_x) * cin
                            value = jnp.where(
                                near_line == row - 2 * k + 2 - step_y, taps_ref[at : at + cin, :], value
                            )
                        halves.append(value)
                    begin = 3 * main + (step_x * 2 + side) * 2 * cin
                    wc[begin : begin + 2 * cin, columns] = (
                        jnp.concatenate(halves, axis=0).astype(jnp.bfloat16)
                    )
            begin = 3 * main + 12 * cin
            wc[begin:, columns] = jnp.zeros((wc.shape[0] - begin, 128), jnp.bfloat16)

    for step_d in range(3):
        for step_x in range(3):
            for odd in range(2):
                value = jnp.zeros((8, 128), jnp.float32)
                for step_y in range(3):
                    at = 9 * step_d + 3 * step_y + step_x
                    value = jnp.where(line[:8] == step_y + odd, agg[at : at + 1, :], value)
                band_w[(step_d * 3 + step_x) * 2 + odd] = value

    once = inner_pairs[::2] + outer_pairs
    at_x = lax.broadcasted_iota(jnp.int32, (D, cols), 1)
    at_i = lax.broadcasted_iota(jnp.int32, (D, cols), 0)
    low = at_x < D
    for j, apart in enumerate((jnp.where(low, at_x - at_i + D, at_x - at_i - D), at_x - at_i)):
        mask[j] = jnp.where((apart >= 1) & (apart <= D - 2), 0.0, -jnp.inf)

    base = 16 + D
    pt[:, base : base + cols, :] = tr_ref[...].astype(jnp.float32)
    ext[:, :, 12 * cin :] = jnp.zeros((2, span + 32, 128 - 12 * cin), jnp.float32)

    @pl.when(my_col < cols_axis - 1)
    def _():
        pl.semaphore_wait(ready, tall)

    send(lambda step: step[1] > 0)

    behind = line - lax.broadcasted_iota(jnp.int32, tile, 0)
    for t, k in enumerate(once):
        hit = [behind == step_y - 2 * k for step_y in range(3)]
        if k == 0:
            hit = [h & (line < 2) for h in hit]
        taps = []
        for step_d in range(3):
            pieces = []
            for step_x in range(3):
                value = jnp.zeros(tile, jnp.float32)
                for step_y in range(3):
                    at = 9 * step_d + 3 * step_y + step_x
                    value = jnp.where(hit[step_y], agg[at : at + 1, :], value)
                pieces.append(value)
            taps.append(pieces)
        gap = [jnp.zeros(tile, jnp.float32)] * (4 - 3)
        none = [jnp.zeros((64, 128), jnp.float32)]
        for j, (step_d, high) in enumerate(((1, 0), (2, 0), (0, 1), (1, 1))):
            some = taps[step_d] + gap
            value = jnp.concatenate(none + some if high else some + none, axis=0)
            end_w[j, t * 128 : (t + 1) * 128, :] = value.T.astype(jnp.bfloat16)

    left_ok = (my_col > 0).astype(jnp.float32)
    right_ok = (my_col < cols_axis - 1).astype(jnp.float32)
    top_ok = (my_row > 0) | (line[:1] > 0)
    end_ok = (my_row < rows_axis - 1) | (line[:1] < 3)
    base = 16 + D
    counts = (wide_l, span)
    origin = (8, lead)
    local = cols - 16

    def gather(image, first, count):
        begin = 8 + origin[1] - origin[image] + first
        for step_x in range(3):
            at = begin + step_x - 1
            lhs[image, first : first + count, step_x * main : (step_x + 1) * main] = (
                pt[image, at : at + count, :].astype(jnp.bfloat16)
            )

    def gather_lines(image, first, count):
        at = 16 + origin[1] - origin[image] + first
        lhs[image, first : first + count, 3 * main :] = ext[image, at : at + count, :].astype(jnp.bfloat16)

    def finish(total, j, k, image):
        value = total[:, j * 128 : (j + 1) * 128] + bias
        value = jnp.maximum(value, value * 0.1)
        value = value.astype(jnp.bfloat16).astype(jnp.float32)
        if image == 0 and k == 0:
            value = jnp.where(top_ok, value, 0.0)
        if image == 0 and k == pairs - 1:
            value = jnp.where(end_ok, value, 0.0)
        return value

    def convolve(rows_in, n, depth):
        return jnp.dot(
            rows_in, wc[:depth, n * 256 : (n + 1) * 256], preferred_element_type=jnp.float32
        )

    def put(image, k, begin, value):
        store = (lf, rf)[image]
        edge = origin[image]
        end = begin + value.shape[0]
        if begin < edge:
            store[k, begin:edge, :] = value[: edge - begin, :] * left_ok
            value, begin = value[edge - begin :, :], edge
        if image == 0 and end > 8 + cols:
            store[k, 8 + cols : end, :] = value[8 + cols - begin :, :] * right_ok
            value = value[: 8 + cols - begin, :]
        store[k, begin : begin + value.shape[0], :] = value

    def place_lines(image, place):
        half = 2 * cin
        block = jnp.concatenate(
            [
                lines[side, place, image * half : (image + 1) * half, :].astype(jnp.float32)
                for side in range(2)
            ]
            * 3
            + [jnp.zeros((128 - 6 * half, cols), jnp.float32)],
            axis=0,
        ).T
        at = 8 + base
        if place == 0:
            keep = reach if image else 16
            at, block = at - keep, block[cols - keep :, :]
        elif place == 2:
            at, block = at + cols, block[:16, :]
        for step_x in range(3):
            begin = at + 1 - step_x
            some = slice(step_x * 2 * half, (step_x + 1) * 2 * half)
            ext[image, begin : begin + block.shape[0], some] = block[:, some]

    def build_right(k, begin, count):
        for delta in range(-2, 3):
            at = lead - D + delta + begin
            right_m[k, begin : begin + count, (delta + 2) * 128 : (delta + 3) * 128] = (
                rf[k, at : at + count, :].astype(jnp.bfloat16)
            )

    def build_left(k, chunks):
        for chunk in chunks:
            at = 7 + chunk * 16
            shifted = [lf[k, at + c : at + c + 16, :].reshape(2, 8, 128) for c in range(3)]
            for odd in range(2):
                for delta in range(-2, 3):
                    value = None
                    for c in range(3):
                        a = c - delta
                        if 0 <= a < 3:
                            term = shifted[c] * band_w[(a * 3 + c) * 2 + odd]
                            value = term if value is None else value + term
                    left_m[
                        k,
                        odd * cols + chunk * 16 : odd * cols + chunk * 16 + 16,
                        (delta + 2) * 128 : (delta + 3) * 128,
                    ] = value.reshape(16, 128).astype(jnp.bfloat16)

    def end_product(k, d, x, count):
        return lf[k, 8 + x : 8 + x + count, :] * rf[k, lead + x - d : lead + x - d + count, :]

    def build_ends(own, k):
        if k not in once:
            return
        columns = slice(once.index(k) * 128, (once.index(k) + 1) * 128)
        gap = jnp.zeros((8, 128), jnp.float32)
        for j, d in enumerate((0, 1, D - 2, D - 1)):
            reached = 16 if j < 2 else D + 16
            if own:
                spans = [(reached, cols - 16 - reached)]
            else:
                spans = [(0, reached), (cols - 16, 16)]
                block = jnp.concatenate([gap, end_product(k, d, -8, 8)], axis=0)
                end_in[j, 0:16, columns] = block.astype(jnp.bfloat16)
                block = jnp.concatenate([end_product(k, d, cols, 8), gap], axis=0)
                end_in[j, 16 + cols :, columns] = block.astype(jnp.bfloat16)
            for x, count in spans:
                end_in[j, 16 + x : 16 + x + count, columns] = end_product(k, d, x, count).astype(jnp.bfloat16)

    chunks = cols // 16
    inner = len(inner_pairs) // 2
    strips = ((1, 0, lead + 8), (0, 0, 16), (1, span - 16, 16), (0, wide_l - 16, 16))

    def own_columns(pairs_in, n, depth):
        for image in range(2):
            first = origin[image] + 8
            total = convolve(lhs[image, first : first + local, :depth], n, depth)
            for j, k in enumerate(pairs_in):
                put(image, k, first, finish(total, j, k, image))
        for k in pairs_in:
            build_right(k, D + 16, cols - 32)
            build_left(k, range(1, chunks - 1))
            build_ends(True, k)

    def other_columns(pairs_in, n, depth):
        rows_in = jnp.concatenate(
            [lhs[image, first : first + count, :depth] for image, first, count in strips], axis=0
        )
        total = convolve(rows_in, n, depth)
        for j, k in enumerate(pairs_in):
            at = 0
            for image, first, count in strips:
                put(image, k, first, finish(total[at : at + count, :], j, k, image))
                at += count
        for k in pairs_in:
            build_right(k, 0, D + 16)
            build_right(k, D + cols - 16, 16)
            build_left(k, [0, chunks - 1])
            build_ends(False, k)

    for image in range(2):
        gather(image, origin[image] + 8, local)
    for n in range(inner):
        own_columns(inner_pairs[2 * n : 2 * n + 2], n, 3 * main)

    receive(lambda step: step[1] == 0)
    for image in range(2):
        place_lines(image, 1)
        gather_lines(image, origin[image] + 8, local)
    own_columns(outer_pairs, inner, 3 * main + 128)

    receive(lambda step: step[1] != 0)
    pt[1, base - reach : base, :] = near1[...].astype(jnp.float32)
    pt[0, base - 16 : base, :] = near0[...].astype(jnp.float32)
    pt[:, base + cols : base + cols + 16, :] = far[...].astype(jnp.float32)
    for image, first, count in strips:
        gather(image, first, count)
    for image in range(2):
        for place in (0, 2):
            place_lines(image, place)
    for image, first, count in strips:
        gather_lines(image, first, count)
    for n in range(inner):
        other_columns(inner_pairs[2 * n : 2 * n + 2], n, 3 * main)
    other_columns(outer_pairs, inner, 3 * main + 128)
    total = None
    for j in range(4):
        term = jnp.dot(end_in[j], end_w[j], preferred_element_type=jnp.float32)
        total = term if total is None else total + term
    end_sum[...] = total
    place = lax.broadcasted_iota(jnp.int32, (cols, 128), 1) % 64 // 16
    total = end_sum[15 : 15 + cols, :]
    for step_x in (1, 2):
        total = jnp.where(place == step_x, end_sum[15 + step_x : 15 + step_x + cols, :], total)
    total = total.T
    ends = []
    for j in (0, 64):
        ends.append(total[j : j + 16, :] + total[j + 16 : j + 32, :] + total[j + 32 : j + 48, :])

    low_lane = lax.broadcasted_iota(jnp.int32, (D, cols), 1) < D
    lane8 = lax.broadcasted_iota(jnp.int32, (8, cols), 1)
    from_x = (lane8 - lax.broadcasted_iota(jnp.int32, (8, cols), 0)).astype(jnp.float32)
    jump = jnp.where(lane8 < D, float(D), -float(D))

    def attend(k):
        score = lax.dot_general(right_m[k], left_m[k], nt, preferred_element_type=jnp.float32)
        for odd in range(2):
            mine = slice(odd * cols, (odd + 1) * cols)
            outer = jnp.where(low_lane, score[:D, mine], score[2 * D :, mine]) + mask[0]
            inner = score[D : 2 * D, mine] + mask[1]
            outer = outer.reshape(D // 8, 8, cols)
            inner = inner.reshape(D // 8, 8, cols)
            best = jnp.maximum(jnp.max(outer, axis=0), jnp.max(inner, axis=0))
            outer = jnp.exp2(outer - best)
            both = outer + jnp.exp2(inner - best)
            tail, steps = both[D // 8 - 1], None
            for j in range(D // 8 - 2, -1, -1):
                steps = tail if steps is None else steps + tail
                tail = tail + both[j]
            moment = from_x * tail - 8.0 * steps + jump * jnp.sum(outer, axis=0)
            y = 2 * k + odd
            for j, value in enumerate((best, tail, moment)):
                part[j, y * 8 : (y + 1) * 8, :] = value

    for k in inner_pairs:
        attend(k)

    for k in outer_pairs:
        attend(k)

    for h in range(rows // 8):
        first = ends[0][h * 8 : (h + 1) * 8, :]
        last = ends[1][h * 8 : (h + 1) * 8, :]
        tops = [part[0, pl.ds(h * 64 + j, 8, stride=8), :] for j in range(8)]
        best = jnp.maximum(first, last)
        for top in tops:
            best = jnp.maximum(best, top)
        last = jnp.exp2(last - best)
        total = jnp.exp2(first - best) + last
        moment = last * float(D - 1)
        for j in range(8):
            weight = jnp.exp2(tops[j] - best)
            total = total + weight * part[1, pl.ds(h * 64 + j, 8, stride=8), :]
            moment = moment + weight * part[2, pl.ds(h * 64 + j, 8, stride=8), :]
        out_ref[h * 8 : (h + 1) * 8, :] = moment / total / D

    for step, copy in copies:

        @pl.when(exists(step))
        def _(copy=copy):
            copy.wait_send()


def on_device(images, conv_weight, conv_bias, agg_weight):
    cin, rows, cols = images.shape[1:]
    groups = agg_weight.shape[0]
    per = conv_weight.shape[0] // groups
    main = rows * cin
    pairs = rows // 2
    span = cols + D + 16
    reach = -(-(D + 2) // 16) * 16
    return pl.pallas_call(
        functools.partial(body, (rows, cols, groups, per, cin)),
        out_shape=pltpu.VMEM((rows, cols), jnp.float32),
        in_specs=[pl.BlockSpec(memory_space=pl.ANY)] * 4,
        out_specs=pl.BlockSpec(memory_space=pltpu.VMEM),
        scratch_shapes=[
            pltpu.VMEM(images.shape, images.dtype),
            pltpu.VMEM(conv_weight.shape, conv_weight.dtype),
            pltpu.VMEM((1,) + conv_bias.shape, conv_bias.dtype),
            pltpu.VMEM(agg_weight.shape, agg_weight.dtype),
            pltpu.SemaphoreType.DMA((4,)),
            pltpu.VMEM((2, span + 16, main), jnp.float32),
            pltpu.VMEM((2, span + 32, 128), jnp.float32),
            pltpu.VMEM((2, span, 3 * main + 128), jnp.bfloat16),
            pltpu.VMEM((3 * main + 128, pairs * 128), jnp.bfloat16),
            pltpu.VMEM((4, (pairs // 2 + 1) * 128, 128), jnp.bfloat16),
            pltpu.VMEM((4, cols + 32, (pairs // 2 + 1) * 128), jnp.bfloat16),
            pltpu.VMEM((cols + 32, 128), jnp.float32),
            pltpu.VMEM((9 * cin, 128), jnp.float32),
            pltpu.VMEM((18, 8, 128), jnp.float32),
            pltpu.VMEM((2, D, cols), jnp.float32),
            pltpu.VMEM((pairs, cols + 16, 128), jnp.float32),
            pltpu.VMEM((pairs, span, 128), jnp.float32),
            pltpu.VMEM((pairs, 2 * cols, 640), jnp.bfloat16),
            pltpu.VMEM((pairs, D + cols, 640), jnp.bfloat16),
            pltpu.VMEM((3, rows * 8, cols), jnp.float32),
            pltpu.VMEM((2, cols, main), jnp.bfloat16),
            pltpu.VMEM((2, 4 * cin, cols), jnp.bfloat16),
            pltpu.VMEM((16, main), jnp.bfloat16),
            pltpu.VMEM((reach, main), jnp.bfloat16),
            pltpu.VMEM((2, 16, main), jnp.bfloat16),
            pltpu.VMEM((2, 3, 4 * cin, cols), jnp.bfloat16),
            pltpu.SemaphoreType.DMA((9,)),
            pltpu.SemaphoreType.DMA((9,)),
            pltpu.SemaphoreType.REGULAR,
        ],
        compiler_params=pltpu.CompilerParams(collective_id=0, has_side_effects=True),
    )(images, conv_weight, conv_bias[None], agg_weight)


def solution(mesh):
    in_specs = (P("pairs", None, "row", "col"), P(), P(), P())
    out_specs = P(("pairs", "row"), "col")
    return jax.shard_map(
        on_device, mesh=mesh, in_specs=in_specs, out_specs=out_specs, check_vma=False
    )
```

```python
import functools

import jax
import jax.numpy as jnp
from jax import lax
from jax.experimental import pallas as pl
from jax.experimental.pallas import tpu as pltpu
from jax.sharding import PartitionSpec as P

D = 64
LOG2E = 1.4426950408889634


MESH = pl.DeviceIdType.MESH
STEPS = ((0, 1), (0, -1), (1, 0), (-1, 0), (1, 1), (1, -1), (-1, 1), (-1, -1))


def body(
    shape, images_hbm, weight_hbm, bias_hbm, agg_hbm, out_ref,
    images_ref, weight_ref, bias_in, agg_in, load_sem,
    pt, ext, lhs, wc, end_w, end_in, end_sum, ends, taps_ref, band_w, mask, lf, rf, left_m, right_m, part, strip_out,
    tr_ref, edge_ref, near0, near1, far, lines, send_sem, recv_sem, ready,
):
    rows, cols, groups, per, cin = shape
    feats = groups * per
    pairs = rows // 2
    lead = D + 8
    span = rf.shape[1]
    wide_l = lf.shape[1]
    rows_axis, cols_axis = lax.axis_size("row"), lax.axis_size("col")
    my_row, my_col = lax.axis_index("row"), lax.axis_index("col")
    reach = near1.shape[0]

    def exists(step):
        r, c = my_row + step[0], my_col + step[1]
        return (r >= 0) & (r < rows_axis) & (c >= 0) & (c < cols_axis)

    def device(step):
        return {"row": my_row + step[0], "col": my_col + step[1]}

    odd_row = lax.rem(my_row, 2) == 1
    even_row = jnp.logical_not(odd_row)
    beside, later, earlier = ((1, 0), (-1, 0)), ((0, 1), (1, 1), (-1, 1)), ((0, -1), (1, -1), (-1, -1))

    barrier = pltpu.get_barrier_semaphore()
    for step in later + beside:
        allowed = exists(step) if step in later else exists(step) & odd_row

        @pl.when(allowed)
        def _(step=step):
            pl.semaphore_signal(barrier, inc=1, device_id=device(step), device_id_type=MESH)

    quarter = cin // 2
    loads = [
        pltpu.make_async_copy(
            images_hbm.at[image, pl.ds(part_at, quarter)],
            images_ref.at[image, pl.ds(part_at, quarter)],
            load_sem.at[2 * image + part_at // quarter],
        )
        for image in range(2)
        for part_at in (0, quarter)
    ]
    small_loads = [
        pltpu.make_async_copy(source, target, load_sem.at[4 + k])
        for k, (source, target) in enumerate(
            ((weight_hbm, weight_ref), (bias_hbm, bias_in), (agg_hbm, agg_in))
        )
    ]
    for load in loads + small_loads:
        load.start()
    tall = 1 + (my_row > 0).astype(jnp.int32) + (my_row < rows_axis - 1).astype(jnp.int32)
    greeted = jnp.where(my_col > 0, tall, 0) + jnp.where(even_row, tall - 1, 0)

    @pl.when(greeted > 0)
    def _():
        pl.semaphore_wait(barrier, greeted)

    for n, step in enumerate(earlier):

        @pl.when(exists(step))
        def _(n=n, step=step):
            pl.semaphore_signal(ready.at[n], inc=1, device_id=device(step), device_id_type=MESH)

    for step in beside:

        @pl.when(exists(step) & even_row)
        def _(step=step):
            pl.semaphore_signal(ready.at[3], inc=1, device_id=device(step), device_id_type=MESH)

    for load in loads:
        load.wait()

    main = rows * cin
    for image in range(2):
        for side, first in ((0, 0), (1, rows - 2)):
            pair = [images_ref[image, :, first + y, :] for y in range(2)]
            edge_ref[side, image * 2 * cin : (image + 1) * 2 * cin, :] = jnp.concatenate(
                pair, axis=0
            ).astype(jnp.bfloat16)

    plan = [
        ((0, 1), tr_ref.at[1, pl.ds(cols - reach, reach), :], near1),
        ((0, 1), tr_ref.at[0, pl.ds(cols - 16, 16), :], near0),
        ((0, -1), tr_ref.at[:, pl.ds(0, 16), :], far),
    ]
    for r in (1, -1):
        side = 0 if r == 1 else 1
        for c in (0, 1, -1):
            plan.append(((r, c), edge_ref.at[1 - side], lines.at[side, 1 - c]))
    copies = []
    for k, (step, source, target) in enumerate(plan):
        copy = pltpu.make_async_remote_copy(
            src_ref=source,
            dst_ref=target,
            send_sem=send_sem.at[k],
            recv_sem=recv_sem.at[k],
            device_id=device(step),
            device_id_type=MESH,
        )
        copies.append((step, copy))

    def send(chosen):
        for step, copy in copies:
            if chosen(step):

                @pl.when(exists(step))
                def _(copy=copy):
                    copy.start()

    def receive(chosen):
        for step, copy in copies:
            if chosen(step):

                @pl.when(exists((-step[0], -step[1])))
                def _(copy=copy):
                    copy.wait_recv()

    send(lambda step: step in earlier[1:])
    for image in range(2):
        tr_ref[image] = images_ref[image].reshape(main, cols).T.astype(jnp.bfloat16)
    send(lambda step: step == earlier[0])

    @pl.when(even_row)
    def _():
        send(lambda step: step in beside)

    for k, (step, source, target) in enumerate(plan):

        @pl.when(jnp.logical_not(exists((-step[0], -step[1]))))
        def _(target=target):
            target[...] = jnp.zeros(target.shape, target.dtype)

    for load in small_loads:
        load.wait()


    tn = (((0,), (0,)), ((), ()))
    nt = (((1,), (1,)), ((), ()))
    tile = (rows, 128)
    lane = lax.broadcasted_iota(jnp.int32, tile, 1)
    line = lane // feats
    spread = (
        lax.broadcasted_iota(jnp.int32, (feats, 128), 1) % feats
        == lax.broadcasted_iota(jnp.int32, (feats, 128), 0)
    ).astype(jnp.float32)
    one = (
        lax.broadcasted_iota(jnp.int32, (groups, 128), 1) % feats // per
        == lax.broadcasted_iota(jnp.int32, (groups, 128), 0)
    ).astype(jnp.float32)
    exact = dict(precision=lax.Precision.HIGHEST, preferred_element_type=jnp.float32)
    bias = jnp.dot(bias_in[...], spread, **exact)
    taps_ref[...] = lax.dot_general(
        weight_ref[...].astype(jnp.float32), spread, tn, preferred_element_type=jnp.float32
    )
    agg = lax.dot_general(agg_in[...], one, tn, **exact) * (LOG2E / per)

    above = lax.broadcasted_iota(jnp.int32, tile, 0) - line + 2
    near_line = line[:cin]
    inner_pairs, outer_pairs = list(range(1, pairs - 1)), [0, pairs - 1]
    for n, k in enumerate(inner_pairs + outer_pairs):
        columns = slice(n * 128, (n + 1) * 128)
        hit = [above == step_y + 2 * k for step_y in range(3)]
        for step_x in range(3):
            for c in range(cin):
                value = jnp.zeros(tile, jnp.float32)
                for step_y in range(3):
                    at = (step_y * 3 + step_x) * cin + c
                    value = jnp.where(hit[step_y], taps_ref[at : at + 1, :], value)
                begin = step_x * main + c * rows
                wc[begin : begin + rows, columns] = value.astype(jnp.bfloat16)
        if k in outer_pairs:
            for step_x in range(3):
                for side in range(2):
                    halves = []
                    for y in range(2):
                        row = y - 2 if side == 0 else rows + y
                        value = jnp.zeros((cin, 128), jnp.float32)
                        for step_y in range(3):
                            at = (step_y * 3 + step_x) * cin
                            value = jnp.where(
                                near_line == row - 2 * k + 2 - step_y, taps_ref[at : at + cin, :], value
                            )
                        halves.append(value)
                    begin = 3 * main + (step_x * 2 + side) * 2 * cin
                    wc[begin : begin + 2 * cin, columns] = (
                        jnp.concatenate(halves, axis=0).astype(jnp.bfloat16)
                    )
            begin = 3 * main + 12 * cin
            wc[begin:, columns] = jnp.zeros((wc.shape[0] - begin, 128), jnp.bfloat16)

    for step_d in range(3):
        for step_x in range(3):
            for odd in range(2):
                value = jnp.zeros((8, 128), jnp.float32)
                for step_y in range(3):
                    at = 9 * step_d + 3 * step_y + step_x
                    value = jnp.where(line[:8] == step_y + odd, agg[at : at + 1, :], value)
                band_w[(step_d * 3 + step_x) * 2 + odd] = value

    once = inner_pairs[::2] + outer_pairs
    at_x = lax.broadcasted_iota(jnp.int32, (D, cols), 1)
    at_i = lax.broadcasted_iota(jnp.int32, (D, cols), 0)
    low = at_x < D
    for j, apart in enumerate((jnp.where(low, at_x - at_i + D, at_x - at_i - D), at_x - at_i)):
        mask[j] = jnp.where((apart >= 1) & (apart <= D - 2), 0.0, -jnp.inf)

    base = 16 + D
    pt[:, base : base + cols, :] = tr_ref[...].astype(jnp.float32)
    ext[:, :, 12 * cin :] = jnp.zeros((2, span + 32, 128 - 12 * cin), jnp.float32)

    @pl.when(my_col == 0)
    def _():
        right_m[:, D + cols - 16 :, :] = jnp.zeros((pairs, 16, 640), jnp.bfloat16)

    left_ok = (my_col > 0).astype(jnp.float32)
    right_ok = (my_col < cols_axis - 1).astype(jnp.float32)
    top_ok = (my_row > 0) | (line[:1] > 0)
    end_ok = (my_row < rows_axis - 1) | (line[:1] < 3)
    base = 16 + D
    counts = (wide_l, span)
    origin = (8, lead)
    local = cols - 16

    def gather(image, first, count):
        begin = 8 + origin[1] - origin[image] + first
        for step_x in range(3):
            at = begin + step_x - 1
            lhs[image, first : first + count, step_x * main : (step_x + 1) * main] = (
                pt[image, at : at + count, :].astype(jnp.bfloat16)
            )

    def gather_lines(image, first, count):
        at = 16 + origin[1] - origin[image] + first
        lhs[image, first : first + count, 3 * main :] = ext[image, at : at + count, :].astype(jnp.bfloat16)

    def finish(total, j, k, image):
        value = total[:, j * 128 : (j + 1) * 128] + bias
        value = jnp.maximum(value, value * 0.1)
        value = value.astype(jnp.bfloat16).astype(jnp.float32)
        if image == 0 and k == 0:
            value = jnp.where(top_ok, value, 0.0)
        if image == 0 and k == pairs - 1:
            value = jnp.where(end_ok, value, 0.0)
        return value

    def convolve(rows_in, n, depth):
        return jnp.dot(
            rows_in, wc[:depth, n * 256 : (n + 1) * 256], preferred_element_type=jnp.float32
        )

    def put(image, k, begin, value):
        store = (lf, rf)[image]
        edge = origin[image]
        end = begin + value.shape[0]
        if begin < edge:
            store[k, begin:edge, :] = value[: edge - begin, :] * left_ok
            value, begin = value[edge - begin :, :], edge
        if image == 0 and end > 8 + cols:
            store[k, 8 + cols : end, :] = value[8 + cols - begin :, :] * right_ok
            value = value[: 8 + cols - begin, :]
        store[k, begin : begin + value.shape[0], :] = value

    def place_lines(image, place):
        half = 2 * cin
        block = jnp.concatenate(
            [
                lines[side, place, image * half : (image + 1) * half, :].astype(jnp.float32)
                for side in range(2)
            ]
            * 3
            + [jnp.zeros((128 - 6 * half, cols), jnp.float32)],
            axis=0,
        ).T
        at = 8 + base
        if place == 0:
            keep = reach if image else 16
            at, block = at - keep, block[cols - keep :, :]
        elif place == 2:
            at, block = at + cols, block[:16, :]
        for step_x in range(3):
            begin = at + 1 - step_x
            some = slice(step_x * 2 * half, (step_x + 1) * 2 * half)
            ext[image, begin : begin + block.shape[0], some] = block[:, some]

    def build_right(k, begin, count):
        for delta in range(-2, 3):
            at = lead - D + delta + begin
            right_m[k, begin : begin + count, (delta + 2) * 128 : (delta + 3) * 128] = (
                rf[k, at : at + count, :].astype(jnp.bfloat16)
            )

    def build_left(k, chunks):
        for chunk in chunks:
            at = 7 + chunk * 16
            shifted = [lf[k, at + c : at + c + 16, :].reshape(2, 8, 128) for c in range(3)]
            for odd in range(2):
                for delta in range(-2, 3):
                    value = None
                    for c in range(3):
                        a = c - delta
                        if 0 <= a < 3:
                            term = shifted[c] * band_w[(a * 3 + c) * 2 + odd]
                            value = term if value is None else value + term
                    left_m[
                        k,
                        odd * cols + chunk * 16 : odd * cols + chunk * 16 + 16,
                        (delta + 2) * 128 : (delta + 3) * 128,
                    ] = value.reshape(16, 128).astype(jnp.bfloat16)

    def end_product(k, d, x, count):
        return lf[k, 8 + x : 8 + x + count, :] * rf[k, lead + x - d : lead + x - d + count, :]

    def build_ends(where, k):
        if k not in once:
            return
        columns = slice(once.index(k) * 128, (once.index(k) + 1) * 128)
        gap = jnp.zeros((8, 128), jnp.float32)
        for j, d in enumerate((0, 1, D - 2, D - 1)):
            reached = 16 if j < 2 else D + 16
            if where == 2:
                x, count = reached, cols - 16 - reached
            elif where == 0:
                x, count = 0, reached
                block = jnp.concatenate([gap, end_product(k, d, -8, 8)], axis=0)
                end_in[j, 0:16, columns] = block.astype(jnp.bfloat16)
            else:
                x, count = cols - 16, 16
                block = jnp.concatenate([end_product(k, d, cols, 8), gap], axis=0)
                end_in[j, 16 + cols :, columns] = block.astype(jnp.bfloat16)
            end_in[j, 16 + x : 16 + x + count, columns] = end_product(k, d, x, count).astype(jnp.bfloat16)

    chunks = cols // 16
    inner = len(inner_pairs) // 2
    strips = (((1, 0, lead + 8), (0, 0, 16)), ((1, span - 16, 16), (0, wide_l - 16, 16)))

    def own_columns(pairs_in, n, depth):
        for image in range(2):
            first = origin[image] + 8
            total = convolve(lhs[image, first : first + local, :depth], n, depth)
            for j, k in enumerate(pairs_in):
                put(image, k, first, finish(total, j, k, image))
        for k in pairs_in:
            build_right(k, D + 16, cols - 32)
            build_left(k, range(1, chunks - 1))
            build_ends(2, k)

    def other_columns(sides, pairs_in, n, depth):
        some = [strip for side in sides for strip in strips[side]]
        rows_in = jnp.concatenate(
            [lhs[image, first : first + count, :depth] for image, first, count in some], axis=0
        )
        total = convolve(rows_in, n, depth)
        for j, k in enumerate(pairs_in):
            at = 0
            for image, first, count in some:
                put(image, k, first, finish(total[at : at + count, :], j, k, image))
                at += count
        for k in pairs_in:
            if 0 in sides:
                build_right(k, 0, D + 16)
                build_left(k, [0])
            if 1 in sides:
                build_right(k, D + cols - 16, 16)
                build_left(k, [chunks - 1])
            for side in sides:
                build_ends(side, k)

    def columns_in(side):
        if side == 0:
            pt[1, base - reach : base, :] = near1[...].astype(jnp.float32)
            pt[0, base - 16 : base, :] = near0[...].astype(jnp.float32)
        else:
            pt[:, base + cols : base + cols + 16, :] = far[...].astype(jnp.float32)
        for image, first, count in strips[side]:
            gather(image, first, count)

    def corners_in(side):
        for image in range(2):
            place_lines(image, 2 * side)
        for image, first, count in strips[side]:
            gather_lines(image, first, count)

    def inner_columns(sides):
        for n in range(inner):
            other_columns(sides, inner_pairs[2 * n : 2 * n + 2], n, 3 * main)

    def outer_columns(sides):
        other_columns(sides, outer_pairs, inner, 3 * main + 128)

    low_lane = lax.broadcasted_iota(jnp.int32, (D, cols), 1) < D
    lane8 = lax.broadcasted_iota(jnp.int32, (8, cols), 1)
    from_x = (lane8 - lax.broadcasted_iota(jnp.int32, (8, cols), 0)).astype(jnp.float32)
    jump = jnp.where(lane8 < D, float(D), -float(D))

    def attend(k):
        score = lax.dot_general(right_m[k], left_m[k], nt, preferred_element_type=jnp.float32)
        for odd in range(2):
            mine = slice(odd * cols, (odd + 1) * cols)
            outer = jnp.where(low_lane, score[:D, mine], score[2 * D :, mine]) + mask[0]
            inner = score[D : 2 * D, mine] + mask[1]
            outer = outer.reshape(D // 8, 8, cols)
            inner = inner.reshape(D // 8, 8, cols)
            best = jnp.maximum(jnp.max(outer, axis=0), jnp.max(inner, axis=0))
            outer = jnp.exp2(outer - best)
            both = outer + jnp.exp2(inner - best)
            tail, steps = both[D // 8 - 1], None
            for j in range(D // 8 - 2, -1, -1):
                steps = tail if steps is None else steps + tail
                tail = tail + both[j]
            moment = from_x * tail - 8.0 * steps + jump * jnp.sum(outer, axis=0)
            y = 2 * k + odd
            for j, value in enumerate((best, tail, moment)):
                part[j, y * 8 : (y + 1) * 8, :] = value

    strip_rows = D + 16
    lane_s = lax.broadcasted_iota(jnp.int32, (strip_rows, 32), 1) % 16
    apart_s = lane_s + D - lax.broadcasted_iota(jnp.int32, (strip_rows, 32), 0)
    within_s = (apart_s >= 1) & (apart_s <= D - 2)
    from_s = apart_s[:8].astype(jnp.float32)

    def attend_strip(k):
        columns = jnp.concatenate([left_m[k, cols - 16 : cols, :], left_m[k, 2 * cols - 16 :, :]], axis=0)
        score = lax.dot_general(
            right_m[k, D + cols - strip_rows :, :], columns, nt, preferred_element_type=jnp.float32
        )
        score = jnp.where(within_s, score, -jnp.inf).reshape(strip_rows // 8, 8, 32)
        best = jnp.max(score, axis=0)
        weight = jnp.exp2(score - best)
        tail, steps = weight[strip_rows // 8 - 1], None
        for j in range(strip_rows // 8 - 2, -1, -1):
            steps = tail if steps is None else steps + tail
            tail = tail + weight[j]
        moment = from_s * tail - 8.0 * steps
        for j, value in enumerate((best, tail, moment)):
            at = (j * pairs + k) * 8
            strip_out[at : at + 8, :32] = value
            value = strip_out[at : at + 8, :]
            part[j, 16 * k : 16 * k + 8, cols - 16 :] = pltpu.roll(value, cols - 16, 1)[:, cols - 16 :]
            part[j, 16 * k + 8 : 16 * k + 16, cols - 16 :] = pltpu.roll(value, cols - 32, 1)[:, cols - 16 :]

    def send_later(order):
        for step in order:
            n = later.index(step)

            @pl.when(exists(step))
            def _(n=n):
                pl.semaphore_wait(ready.at[(0, 2, 1)[n]], 1)

            send(lambda other: other == step)

    def send_rest():
        @pl.when(even_row)
        def _():
            send_later(later[1:] + later[:1])

        @pl.when(odd_row)
        def _():
            @pl.when(tall > 1)
            def _():
                pl.semaphore_wait(ready.at[3], tall - 1)

            send_later(later[:1])
            send(lambda step: step in beside)
            send_later(later[1:])

    root = (my_col == 0) & (my_row < 2) & (lax.axis_index("pairs") == 0)

    @pl.when(my_col > 0)
    def _():
        send_rest()

    for image in range(2):
        gather(image, origin[image] + 8, local)
    for n in range(inner):
        own_columns(inner_pairs[2 * n : 2 * n + 2], n, 3 * main)

    @pl.when((my_col == 0) & jnp.logical_not(root))
    def _():
        send_rest()

    @pl.when(my_col == 0)
    def _():
        columns_in(0)
        inner_columns([0])
        for k in inner_pairs:
            attend(k)

    @pl.when(root)
    def _():
        send_rest()

    behind = line - lax.broadcasted_iota(jnp.int32, tile, 0)
    for t, k in enumerate(once):
        hit = [behind == step_y - 2 * k for step_y in range(3)]
        if k == 0:
            hit = [h & (line < 2) for h in hit]
        taps = []
        for step_d in range(3):
            pieces = []
            for step_x in range(3):
                value = jnp.zeros(tile, jnp.float32)
                for step_y in range(3):
                    at = 9 * step_d + 3 * step_y + step_x
                    value = jnp.where(hit[step_y], agg[at : at + 1, :], value)
                pieces.append(value)
            taps.append(pieces)
        gap = [jnp.zeros(tile, jnp.float32)] * (4 - 3)
        none = [jnp.zeros((64, 128), jnp.float32)]
        for j, (step_d, high) in enumerate(((1, 0), (2, 0), (0, 1), (1, 1))):
            some = taps[step_d] + gap
            value = jnp.concatenate(none + some if high else some + none, axis=0)
            end_w[j, t * 128 : (t + 1) * 128, :] = value.T.astype(jnp.bfloat16)

    receive(lambda step: step[1] == 0)
    for image in range(2):
        place_lines(image, 1)
        gather_lines(image, origin[image] + 8, local)
    own_columns(outer_pairs, inner, 3 * main + 128)

    @pl.when(my_col == 0)
    def _():
        corners_in(0)
        outer_columns([0])
        for k in outer_pairs:
            attend(k)

    def sum_ends():
        total = None
        for j in range(4):
            term = jnp.dot(end_in[j], end_w[j], preferred_element_type=jnp.float32)
            total = term if total is None else total + term
        end_sum[...] = total
        place = lax.broadcasted_iota(jnp.int32, (cols, 128), 1) % 64 // 16
        total = end_sum[15 : 15 + cols, :]
        for step_x in (1, 2):
            total = jnp.where(place == step_x, end_sum[15 + step_x : 15 + step_x + cols, :], total)
        total = total.T
        for n, j in enumerate((0, 64)):
            ends[n] = total[j : j + 16, :] + total[j + 16 : j + 32, :] + total[j + 32 : j + 48, :]

    receive(lambda step: step[1] != 0)

    @pl.when(my_col == 0)
    def _():
        columns_in(1)
        corners_in(1)
        inner_columns([1])
        outer_columns([1])
        sum_ends()
        for k in range(pairs):
            attend_strip(k)

    @pl.when(my_col > 0)
    def _():
        for side in range(2):
            columns_in(side)
            corners_in(side)
        inner_columns([0, 1])
        outer_columns([0, 1])
        sum_ends()
        for k in range(pairs):
            attend(k)

    for h in range(rows // 8):
        first = ends[0, h * 8 : (h + 1) * 8, :]
        last = ends[1, h * 8 : (h + 1) * 8, :]
        tops = [part[0, pl.ds(h * 64 + j, 8, stride=8), :] for j in range(8)]
        best = jnp.maximum(first, last)
        for top in tops:
            best = jnp.maximum(best, top)
        last = jnp.exp2(last - best)
        total = jnp.exp2(first - best) + last
        moment = last * float(D - 1)
        for j in range(8):
            weight = jnp.exp2(tops[j] - best)
            total = total + weight * part[1, pl.ds(h * 64 + j, 8, stride=8), :]
            moment = moment + weight * part[2, pl.ds(h * 64 + j, 8, stride=8), :]
        out_ref[h * 8 : (h + 1) * 8, :] = moment / total / D

    for step, copy in copies:

        @pl.when(exists(step))
        def _(copy=copy):
            copy.wait_send()


def on_device(images, conv_weight, conv_bias, agg_weight):
    cin, rows, cols = images.shape[1:]
    groups = agg_weight.shape[0]
    per = conv_weight.shape[0] // groups
    main = rows * cin
    pairs = rows // 2
    span = cols + D + 16
    reach = -(-(D + 2) // 16) * 16
    return pl.pallas_call(
        functools.partial(body, (rows, cols, groups, per, cin)),
        out_shape=pltpu.VMEM((rows, cols), jnp.float32),
        in_specs=[pl.BlockSpec(memory_space=pl.ANY)] * 4,
        out_specs=pl.BlockSpec(memory_space=pltpu.VMEM),
        scratch_shapes=[
            pltpu.VMEM(images.shape, images.dtype),
            pltpu.VMEM(conv_weight.shape, conv_weight.dtype),
            pltpu.VMEM((1,) + conv_bias.shape, conv_bias.dtype),
            pltpu.VMEM(agg_weight.shape, agg_weight.dtype),
            pltpu.SemaphoreType.DMA((7,)),
            pltpu.VMEM((2, span + 16, main), jnp.float32),
            pltpu.VMEM((2, span + 32, 128), jnp.float32),
            pltpu.VMEM((2, span, 3 * main + 128), jnp.bfloat16),
            pltpu.VMEM((3 * main + 128, pairs * 128), jnp.bfloat16),
            pltpu.VMEM((4, (pairs // 2 + 1) * 128, 128), jnp.bfloat16),
            pltpu.VMEM((4, cols + 32, (pairs // 2 + 1) * 128), jnp.bfloat16),
            pltpu.VMEM((cols + 32, 128), jnp.float32),
            pltpu.VMEM((2, rows, cols), jnp.float32),
            pltpu.VMEM((9 * cin, 128), jnp.float32),
            pltpu.VMEM((18, 8, 128), jnp.float32),
            pltpu.VMEM((2, D, cols), jnp.float32),
            pltpu.VMEM((pairs, cols + 16, 128), jnp.float32),
            pltpu.VMEM((pairs, span, 128), jnp.float32),
            pltpu.VMEM((pairs, 2 * cols, 640), jnp.bfloat16),
            pltpu.VMEM((pairs, D + cols, 640), jnp.bfloat16),
            pltpu.VMEM((3, rows * 8, cols), jnp.float32),
            pltpu.VMEM((3 * pairs * 8, 128), jnp.float32),
            pltpu.VMEM((2, cols, main), jnp.bfloat16),
            pltpu.VMEM((2, 4 * cin, cols), jnp.bfloat16),
            pltpu.VMEM((16, main), jnp.bfloat16),
            pltpu.VMEM((reach, main), jnp.bfloat16),
            pltpu.VMEM((2, 16, main), jnp.bfloat16),
            pltpu.VMEM((2, 3, 4 * cin, cols), jnp.bfloat16),
            pltpu.SemaphoreType.DMA((9,)),
            pltpu.SemaphoreType.DMA((9,)),
            pltpu.SemaphoreType.REGULAR((4,)),
        ],
        compiler_params=pltpu.CompilerParams(collective_id=0, has_side_effects=True),
    )(images, conv_weight, conv_bias[None], agg_weight)


def solution(mesh):
    in_specs = (P("pairs", None, "row", "col"), P(), P(), P())
    out_specs = P(("pairs", "row"), "col")
    return jax.shard_map(
        on_device, mesh=mesh, in_specs=in_specs, out_specs=out_specs, check_vma=False
    )
```

```python
import functools

import jax
import jax.numpy as jnp
from jax import lax
from jax.experimental import pallas as pl
from jax.experimental.pallas import tpu as pltpu
from jax.sharding import PartitionSpec as P

D = 64
LOG2E = 1.4426950408889634


MESH = pl.DeviceIdType.MESH
STEPS = ((0, 1), (0, -1), (1, 0), (-1, 0), (1, 1), (1, -1), (-1, 1), (-1, -1))


def body(
    shape, images_hbm, weight_hbm, bias_hbm, agg_hbm, out_ref,
    images_ref, weight_ref, bias_in, agg_in, load_sem,
    pt, ext, lhs, wc, end_w, end_in, end_sum, ends, taps_ref, band_w, mask, lf, rf, left_m, right_m, part, strip_out,
    tr_ref, edge_ref, near0, near1, far, lines, send_sem, recv_sem, ready,
):
    rows, cols, groups, per, cin = shape
    feats = groups * per
    pairs = rows // 2
    lead = D + 8
    span = rf.shape[1]
    wide_l = lf.shape[1]
    rows_axis, cols_axis = lax.axis_size("row"), lax.axis_size("col")
    my_row, my_col = lax.axis_index("row"), lax.axis_index("col")
    reach = near1.shape[0]

    def exists(step):
        r, c = my_row + step[0], my_col + step[1]
        return (r >= 0) & (r < rows_axis) & (c >= 0) & (c < cols_axis)

    def device(step):
        return {"row": my_row + step[0], "col": my_col + step[1]}

    odd_row = lax.rem(my_row, 2) == 1
    even_row = jnp.logical_not(odd_row)
    beside, later, earlier = ((1, 0), (-1, 0)), ((0, 1), (1, 1), (-1, 1)), ((0, -1), (1, -1), (-1, -1))

    barrier = pltpu.get_barrier_semaphore()
    for step in later + beside:
        allowed = exists(step) if step in later else exists(step) & odd_row

        @pl.when(allowed)
        def _(step=step):
            pl.semaphore_signal(barrier, inc=1, device_id=device(step), device_id_type=MESH)

    quarter = cin // 2
    loads = [
        pltpu.make_async_copy(
            images_hbm.at[image, pl.ds(part_at, quarter)],
            images_ref.at[image, pl.ds(part_at, quarter)],
            load_sem.at[2 * image + part_at // quarter],
        )
        for image in range(2)
        for part_at in (0, quarter)
    ]
    small_loads = [
        pltpu.make_async_copy(source, target, load_sem.at[4 + k])
        for k, (source, target) in enumerate(
            ((weight_hbm, weight_ref), (bias_hbm, bias_in), (agg_hbm, agg_in))
        )
    ]
    for load in loads + small_loads:
        load.start()
    tall = 1 + (my_row > 0).astype(jnp.int32) + (my_row < rows_axis - 1).astype(jnp.int32)
    greeted = jnp.where(my_col > 0, tall, 0) + jnp.where(even_row, tall - 1, 0)

    @pl.when(greeted > 0)
    def _():
        pl.semaphore_wait(barrier, greeted)

    for n, step in enumerate(earlier):

        @pl.when(exists(step))
        def _(n=n, step=step):
            pl.semaphore_signal(ready.at[n], inc=1, device_id=device(step), device_id_type=MESH)

    for step in beside:

        @pl.when(exists(step) & even_row)
        def _(step=step):
            pl.semaphore_signal(ready.at[3], inc=1, device_id=device(step), device_id_type=MESH)

    for load in loads:
        load.wait()

    main = rows * cin
    for image in range(2):
        for side, first in ((0, 0), (1, rows - 2)):
            pair = [images_ref[image, :, first + y, :] for y in range(2)]
            edge_ref[side, image * 2 * cin : (image + 1) * 2 * cin, :] = jnp.concatenate(
                pair, axis=0
            ).astype(jnp.bfloat16)

    plan = [
        ((0, 1), tr_ref.at[1, pl.ds(cols - reach, reach), :], near1),
        ((0, 1), tr_ref.at[0, pl.ds(cols - 16, 16), :], near0),
        ((0, -1), tr_ref.at[:, pl.ds(0, 16), :], far),
    ]
    for r in (1, -1):
        side = 0 if r == 1 else 1
        for c in (0, 1, -1):
            plan.append(((r, c), edge_ref.at[1 - side], lines.at[side, 1 - c]))
    copies = []
    for k, (step, source, target) in enumerate(plan):
        copy = pltpu.make_async_remote_copy(
            src_ref=source,
            dst_ref=target,
            send_sem=send_sem.at[k],
            recv_sem=recv_sem.at[k],
            device_id=device(step),
            device_id_type=MESH,
        )
        copies.append((step, copy))

    def send(chosen):
        for step, copy in copies:
            if chosen(step):

                @pl.when(exists(step))
                def _(copy=copy):
                    copy.start()

    def receive(chosen):
        for step, copy in copies:
            if chosen(step):

                @pl.when(exists((-step[0], -step[1])))
                def _(copy=copy):
                    copy.wait_recv()

    send(lambda step: step in earlier[1:])
    for image in range(2):
        tr_ref[image] = images_ref[image].reshape(main, cols).T.astype(jnp.bfloat16)
    send(lambda step: step == earlier[0])

    @pl.when(even_row)
    def _():
        send(lambda step: step in beside)

    for k, (step, source, target) in enumerate(plan):

        @pl.when(jnp.logical_not(exists((-step[0], -step[1]))))
        def _(target=target):
            target[...] = jnp.zeros(target.shape, target.dtype)

    for load in small_loads:
        load.wait()


    tn = (((0,), (0,)), ((), ()))
    nt = (((1,), (1,)), ((), ()))
    tile = (rows, 128)
    lane = lax.broadcasted_iota(jnp.int32, tile, 1)
    line = lane // feats
    spread = (
        lax.broadcasted_iota(jnp.int32, (feats, 128), 1) % feats
        == lax.broadcasted_iota(jnp.int32, (feats, 128), 0)
    ).astype(jnp.float32)
    one = (
        lax.broadcasted_iota(jnp.int32, (groups, 128), 1) % feats // per
        == lax.broadcasted_iota(jnp.int32, (groups, 128), 0)
    ).astype(jnp.float32)
    exact = dict(precision=lax.Precision.HIGHEST, preferred_element_type=jnp.float32)
    bias = jnp.dot(bias_in[...], spread, **exact)
    taps_ref[...] = lax.dot_general(
        weight_ref[...].astype(jnp.float32), spread, tn, preferred_element_type=jnp.float32
    )
    agg = lax.dot_general(agg_in[...], one, tn, **exact) * (LOG2E / per)

    above = lax.broadcasted_iota(jnp.int32, tile, 0) - line + 2
    near_line = line[:cin]
    inner_pairs, outer_pairs = list(range(1, pairs - 1)), [0, pairs - 1]
    for n, k in enumerate(inner_pairs + outer_pairs):
        columns = slice(n * 128, (n + 1) * 128)
        hit = [above == step_y + 2 * k for step_y in range(3)]
        for step_x in range(3):
            for c in range(cin):
                value = jnp.zeros(tile, jnp.float32)
                for step_y in range(3):
                    at = (step_y * 3 + step_x) * cin + c
                    value = jnp.where(hit[step_y], taps_ref[at : at + 1, :], value)
                begin = step_x * main + c * rows
                wc[begin : begin + rows, columns] = value.astype(jnp.bfloat16)
        if k in outer_pairs:
            for step_x in range(3):
                for side in range(2):
                    halves = []
                    for y in range(2):
                        row = y - 2 if side == 0 else rows + y
                        value = jnp.zeros((cin, 128), jnp.float32)
                        for step_y in range(3):
                            at = (step_y * 3 + step_x) * cin
                            value = jnp.where(
                                near_line == row - 2 * k + 2 - step_y, taps_ref[at : at + cin, :], value
                            )
                        halves.append(value)
                    begin = 3 * main + (step_x * 2 + side) * 2 * cin
                    wc[begin : begin + 2 * cin, columns] = (
                        jnp.concatenate(halves, axis=0).astype(jnp.bfloat16)
                    )
            begin = 3 * main + 12 * cin
            wc[begin:, columns] = jnp.zeros((wc.shape[0] - begin, 128), jnp.bfloat16)

    for step_d in range(3):
        for step_x in range(3):
            for odd in range(2):
                value = jnp.zeros((8, 128), jnp.float32)
                for step_y in range(3):
                    at = 9 * step_d + 3 * step_y + step_x
                    value = jnp.where(line[:8] == step_y + odd, agg[at : at + 1, :], value)
                band_w[(step_d * 3 + step_x) * 2 + odd] = value

    once = inner_pairs[::2] + outer_pairs
    at_x = lax.broadcasted_iota(jnp.int32, (D, cols), 1)
    at_i = lax.broadcasted_iota(jnp.int32, (D, cols), 0)
    low = at_x < D
    for j, apart in enumerate((jnp.where(low, at_x - at_i + D, at_x - at_i - D), at_x - at_i)):
        mask[j] = jnp.where((apart >= 1) & (apart <= D - 2), 0.0, -jnp.inf)

    base = 16 + D
    pt[:, base : base + cols, :] = tr_ref[...].astype(jnp.float32)
    ext[:, :, 12 * cin :] = jnp.zeros((2, span + 32, 128 - 12 * cin), jnp.float32)

    @pl.when(my_col == 0)
    def _():
        right_m[:, D + cols - 16 :, :] = jnp.zeros((pairs, 16, 640), jnp.bfloat16)

    left_ok = (my_col > 0).astype(jnp.float32)
    right_ok = (my_col < cols_axis - 1).astype(jnp.float32)
    top_ok = (my_row > 0) | (line[:1] > 0)
    end_ok = (my_row < rows_axis - 1) | (line[:1] < 3)
    base = 16 + D
    counts = (wide_l, span)
    origin = (8, lead)
    local = cols - 16

    def gather(image, first, count):
        begin = 8 + origin[1] - origin[image] + first
        for step_x in range(3):
            at = begin + step_x - 1
            lhs[image, first : first + count, step_x * main : (step_x + 1) * main] = (
                pt[image, at : at + count, :].astype(jnp.bfloat16)
            )

    def gather_lines(image, first, count):
        at = 16 + origin[1] - origin[image] + first
        lhs[image, first : first + count, 3 * main :] = ext[image, at : at + count, :].astype(jnp.bfloat16)

    def finish(total, j, k, image):
        value = total[:, j * 128 : (j + 1) * 128] + bias
        value = jnp.maximum(value, value * 0.1)
        value = value.astype(jnp.bfloat16).astype(jnp.float32)
        if image == 0 and k == 0:
            value = jnp.where(top_ok, value, 0.0)
        if image == 0 and k == pairs - 1:
            value = jnp.where(end_ok, value, 0.0)
        return value

    def convolve(rows_in, n, depth):
        return jnp.dot(
            rows_in, wc[:depth, n * 256 : (n + 1) * 256], preferred_element_type=jnp.float32
        )

    def put(image, k, begin, value):
        store = (lf, rf)[image]
        edge = origin[image]
        end = begin + value.shape[0]
        if begin < edge:
            store[k, begin:edge, :] = value[: edge - begin, :] * left_ok
            value, begin = value[edge - begin :, :], edge
        if image == 0 and end > 8 + cols:
            store[k, 8 + cols : end, :] = value[8 + cols - begin :, :] * right_ok
            value = value[: 8 + cols - begin, :]
        store[k, begin : begin + value.shape[0], :] = value

    def place_lines(image, place):
        half = 2 * cin
        block = jnp.concatenate(
            [
                lines[side, place, image * half : (image + 1) * half, :].astype(jnp.float32)
                for side in range(2)
            ]
            * 3
            + [jnp.zeros((128 - 6 * half, cols), jnp.float32)],
            axis=0,
        ).T
        at = 8 + base
        if place == 0:
            keep = reach if image else 16
            at, block = at - keep, block[cols - keep :, :]
        elif place == 2:
            at, block = at + cols, block[:16, :]
        for step_x in range(3):
            begin = at + 1 - step_x
            some = slice(step_x * 2 * half, (step_x + 1) * 2 * half)
            ext[image, begin : begin + block.shape[0], some] = block[:, some]

    def build_right(k, begin, count):
        for delta in range(-2, 3):
            at = lead - D + delta + begin
            right_m[k, begin : begin + count, (delta + 2) * 128 : (delta + 3) * 128] = (
                rf[k, at : at + count, :].astype(jnp.bfloat16)
            )

    def build_left(k, chunks):
        for chunk in chunks:
            at = 7 + chunk * 16
            shifted = [lf[k, at + c : at + c + 16, :].reshape(2, 8, 128) for c in range(3)]
            for odd in range(2):
                for delta in range(-2, 3):
                    value = None
                    for c in range(3):
                        a = c - delta
                        if 0 <= a < 3:
                            term = shifted[c] * band_w[(a * 3 + c) * 2 + odd]
                            value = term if value is None else value + term
                    left_m[
                        k,
                        odd * cols + chunk * 16 : odd * cols + chunk * 16 + 16,
                        (delta + 2) * 128 : (delta + 3) * 128,
                    ] = value.reshape(16, 128).astype(jnp.bfloat16)

    def end_product(k, d, x, count):
        return lf[k, 8 + x : 8 + x + count, :] * rf[k, lead + x - d : lead + x - d + count, :]

    def build_ends(where, k):
        if k not in once:
            return
        columns = slice(once.index(k) * 128, (once.index(k) + 1) * 128)
        gap = jnp.zeros((8, 128), jnp.float32)
        for j, d in enumerate((0, 1, D - 2, D - 1)):
            reached = 16 if j < 2 else D + 16
            if where == 2:
                x, count = reached, cols - 16 - reached
            elif where == 0:
                x, count = 0, reached
                block = jnp.concatenate([gap, end_product(k, d, -8, 8)], axis=0)
                end_in[j, 0:16, columns] = block.astype(jnp.bfloat16)
            else:
                x, count = cols - 16, 16
                block = jnp.concatenate([end_product(k, d, cols, 8), gap], axis=0)
                end_in[j, 16 + cols :, columns] = block.astype(jnp.bfloat16)
            end_in[j, 16 + x : 16 + x + count, columns] = end_product(k, d, x, count).astype(jnp.bfloat16)

    chunks = cols // 16
    inner = len(inner_pairs) // 2
    strips = (((1, 0, lead + 8), (0, 0, 16)), ((1, span - 16, 16), (0, wide_l - 16, 16)))

    def own_columns(pairs_in, n, depth):
        for image in range(2):
            first = origin[image] + 8
            total = convolve(lhs[image, first : first + local, :depth], n, depth)
            for j, k in enumerate(pairs_in):
                put(image, k, first, finish(total, j, k, image))
        for k in pairs_in:
            build_right(k, D + 16, cols - 32)
            build_left(k, range(1, chunks - 1))
            build_ends(2, k)

    def other_columns(sides, pairs_in, n, depth):
        some = [strip for side in sides for strip in strips[side]]
        rows_in = jnp.concatenate(
            [lhs[image, first : first + count, :depth] for image, first, count in some], axis=0
        )
        total = convolve(rows_in, n, depth)
        for j, k in enumerate(pairs_in):
            at = 0
            for image, first, count in some:
                put(image, k, first, finish(total[at : at + count, :], j, k, image))
                at += count
        for k in pairs_in:
            if 0 in sides:
                build_right(k, 0, D + 16)
                build_left(k, [0])
            if 1 in sides:
                build_right(k, D + cols - 16, 16)
                build_left(k, [chunks - 1])
            for side in sides:
                build_ends(side, k)

    def columns_in(side):
        if side == 0:
            pt[1, base - reach : base, :] = near1[...].astype(jnp.float32)
            pt[0, base - 16 : base, :] = near0[...].astype(jnp.float32)
        else:
            pt[:, base + cols : base + cols + 16, :] = far[...].astype(jnp.float32)
        for image, first, count in strips[side]:
            gather(image, first, count)

    def corners_in(side):
        for image in range(2):
            place_lines(image, 2 * side)
        for image, first, count in strips[side]:
            gather_lines(image, first, count)

    def inner_columns(sides):
        for n in range(inner):
            other_columns(sides, inner_pairs[2 * n : 2 * n + 2], n, 3 * main)

    def outer_columns(sides):
        other_columns(sides, outer_pairs, inner, 3 * main + 128)

    low_lane = lax.broadcasted_iota(jnp.int32, (D, cols), 1) < D
    lane8 = lax.broadcasted_iota(jnp.int32, (8, cols), 1)
    from_x = (lane8 - lax.broadcasted_iota(jnp.int32, (8, cols), 0)).astype(jnp.float32)
    jump = jnp.where(lane8 < D, float(D), -float(D))

    def attend(k):
        score = lax.dot_general(right_m[k], left_m[k], nt, preferred_element_type=jnp.float32)
        for odd in range(2):
            mine = slice(odd * cols, (odd + 1) * cols)
            outer = jnp.where(low_lane, score[:D, mine], score[2 * D :, mine]) + mask[0]
            inner = score[D : 2 * D, mine] + mask[1]
            outer = outer.reshape(D // 8, 8, cols)
            inner = inner.reshape(D // 8, 8, cols)
            best = jnp.maximum(jnp.max(outer, axis=0), jnp.max(inner, axis=0))
            outer = jnp.exp2(outer - best)
            both = outer + jnp.exp2(inner - best)
            tail, steps = both[D // 8 - 1], None
            for j in range(D // 8 - 2, -1, -1):
                steps = tail if steps is None else steps + tail
                tail = tail + both[j]
            moment = from_x * tail - 8.0 * steps + jump * jnp.sum(outer, axis=0)
            y = 2 * k + odd
            for j, value in enumerate((best, tail, moment)):
                part[j, y * 8 : (y + 1) * 8, :] = value

    strip_rows = D + 16
    lane_s = lax.broadcasted_iota(jnp.int32, (strip_rows, 32), 1) % 16
    apart_s = lane_s + D - lax.broadcasted_iota(jnp.int32, (strip_rows, 32), 0)
    within_s = (apart_s >= 1) & (apart_s <= D - 2)
    from_s = apart_s[:8].astype(jnp.float32)

    def attend_strip(k):
        columns = jnp.concatenate([left_m[k, cols - 16 : cols, :], left_m[k, 2 * cols - 16 :, :]], axis=0)
        score = lax.dot_general(
            right_m[k, D + cols - strip_rows :, :], columns, nt, preferred_element_type=jnp.float32
        )
        score = jnp.where(within_s, score, -jnp.inf).reshape(strip_rows // 8, 8, 32)
        best = jnp.max(score, axis=0)
        weight = jnp.exp2(score - best)
        tail, steps = weight[strip_rows // 8 - 1], None
        for j in range(strip_rows // 8 - 2, -1, -1):
            steps = tail if steps is None else steps + tail
            tail = tail + weight[j]
        moment = from_s * tail - 8.0 * steps
        for j, value in enumerate((best, tail, moment)):
            at = (j * pairs + k) * 8
            strip_out[at : at + 8, :32] = value
            value = strip_out[at : at + 8, :]
            part[j, 16 * k : 16 * k + 8, cols - 16 :] = pltpu.roll(value, cols - 16, 1)[:, cols - 16 :]
            part[j, 16 * k + 8 : 16 * k + 16, cols - 16 :] = pltpu.roll(value, cols - 32, 1)[:, cols - 16 :]

    def send_later(order):
        for step in order:
            n = later.index(step)

            @pl.when(exists(step))
            def _(n=n):
                pl.semaphore_wait(ready.at[(0, 2, 1)[n]], 1)

            send(lambda other: other == step)

    def send_beside():
        @pl.when(odd_row & (tall > 1))
        def _():
            pl.semaphore_wait(ready.at[3], tall - 1)

        @pl.when(odd_row)
        def _():
            send(lambda step: step in beside)

    def send_all_later():
        @pl.when(even_row)
        def _():
            send_later(later[1:] + later[:1])

        @pl.when(odd_row)
        def _():
            send_later(later)

    def send_rest():
        send_beside()
        send_all_later()

    root = (my_col == 0) & (my_row < 2) & (lax.axis_index("pairs") == 0)

    @pl.when(my_col > 0)
    def _():
        send_rest()

    for image in range(2):
        gather(image, origin[image] + 8, local)
    for n in range(inner):
        own_columns(inner_pairs[2 * n : 2 * n + 2], n, 3 * main)

    @pl.when((my_col == 0) & jnp.logical_not(root))
    def _():
        send_rest()

    @pl.when(my_col == 0)
    def _():
        columns_in(0)
        inner_columns([0])
        for k in inner_pairs:
            attend(k)

    @pl.when(root)
    def _():
        send_beside()

    half_lane = lax.broadcasted_iota(jnp.int32, (128, 128), 1) < 64
    behind = line - lax.broadcasted_iota(jnp.int32, tile, 0)
    for t, k in enumerate(once):
        hit = [behind == step_y - 2 * k for step_y in range(3)]
        if k == 0:
            hit = [h & (line < 2) for h in hit]
        taps = []
        for step_d in range(3):
            pieces = []
            for step_x in range(3):
                value = jnp.zeros(tile, jnp.float32)
                for step_y in range(3):
                    at = 9 * step_d + 3 * step_y + step_x
                    value = jnp.where(hit[step_y], agg[at : at + 1, :], value)
                pieces.append(value)
            taps.append(pieces)
        gap = [jnp.zeros(tile, jnp.float32)]
        for j, (low_d, high_d) in enumerate(((1, 1), (2, 0))):
            value = jnp.concatenate(taps[low_d] + gap + taps[high_d] + gap, axis=0).T
            for n, keep in ((j, half_lane), (3 - j, jnp.logical_not(half_lane))):
                end_w[n, t * 128 : (t + 1) * 128, :] = jnp.where(keep, value, 0.0).astype(jnp.bfloat16)

    @pl.when(root)
    def _():
        send_all_later()

    tiles = len(once) - len(outer_pairs)

    def sum_ends(columns, where=slice(None)):
        total = None
        for j in range(4):
            term = jnp.dot(
                end_in[j, where, columns], end_w[j, columns, :], preferred_element_type=jnp.float32
            )
            total = term if total is None else total + term
        return total

    def sum_inner_ends():
        end_sum[...] = sum_ends(slice(0, tiles * 128))

    def sum_outer_ends():
        end_sum[...] += sum_ends(slice(tiles * 128, len(once) * 128))
        spread_ends()

    def spread_ends():
        place = lax.broadcasted_iota(jnp.int32, (cols, 128), 1) % 64 // 16
        total = end_sum[15 : 15 + cols, :]
        for step_x in (1, 2):
            total = jnp.where(place == step_x, end_sum[15 + step_x : 15 + step_x + cols, :], total)
        total = total.T
        for n, j in enumerate((0, 64)):
            ends[n] = total[j : j + 16, :] + total[j + 16 : j + 32, :] + total[j + 32 : j + 48, :]

    @pl.when(my_col == 0)
    def _():
        sum_inner_ends()

    receive(lambda step: step[1] == 0)
    for image in range(2):
        place_lines(image, 1)
        gather_lines(image, origin[image] + 8, local)
    own_columns(outer_pairs, inner, 3 * main + 128)

    @pl.when(my_col == 0)
    def _():
        corners_in(0)

    def staged(sides, do):
        receive(lambda step: step[0] == 0)
        for side in sides:
            columns_in(side)
        inner_columns(sides)
        sum_inner_ends()
        for k in inner_pairs:
            do(k)
        receive(lambda step: step[0] != 0 and step[1] != 0)
        for side in sides:
            corners_in(side)
        outer_columns(sides)
        sum_outer_ends()
        for k in outer_pairs:
            do(k)

    @pl.when(my_col == 0)
    def _():
        receive(lambda step: step[1] != 0)
        columns_in(1)
        corners_in(1)
        inner_columns([1])
        outer_columns([0, 1])
        end_sum[cols:, :] = sum_ends(slice(0, tiles * 128), slice(cols, cols + 32))
        sum_outer_ends()
        for k in inner_pairs:
            attend_strip(k)
        for k in outer_pairs:
            attend(k)

    @pl.when((my_col > 0) & odd_row)
    def _():
        staged([0, 1], attend)

    @pl.when((my_col > 0) & even_row)
    def _():
        receive(lambda step: step[1] != 0)
        for side in range(2):
            columns_in(side)
            corners_in(side)
        inner_columns([0, 1])
        outer_columns([0, 1])
        sum_inner_ends()
        sum_outer_ends()
        for k in range(pairs):
            attend(k)

    for h in range(rows // 8):
        first = ends[0, h * 8 : (h + 1) * 8, :]
        last = ends[1, h * 8 : (h + 1) * 8, :]
        tops = [part[0, pl.ds(h * 64 + j, 8, stride=8), :] for j in range(8)]
        best = jnp.maximum(first, last)
        for top in tops:
            best = jnp.maximum(best, top)
        last = jnp.exp2(last - best)
        total = jnp.exp2(first - best) + last
        moment = last * float(D - 1)
        for j in range(8):
            weight = jnp.exp2(tops[j] - best)
            total = total + weight * part[1, pl.ds(h * 64 + j, 8, stride=8), :]
            moment = moment + weight * part[2, pl.ds(h * 64 + j, 8, stride=8), :]
        out_ref[h * 8 : (h + 1) * 8, :] = moment / total / D

    for step, copy in copies:

        @pl.when(exists(step))
        def _(copy=copy):
            copy.wait_send()


def on_device(images, conv_weight, conv_bias, agg_weight):
    cin, rows, cols = images.shape[1:]
    groups = agg_weight.shape[0]
    per = conv_weight.shape[0] // groups
    main = rows * cin
    pairs = rows // 2
    span = cols + D + 16
    reach = -(-(D + 2) // 16) * 16
    return pl.pallas_call(
        functools.partial(body, (rows, cols, groups, per, cin)),
        out_shape=pltpu.VMEM((rows, cols), jnp.float32),
        in_specs=[pl.BlockSpec(memory_space=pl.ANY)] * 4,
        out_specs=pl.BlockSpec(memory_space=pltpu.VMEM),
        scratch_shapes=[
            pltpu.VMEM(images.shape, images.dtype),
            pltpu.VMEM(conv_weight.shape, conv_weight.dtype),
            pltpu.VMEM((1,) + conv_bias.shape, conv_bias.dtype),
            pltpu.VMEM(agg_weight.shape, agg_weight.dtype),
            pltpu.SemaphoreType.DMA((7,)),
            pltpu.VMEM((2, span + 16, main), jnp.float32),
            pltpu.VMEM((2, span + 32, 128), jnp.float32),
            pltpu.VMEM((2, span, 3 * main + 128), jnp.bfloat16),
            pltpu.VMEM((3 * main + 128, pairs * 128), jnp.bfloat16),
            pltpu.VMEM((4, (pairs // 2 + 1) * 128, 128), jnp.bfloat16),
            pltpu.VMEM((4, cols + 32, (pairs // 2 + 1) * 128), jnp.bfloat16),
            pltpu.VMEM((cols + 32, 128), jnp.float32),
            pltpu.VMEM((2, rows, cols), jnp.float32),
            pltpu.VMEM((9 * cin, 128), jnp.float32),
            pltpu.VMEM((18, 8, 128), jnp.float32),
            pltpu.VMEM((2, D, cols), jnp.float32),
            pltpu.VMEM((pairs, cols + 16, 128), jnp.float32),
            pltpu.VMEM((pairs, span, 128), jnp.float32),
            pltpu.VMEM((pairs, 2 * cols, 640), jnp.bfloat16),
            pltpu.VMEM((pairs, D + cols, 640), jnp.bfloat16),
            pltpu.VMEM((3, rows * 8, cols), jnp.float32),
            pltpu.VMEM((3 * pairs * 8, 128), jnp.float32),
            pltpu.VMEM((2, cols, main), jnp.bfloat16),
            pltpu.VMEM((2, 4 * cin, cols), jnp.bfloat16),
            pltpu.VMEM((16, main), jnp.bfloat16),
            pltpu.VMEM((reach, main), jnp.bfloat16),
            pltpu.VMEM((2, 16, main), jnp.bfloat16),
            pltpu.VMEM((2, 3, 4 * cin, cols), jnp.bfloat16),
            pltpu.SemaphoreType.DMA((9,)),
            pltpu.SemaphoreType.DMA((9,)),
            pltpu.SemaphoreType.REGULAR((4,)),
        ],
        compiler_params=pltpu.CompilerParams(collective_id=0, has_side_effects=True),
    )(images, conv_weight, conv_bias[None], agg_weight)


def solution(mesh):
    in_specs = (P("pairs", None, "row", "col"), P(), P(), P())
    out_specs = P(("pairs", "row"), "col")
    return jax.shard_map(
        on_device, mesh=mesh, in_specs=in_specs, out_specs=out_specs, check_vma=False
    )
```

```python
import functools

import jax
import jax.numpy as jnp
from jax import lax
from jax.experimental import pallas as pl
from jax.experimental.pallas import tpu as pltpu
from jax.sharding import PartitionSpec as P

D = 64
LOG2E = 1.4426950408889634


MESH = pl.DeviceIdType.MESH
STEPS = ((0, 1), (0, -1), (1, 0), (-1, 0), (1, 1), (1, -1), (-1, 1), (-1, -1))


def body(
    shape, images_hbm, weight_hbm, bias_hbm, agg_hbm, out_ref,
    images_ref, weight_ref, bias_in, agg_in, load_sem,
    pt, ext, lhs, wc, end_w, end_in, end_sum, ends, taps_ref, band_w, mask, lf, rf, left_m, right_m, part, strip_out,
    tr_ref, edge_ref, near0, near1, far, lines, send_sem, recv_sem, ready,
):
    rows, cols, groups, per, cin = shape
    feats = groups * per
    pairs = rows // 2
    lead = D + 8
    span = rf.shape[1]
    wide_l = lf.shape[1]
    rows_axis, cols_axis = lax.axis_size("row"), lax.axis_size("col")
    my_row, my_col = lax.axis_index("row"), lax.axis_index("col")
    reach = near1.shape[0]

    def exists(step):
        r, c = my_row + step[0], my_col + step[1]
        return (r >= 0) & (r < rows_axis) & (c >= 0) & (c < cols_axis)

    def device(step):
        return {"row": my_row + step[0], "col": my_col + step[1]}

    odd_row = lax.rem(my_row, 2) == 1
    even_row = jnp.logical_not(odd_row)
    beside, later, earlier = ((1, 0), (-1, 0)), ((0, 1), (1, 1), (-1, 1)), ((0, -1), (1, -1), (-1, -1))

    barrier = pltpu.get_barrier_semaphore()
    for step in later + beside:
        allowed = exists(step) if step in later else exists(step) & odd_row

        @pl.when(allowed)
        def _(step=step):
            pl.semaphore_signal(barrier, inc=1, device_id=device(step), device_id_type=MESH)

    quarter = cin // 2
    loads = [
        pltpu.make_async_copy(
            images_hbm.at[image, pl.ds(part_at, quarter)],
            images_ref.at[image, pl.ds(part_at, quarter)],
            load_sem.at[2 * image + part_at // quarter],
        )
        for image in range(2)
        for part_at in (0, quarter)
    ]
    small_loads = [
        pltpu.make_async_copy(source, target, load_sem.at[4 + k])
        for k, (source, target) in enumerate(
            ((weight_hbm, weight_ref), (bias_hbm, bias_in), (agg_hbm, agg_in))
        )
    ]
    for load in loads + small_loads:
        load.start()
    tall = 1 + (my_row > 0).astype(jnp.int32) + (my_row < rows_axis - 1).astype(jnp.int32)
    greeted = jnp.where(my_col > 0, tall, 0) + jnp.where(even_row, tall - 1, 0)

    @pl.when(greeted > 0)
    def _():
        pl.semaphore_wait(barrier, greeted)

    for n, step in enumerate(earlier):

        @pl.when(exists(step))
        def _(n=n, step=step):
            pl.semaphore_signal(ready.at[n], inc=1, device_id=device(step), device_id_type=MESH)

    for step in beside:

        @pl.when(exists(step) & even_row)
        def _(step=step):
            pl.semaphore_signal(ready.at[3], inc=1, device_id=device(step), device_id_type=MESH)

    for load in loads:
        load.wait()

    main = rows * cin
    for image in range(2):
        for side, first in ((0, 0), (1, rows - 2)):
            pair = [images_ref[image, :, first + y, :] for y in range(2)]
            edge_ref[side, image * 2 * cin : (image + 1) * 2 * cin, :] = jnp.concatenate(
                pair, axis=0
            ).astype(jnp.bfloat16)

    plan = [
        ((0, 1), tr_ref.at[1, pl.ds(cols - reach, reach), :], near1),
        ((0, 1), tr_ref.at[0, pl.ds(cols - 16, 16), :], near0),
        ((0, -1), tr_ref.at[:, pl.ds(0, 16), :], far),
    ]
    for r in (1, -1):
        side = 0 if r == 1 else 1
        for c in (0, 1, -1):
            plan.append(((r, c), edge_ref.at[1 - side], lines.at[side, 1 - c]))
    copies = []
    for k, (step, source, target) in enumerate(plan):
        copy = pltpu.make_async_remote_copy(
            src_ref=source,
            dst_ref=target,
            send_sem=send_sem.at[k],
            recv_sem=recv_sem.at[k],
            device_id=device(step),
            device_id_type=MESH,
        )
        copies.append((step, copy))

    def send(chosen):
        for step, copy in copies:
            if chosen(step):

                @pl.when(exists(step))
                def _(copy=copy):
                    copy.start()

    def receive(chosen):
        for step, copy in copies:
            if chosen(step):

                @pl.when(exists((-step[0], -step[1])))
                def _(copy=copy):
                    copy.wait_recv()

    send(lambda step: step in earlier[1:])
    for image in range(2):
        tr_ref[image] = images_ref[image].reshape(main, cols).T.astype(jnp.bfloat16)
    send(lambda step: step == earlier[0])

    @pl.when(even_row)
    def _():
        send(lambda step: step in beside)

    for k, (step, source, target) in enumerate(plan):

        @pl.when(jnp.logical_not(exists((-step[0], -step[1]))))
        def _(target=target):
            target[...] = jnp.zeros(target.shape, target.dtype)

    for load in small_loads:
        load.wait()


    tn = (((0,), (0,)), ((), ()))
    nt = (((1,), (1,)), ((), ()))
    tile = (rows, 128)
    lane = lax.broadcasted_iota(jnp.int32, tile, 1)
    line = lane // feats
    spread = (
        lax.broadcasted_iota(jnp.int32, (feats, 128), 1) % feats
        == lax.broadcasted_iota(jnp.int32, (feats, 128), 0)
    ).astype(jnp.float32)
    one = (
        lax.broadcasted_iota(jnp.int32, (groups, 128), 1) % feats // per
        == lax.broadcasted_iota(jnp.int32, (groups, 128), 0)
    ).astype(jnp.float32)
    exact = dict(precision=lax.Precision.HIGHEST, preferred_element_type=jnp.float32)
    bias = jnp.dot(bias_in[...], spread, **exact)
    taps_ref[...] = lax.dot_general(
        weight_ref[...].astype(jnp.float32), spread, tn, preferred_element_type=jnp.float32
    )
    agg = lax.dot_general(agg_in[...], one, tn, **exact) * (LOG2E / per)

    above = lax.broadcasted_iota(jnp.int32, tile, 0) - line + 2
    near_line = line[:cin]
    inner_pairs, outer_pairs = list(range(1, pairs - 1)), [0, pairs - 1]
    for n, k in enumerate(inner_pairs + outer_pairs):
        columns = slice(n * 128, (n + 1) * 128)
        hit = [above == step_y + 2 * k for step_y in range(3)]
        for step_x in range(3):
            for c in range(cin):
                value = jnp.zeros(tile, jnp.float32)
                for step_y in range(3):
                    at = (step_y * 3 + step_x) * cin + c
                    value = jnp.where(hit[step_y], taps_ref[at : at + 1, :], value)
                begin = step_x * main + c * rows
                wc[begin : begin + rows, columns] = value.astype(jnp.bfloat16)
        if k in outer_pairs:
            for step_x in range(3):
                for side in range(2):
                    halves = []
                    for y in range(2):
                        row = y - 2 if side == 0 else rows + y
                        value = jnp.zeros((cin, 128), jnp.float32)
                        for step_y in range(3):
                            at = (step_y * 3 + step_x) * cin
                            value = jnp.where(
                                near_line == row - 2 * k + 2 - step_y, taps_ref[at : at + cin, :], value
                            )
                        halves.append(value)
                    begin = 3 * main + (step_x * 2 + side) * 2 * cin
                    wc[begin : begin + 2 * cin, columns] = (
                        jnp.concatenate(halves, axis=0).astype(jnp.bfloat16)
                    )
            begin = 3 * main + 12 * cin
            wc[begin:, columns] = jnp.zeros((wc.shape[0] - begin, 128), jnp.bfloat16)

    for step_d in range(3):
        for step_x in range(3):
            for odd in range(2):
                value = jnp.zeros((8, 128), jnp.float32)
                for step_y in range(3):
                    at = 9 * step_d + 3 * step_y + step_x
                    value = jnp.where(line[:8] == step_y + odd, agg[at : at + 1, :], value)
                band_w[(step_d * 3 + step_x) * 2 + odd] = value

    once = inner_pairs[::2] + outer_pairs
    at_x = lax.broadcasted_iota(jnp.int32, (D, cols), 1)
    at_i = lax.broadcasted_iota(jnp.int32, (D, cols), 0)
    low = at_x < D
    for j, apart in enumerate((jnp.where(low, at_x - at_i + D, at_x - at_i - D), at_x - at_i)):
        mask[j] = jnp.where((apart >= 1) & (apart <= D - 2), 0.0, -jnp.inf)

    base = 16 + D
    pt[:, base : base + cols, :] = tr_ref[...].astype(jnp.float32)
    ext[:, :, 12 * cin :] = jnp.zeros((2, span + 32, 128 - 12 * cin), jnp.float32)

    @pl.when(my_col == 0)
    def _():
        right_m[:, D + cols - 16 :, :] = jnp.zeros((pairs, 16, 640), jnp.bfloat16)

    left_ok = (my_col > 0).astype(jnp.float32)
    right_ok = (my_col < cols_axis - 1).astype(jnp.float32)
    top_ok = (my_row > 0) | (line[:1] > 0)
    end_ok = (my_row < rows_axis - 1) | (line[:1] < 3)
    base = 16 + D
    counts = (wide_l, span)
    origin = (8, lead)
    local = cols - 16

    def gather(image, first, count):
        begin = 8 + origin[1] - origin[image] + first
        for step_x in range(3):
            at = begin + step_x - 1
            lhs[image, first : first + count, step_x * main : (step_x + 1) * main] = (
                pt[image, at : at + count, :].astype(jnp.bfloat16)
            )

    def gather_lines(image, first, count):
        at = 16 + origin[1] - origin[image] + first
        lhs[image, first : first + count, 3 * main :] = ext[image, at : at + count, :].astype(jnp.bfloat16)

    def finish(total, j, k, image):
        value = total[:, j * 128 : (j + 1) * 128] + bias
        value = jnp.maximum(value, value * 0.1)
        value = value.astype(jnp.bfloat16).astype(jnp.float32)
        if image == 0 and k == 0:
            value = jnp.where(top_ok, value, 0.0)
        if image == 0 and k == pairs - 1:
            value = jnp.where(end_ok, value, 0.0)
        return value

    def convolve(rows_in, n, depth):
        return jnp.dot(
            rows_in, wc[:depth, n * 256 : (n + 1) * 256], preferred_element_type=jnp.float32
        )

    def put(image, k, begin, value):
        store = (lf, rf)[image]
        edge = origin[image]
        end = begin + value.shape[0]
        if begin < edge:
            store[k, begin:edge, :] = value[: edge - begin, :] * left_ok
            value, begin = value[edge - begin :, :], edge
        if image == 0 and end > 8 + cols:
            store[k, 8 + cols : end, :] = value[8 + cols - begin :, :] * right_ok
            value = value[: 8 + cols - begin, :]
        store[k, begin : begin + value.shape[0], :] = value

    def place_lines(image, place):
        half = 2 * cin
        block = jnp.concatenate(
            [
                lines[side, place, image * half : (image + 1) * half, :].astype(jnp.float32)
                for side in range(2)
            ]
            * 3
            + [jnp.zeros((128 - 6 * half, cols), jnp.float32)],
            axis=0,
        ).T
        at = 8 + base
        if place == 0:
            keep = reach if image else 16
            at, block = at - keep, block[cols - keep :, :]
        elif place == 2:
            at, block = at + cols, block[:16, :]
        for step_x in range(3):
            begin = at + 1 - step_x
            some = slice(step_x * 2 * half, (step_x + 1) * 2 * half)
            ext[image, begin : begin + block.shape[0], some] = block[:, some]

    def build_right(k, begin, count):
        for delta in range(-2, 3):
            at = lead - D + delta + begin
            right_m[k, begin : begin + count, (delta + 2) * 128 : (delta + 3) * 128] = (
                rf[k, at : at + count, :].astype(jnp.bfloat16)
            )

    def build_left(k, chunks):
        for chunk in chunks:
            at = 7 + chunk * 16
            shifted = [lf[k, at + c : at + c + 16, :].reshape(2, 8, 128) for c in range(3)]
            for odd in range(2):
                for delta in range(-2, 3):
                    value = None
                    for c in range(3):
                        a = c - delta
                        if 0 <= a < 3:
                            term = shifted[c] * band_w[(a * 3 + c) * 2 + odd]
                            value = term if value is None else value + term
                    left_m[
                        k,
                        odd * cols + chunk * 16 : odd * cols + chunk * 16 + 16,
                        (delta + 2) * 128 : (delta + 3) * 128,
                    ] = value.reshape(16, 128).astype(jnp.bfloat16)

    def end_product(k, d, x, count):
        return lf[k, 8 + x : 8 + x + count, :] * rf[k, lead + x - d : lead + x - d + count, :]

    def build_ends(where, k):
        if k not in once:
            return
        columns = slice(once.index(k) * 128, (once.index(k) + 1) * 128)
        gap = jnp.zeros((8, 128), jnp.float32)
        for j, d in enumerate((0, 1, D - 2, D - 1)):
            reached = 16 if j < 2 else D + 16
            if where == 2:
                x, count = reached, cols - 16 - reached
            elif where == 0:
                x, count = 0, reached
                block = jnp.concatenate([gap, end_product(k, d, -8, 8)], axis=0)
                end_in[j, 0:16, columns] = block.astype(jnp.bfloat16)
            else:
                x, count = cols - 16, 16
                block = jnp.concatenate([end_product(k, d, cols, 8), gap], axis=0)
                end_in[j, 16 + cols :, columns] = block.astype(jnp.bfloat16)
            end_in[j, 16 + x : 16 + x + count, columns] = end_product(k, d, x, count).astype(jnp.bfloat16)

    chunks = cols // 16
    inner = len(inner_pairs) // 2
    strips = (((1, 0, lead + 8), (0, 0, 16)), ((1, span - 16, 16), (0, wide_l - 16, 16)))

    def own_columns(pairs_in, n, depth):
        for image in range(2):
            first = origin[image] + 8
            total = convolve(lhs[image, first : first + local, :depth], n, depth)
            for j, k in enumerate(pairs_in):
                put(image, k, first, finish(total, j, k, image))
        for k in pairs_in:
            build_right(k, D + 16, cols - 32)
            build_left(k, range(1, chunks - 1))
            build_ends(2, k)

    def other_columns(sides, pairs_in, n, depth):
        some = [strip for side in sides for strip in strips[side]]
        rows_in = jnp.concatenate(
            [lhs[image, first : first + count, :depth] for image, first, count in some], axis=0
        )
        total = convolve(rows_in, n, depth)
        for j, k in enumerate(pairs_in):
            at = 0
            for image, first, count in some:
                put(image, k, first, finish(total[at : at + count, :], j, k, image))
                at += count
        for k in pairs_in:
            if 0 in sides:
                build_right(k, 0, D + 16)
                build_left(k, [0])
            if 1 in sides:
                build_right(k, D + cols - 16, 16)
                build_left(k, [chunks - 1])
            for side in sides:
                build_ends(side, k)

    def columns_in(side):
        if side == 0:
            pt[1, base - reach : base, :] = near1[...].astype(jnp.float32)
            pt[0, base - 16 : base, :] = near0[...].astype(jnp.float32)
        else:
            pt[:, base + cols : base + cols + 16, :] = far[...].astype(jnp.float32)
        for image, first, count in strips[side]:
            gather(image, first, count)

    def corners_in(side):
        for image in range(2):
            place_lines(image, 2 * side)
        for image, first, count in strips[side]:
            gather_lines(image, first, count)

    def inner_columns(sides):
        for n in range(inner):
            other_columns(sides, inner_pairs[2 * n : 2 * n + 2], n, 3 * main)

    def outer_columns(sides):
        other_columns(sides, outer_pairs, inner, 3 * main + 128)

    low_lane = lax.broadcasted_iota(jnp.int32, (D, cols), 1) < D
    lane8 = lax.broadcasted_iota(jnp.int32, (8, cols), 1)
    from_x = (lane8 - lax.broadcasted_iota(jnp.int32, (8, cols), 0)).astype(jnp.float32)
    jump = jnp.where(lane8 < D, float(D), -float(D))

    def attend(k):
        score = lax.dot_general(right_m[k], left_m[k], nt, preferred_element_type=jnp.float32)
        for odd in range(2):
            mine = slice(odd * cols, (odd + 1) * cols)
            outer = jnp.where(low_lane, score[:D, mine], score[2 * D :, mine]) + mask[0]
            inner = score[D : 2 * D, mine] + mask[1]
            outer = outer.reshape(D // 8, 8, cols)
            inner = inner.reshape(D // 8, 8, cols)
            best = jnp.maximum(jnp.max(outer, axis=0), jnp.max(inner, axis=0))
            outer = jnp.exp2(outer - best)
            both = outer + jnp.exp2(inner - best)
            tail, steps = both[D // 8 - 1], None
            for j in range(D // 8 - 2, -1, -1):
                steps = tail if steps is None else steps + tail
                tail = tail + both[j]
            moment = from_x * tail - 8.0 * steps + jump * jnp.sum(outer, axis=0)
            y = 2 * k + odd
            for j, value in enumerate((best, tail, moment)):
                part[j, y * 8 : (y + 1) * 8, :] = value

    strip_rows = D + 16
    lane_s = lax.broadcasted_iota(jnp.int32, (strip_rows, 32), 1) % 16
    apart_s = lane_s + D - lax.broadcasted_iota(jnp.int32, (strip_rows, 32), 0)
    within_s = (apart_s >= 1) & (apart_s <= D - 2)
    from_s = apart_s[:8].astype(jnp.float32)

    def attend_strip(k):
        columns = jnp.concatenate([left_m[k, cols - 16 : cols, :], left_m[k, 2 * cols - 16 :, :]], axis=0)
        score = lax.dot_general(
            right_m[k, D + cols - strip_rows :, :], columns, nt, preferred_element_type=jnp.float32
        )
        score = jnp.where(within_s, score, -jnp.inf).reshape(strip_rows // 8, 8, 32)
        best = jnp.max(score, axis=0)
        weight = jnp.exp2(score - best)
        tail, steps = weight[strip_rows // 8 - 1], None
        for j in range(strip_rows // 8 - 2, -1, -1):
            steps = tail if steps is None else steps + tail
            tail = tail + weight[j]
        moment = from_s * tail - 8.0 * steps
        for j, value in enumerate((best, tail, moment)):
            at = (j * pairs + k) * 8
            strip_out[at : at + 8, :32] = value
            value = strip_out[at : at + 8, :]
            part[j, 16 * k : 16 * k + 8, cols - 16 :] = pltpu.roll(value, cols - 16, 1)[:, cols - 16 :]
            part[j, 16 * k + 8 : 16 * k + 16, cols - 16 :] = pltpu.roll(value, cols - 32, 1)[:, cols - 16 :]

    def send_later(order):
        for step in order:
            n = later.index(step)

            @pl.when(exists(step))
            def _(n=n):
                pl.semaphore_wait(ready.at[(0, 2, 1)[n]], 1)

            send(lambda other: other == step)

    def send_beside():
        @pl.when(odd_row & (tall > 1))
        def _():
            pl.semaphore_wait(ready.at[3], tall - 1)

        @pl.when(odd_row)
        def _():
            send(lambda step: step in beside)

    def send_all_later():
        @pl.when(even_row)
        def _():
            send_later(later[1:] + later[:1])

        @pl.when(odd_row)
        def _():
            send_later(later)

    def send_rest():
        send_beside()
        send_all_later()

    root = (my_col == 0) & (my_row < 2) & (lax.axis_index("pairs") == 0)

    @pl.when(my_col > 0)
    def _():
        send_rest()

    for image in range(2):
        gather(image, origin[image] + 8, local)
    for n in range(inner):
        own_columns(inner_pairs[2 * n : 2 * n + 2], n, 3 * main)

    @pl.when((my_col == 0) & jnp.logical_not(root))
    def _():
        send_rest()

    @pl.when(my_col == 0)
    def _():
        columns_in(0)
        inner_columns([0])
        for k in inner_pairs:
            attend(k)

    @pl.when(root)
    def _():
        send_beside()

    half_lane = lax.broadcasted_iota(jnp.int32, (128, 128), 1) < 64
    behind = line - lax.broadcasted_iota(jnp.int32, tile, 0)
    for t, k in enumerate(once):
        hit = [behind == step_y - 2 * k for step_y in range(3)]
        if k == 0:
            hit = [h & (line < 2) for h in hit]
        taps = []
        for step_d in range(3):
            pieces = []
            for step_x in range(3):
                value = jnp.zeros(tile, jnp.float32)
                for step_y in range(3):
                    at = 9 * step_d + 3 * step_y + step_x
                    value = jnp.where(hit[step_y], agg[at : at + 1, :], value)
                pieces.append(value)
            taps.append(pieces)
        gap = [jnp.zeros(tile, jnp.float32)]
        for j, (low_d, high_d) in enumerate(((1, 1), (2, 0))):
            value = jnp.concatenate(taps[low_d] + gap + taps[high_d] + gap, axis=0).T
            for n, keep in ((j, half_lane), (3 - j, jnp.logical_not(half_lane))):
                end_w[n, t * 128 : (t + 1) * 128, :] = jnp.where(keep, value, 0.0).astype(jnp.bfloat16)

    @pl.when(root)
    def _():
        send_all_later()

    tiles = len(once) - len(outer_pairs)

    def sum_ends(columns, where=slice(None)):
        total = None
        for j in range(4):
            term = jnp.dot(
                end_in[j, where, columns], end_w[j, columns, :], preferred_element_type=jnp.float32
            )
            total = term if total is None else total + term
        return total

    def sum_inner_ends():
        end_sum[...] = sum_ends(slice(0, tiles * 128))

    def sum_outer_ends():
        end_sum[...] += sum_ends(slice(tiles * 128, len(once) * 128))
        spread_ends()

    def spread_ends():
        place = lax.broadcasted_iota(jnp.int32, (cols, 128), 1) % 64 // 16
        total = end_sum[15 : 15 + cols, :]
        for step_x in (1, 2):
            total = jnp.where(place == step_x, end_sum[15 + step_x : 15 + step_x + cols, :], total)
        total = total.T
        for n, j in enumerate((0, 64)):
            ends[n] = total[j : j + 16, :] + total[j + 16 : j + 32, :] + total[j + 32 : j + 48, :]

    @pl.when(my_col == 0)
    def _():
        sum_inner_ends()

    receive(lambda step: step[1] == 0)
    for image in range(2):
        place_lines(image, 1)
        gather_lines(image, origin[image] + 8, local)
    own_columns(outer_pairs, inner, 3 * main + 128)

    @pl.when(my_col == 0)
    def _():
        corners_in(0)
        outer_columns([0])

    def staged(sides, do):
        receive(lambda step: step[0] == 0)
        for side in sides:
            columns_in(side)
        inner_columns(sides)
        for k in inner_pairs:
            do(k)
        receive(lambda step: step[0] != 0 and step[1] != 0)
        for side in sides:
            corners_in(side)
        sum_inner_ends()
        outer_columns(sides)
        sum_outer_ends()
        for k in outer_pairs:
            do(k)

    @pl.when(my_col == 0)
    def _():
        receive(lambda step: step[1] != 0)
        columns_in(1)
        corners_in(1)
        inner_columns([1])
        outer_columns([1])
        end_sum[cols:, :] = sum_ends(slice(0, tiles * 128), slice(cols, cols + 32))
        sum_outer_ends()
        for k in inner_pairs:
            attend_strip(k)
        for k in outer_pairs:
            attend(k)

    @pl.when((my_col > 0) & odd_row)
    def _():
        staged([0, 1], attend)

    @pl.when((my_col > 0) & even_row)
    def _():
        receive(lambda step: step[1] != 0)
        for side in range(2):
            columns_in(side)
            corners_in(side)
        inner_columns([0, 1])
        outer_columns([0, 1])
        sum_inner_ends()
        sum_outer_ends()
        for k in range(pairs):
            attend(k)

    for h in range(rows // 8):
        first = ends[0, h * 8 : (h + 1) * 8, :]
        last = ends[1, h * 8 : (h + 1) * 8, :]
        tops = [part[0, pl.ds(h * 64 + j, 8, stride=8), :] for j in range(8)]
        best = jnp.maximum(first, last)
        for top in tops:
            best = jnp.maximum(best, top)
        last = jnp.exp2(last - best)
        total = jnp.exp2(first - best) + last
        moment = last * float(D - 1)
        for j in range(8):
            weight = jnp.exp2(tops[j] - best)
            total = total + weight * part[1, pl.ds(h * 64 + j, 8, stride=8), :]
            moment = moment + weight * part[2, pl.ds(h * 64 + j, 8, stride=8), :]
        out_ref[h * 8 : (h + 1) * 8, :] = moment / total / D

    for step, copy in copies:

        @pl.when(exists(step))
        def _(copy=copy):
            copy.wait_send()


def on_device(images, conv_weight, conv_bias, agg_weight):
    cin, rows, cols = images.shape[1:]
    groups = agg_weight.shape[0]
    per = conv_weight.shape[0] // groups
    main = rows * cin
    pairs = rows // 2
    span = cols + D + 16
    reach = -(-(D + 2) // 16) * 16
    return pl.pallas_call(
        functools.partial(body, (rows, cols, groups, per, cin)),
        out_shape=pltpu.VMEM((rows, cols), jnp.float32),
        in_specs=[pl.BlockSpec(memory_space=pl.ANY)] * 4,
        out_specs=pl.BlockSpec(memory_space=pltpu.VMEM),
        scratch_shapes=[
            pltpu.VMEM(images.shape, images.dtype),
            pltpu.VMEM(conv_weight.shape, conv_weight.dtype),
            pltpu.VMEM((1,) + conv_bias.shape, conv_bias.dtype),
            pltpu.VMEM(agg_weight.shape, agg_weight.dtype),
            pltpu.SemaphoreType.DMA((7,)),
            pltpu.VMEM((2, span + 16, main), jnp.float32),
            pltpu.VMEM((2, span + 32, 128), jnp.float32),
            pltpu.VMEM((2, span, 3 * main + 128), jnp.bfloat16),
            pltpu.VMEM((3 * main + 128, pairs * 128), jnp.bfloat16),
            pltpu.VMEM((4, (pairs // 2 + 1) * 128, 128), jnp.bfloat16),
            pltpu.VMEM((4, cols + 32, (pairs // 2 + 1) * 128), jnp.bfloat16),
            pltpu.VMEM((cols + 32, 128), jnp.float32),
            pltpu.VMEM((2, rows, cols), jnp.float32),
            pltpu.VMEM((9 * cin, 128), jnp.float32),
            pltpu.VMEM((18, 8, 128), jnp.float32),
            pltpu.VMEM((2, D, cols), jnp.float32),
            pltpu.VMEM((pairs, cols + 16, 128), jnp.float32),
            pltpu.VMEM((pairs, span, 128), jnp.float32),
            pltpu.VMEM((pairs, 2 * cols, 640), jnp.bfloat16),
            pltpu.VMEM((pairs, D + cols, 640), jnp.bfloat16),
            pltpu.VMEM((3, rows * 8, cols), jnp.float32),
            pltpu.VMEM((3 * pairs * 8, 128), jnp.float32),
            pltpu.VMEM((2, cols, main), jnp.bfloat16),
            pltpu.VMEM((2, 4 * cin, cols), jnp.bfloat16),
            pltpu.VMEM((16, main), jnp.bfloat16),
            pltpu.VMEM((reach, main), jnp.bfloat16),
            pltpu.VMEM((2, 16, main), jnp.bfloat16),
            pltpu.VMEM((2, 3, 4 * cin, cols), jnp.bfloat16),
            pltpu.SemaphoreType.DMA((9,)),
            pltpu.SemaphoreType.DMA((9,)),
            pltpu.SemaphoreType.REGULAR((4,)),
        ],
        compiler_params=pltpu.CompilerParams(collective_id=0, has_side_effects=True),
    )(images, conv_weight, conv_bias[None], agg_weight)


def solution(mesh):
    in_specs = (P("pairs", None, "row", "col"), P(), P(), P())
    out_specs = P(("pairs", "row"), "col")
    return jax.shard_map(
        on_device, mesh=mesh, in_specs=in_specs, out_specs=out_specs, check_vma=False
    )
```

```python
import functools

import jax
import jax.numpy as jnp
from jax import lax
from jax.experimental import pallas as pl
from jax.experimental.pallas import tpu as pltpu
from jax.sharding import PartitionSpec as P

D = 64
LOG2E = 1.4426950408889634


MESH = pl.DeviceIdType.MESH
STEPS = ((0, 1), (0, -1), (1, 0), (-1, 0), (1, 1), (1, -1), (-1, 1), (-1, -1))


def body(
    shape, images_hbm, weight_hbm, bias_hbm, agg_hbm, out_ref,
    images_ref, weight_ref, bias_in, agg_in, load_sem,
    pt, ext, lhs, wc, end_w, end_in, end_sum, ends, taps_ref, band_w, mask, lf, rf, left_m, right_m, part, strip_out,
    tr_ref, edge_ref, near0, near1, far, lines, send_sem, recv_sem, ready,
):
    rows, cols, groups, per, cin = shape
    feats = groups * per
    pairs = rows // 2
    lead = D + 8
    span = rf.shape[1]
    wide_l = lf.shape[1]
    rows_axis, cols_axis = lax.axis_size("row"), lax.axis_size("col")
    my_row, my_col = lax.axis_index("row"), lax.axis_index("col")
    reach = near1.shape[0]

    def exists(step):
        r, c = my_row + step[0], my_col + step[1]
        return (r >= 0) & (r < rows_axis) & (c >= 0) & (c < cols_axis)

    def device(step):
        return {"row": my_row + step[0], "col": my_col + step[1]}

    odd_row = lax.rem(my_row, 2) == 1
    even_row = jnp.logical_not(odd_row)
    beside, later, earlier = ((1, 0), (-1, 0)), ((0, 1), (1, 1), (-1, 1)), ((0, -1), (1, -1), (-1, -1))

    quarter = cin // 2
    loads = [
        pltpu.make_async_copy(
            images_hbm.at[image, pl.ds(part_at, quarter)],
            images_ref.at[image, pl.ds(part_at, quarter)],
            load_sem.at[2 * image + part_at // quarter],
        )
        for image in range(2)
        for part_at in (0, quarter)
    ]
    for load in loads:
        load.start()

    barrier = pltpu.get_barrier_semaphore()
    for step in later + beside:
        allowed = exists(step) if step in later else exists(step) & odd_row

        @pl.when(allowed)
        def _(step=step):
            pl.semaphore_signal(barrier, inc=1, device_id=device(step), device_id_type=MESH)

    small_loads = [
        pltpu.make_async_copy(source, target, load_sem.at[4 + k])
        for k, (source, target) in enumerate(
            ((weight_hbm, weight_ref), (bias_hbm, bias_in), (agg_hbm, agg_in))
        )
    ]
    tall = 1 + (my_row > 0).astype(jnp.int32) + (my_row < rows_axis - 1).astype(jnp.int32)
    greeted = jnp.where(my_col > 0, tall, 0) + jnp.where(even_row, tall - 1, 0)

    @pl.when(greeted > 0)
    def _():
        pl.semaphore_wait(barrier, greeted)

    for n, step in enumerate(earlier):

        @pl.when(exists(step))
        def _(n=n, step=step):
            pl.semaphore_signal(ready.at[n], inc=1, device_id=device(step), device_id_type=MESH)

    for step in beside:

        @pl.when(exists(step) & even_row)
        def _(step=step):
            pl.semaphore_signal(ready.at[3], inc=1, device_id=device(step), device_id_type=MESH)

    for load in small_loads:
        load.start()
    for load in loads:
        load.wait()

    main = rows * cin
    for image in range(2):
        for side, first in ((0, 0), (1, rows - 2)):
            pair = [images_ref[image, :, first + y, :] for y in range(2)]
            edge_ref[side, image * 2 * cin : (image + 1) * 2 * cin, :] = jnp.concatenate(
                pair, axis=0
            ).astype(jnp.bfloat16)

    plan = [
        ((0, 1), tr_ref.at[1, pl.ds(cols - reach, reach), :], near1),
        ((0, 1), tr_ref.at[0, pl.ds(cols - 16, 16), :], near0),
        ((0, -1), tr_ref.at[:, pl.ds(0, 16), :], far),
    ]
    for r in (1, -1):
        side = 0 if r == 1 else 1
        for c in (0, 1, -1):
            plan.append(((r, c), edge_ref.at[1 - side], lines.at[side, 1 - c]))
    copies = []
    for k, (step, source, target) in enumerate(plan):
        copy = pltpu.make_async_remote_copy(
            src_ref=source,
            dst_ref=target,
            send_sem=send_sem.at[k],
            recv_sem=recv_sem.at[k],
            device_id=device(step),
            device_id_type=MESH,
        )
        copies.append((step, copy))

    def send(chosen):
        for step, copy in copies:
            if chosen(step):

                @pl.when(exists(step))
                def _(copy=copy):
                    copy.start()

    def receive(chosen):
        for step, copy in copies:
            if chosen(step):

                @pl.when(exists((-step[0], -step[1])))
                def _(copy=copy):
                    copy.wait_recv()

    send(lambda step: step in earlier[1:])

    @pl.when(even_row)
    def _():
        send(lambda step: step in beside)

    for image in range(2):
        tr_ref[image] = images_ref[image].reshape(main, cols).T.astype(jnp.bfloat16)
    send(lambda step: step == earlier[0])

    for k, (step, source, target) in enumerate(plan):

        @pl.when(jnp.logical_not(exists((-step[0], -step[1]))))
        def _(target=target):
            target[...] = jnp.zeros(target.shape, target.dtype)

    for load in small_loads:
        load.wait()


    tn = (((0,), (0,)), ((), ()))
    nt = (((1,), (1,)), ((), ()))
    tile = (rows, 128)
    lane = lax.broadcasted_iota(jnp.int32, tile, 1)
    line = lane // feats
    spread = (
        lax.broadcasted_iota(jnp.int32, (feats, 128), 1) % feats
        == lax.broadcasted_iota(jnp.int32, (feats, 128), 0)
    ).astype(jnp.float32)
    one = (
        lax.broadcasted_iota(jnp.int32, (groups, 128), 1) % feats // per
        == lax.broadcasted_iota(jnp.int32, (groups, 128), 0)
    ).astype(jnp.float32)
    exact = dict(precision=lax.Precision.HIGHEST, preferred_element_type=jnp.float32)
    bias = jnp.dot(bias_in[...], spread, **exact)
    taps_ref[...] = lax.dot_general(
        weight_ref[...].astype(jnp.float32), spread, tn, preferred_element_type=jnp.float32
    )
    agg = lax.dot_general(agg_in[...], one, tn, **exact) * (LOG2E / per)

    above = lax.broadcasted_iota(jnp.int32, tile, 0) - line + 2
    near_line = line[:cin]
    inner_pairs, outer_pairs = list(range(1, pairs - 1)), [0, pairs - 1]
    for n, k in enumerate(inner_pairs + outer_pairs):
        columns = slice(n * 128, (n + 1) * 128)
        hit = [above == step_y + 2 * k for step_y in range(3)]
        for step_x in range(3):
            for c in range(cin):
                value = jnp.zeros(tile, jnp.float32)
                for step_y in range(3):
                    at = (step_y * 3 + step_x) * cin + c
                    value = jnp.where(hit[step_y], taps_ref[at : at + 1, :], value)
                begin = step_x * main + c * rows
                wc[begin : begin + rows, columns] = value.astype(jnp.bfloat16)
        if k in outer_pairs:
            for step_x in range(3):
                for side in range(2):
                    halves = []
                    for y in range(2):
                        row = y - 2 if side == 0 else rows + y
                        value = jnp.zeros((cin, 128), jnp.float32)
                        for step_y in range(3):
                            at = (step_y * 3 + step_x) * cin
                            value = jnp.where(
                                near_line == row - 2 * k + 2 - step_y, taps_ref[at : at + cin, :], value
                            )
                        halves.append(value)
                    begin = 3 * main + (step_x * 2 + side) * 2 * cin
                    wc[begin : begin + 2 * cin, columns] = (
                        jnp.concatenate(halves, axis=0).astype(jnp.bfloat16)
                    )
            begin = 3 * main + 12 * cin
            wc[begin:, columns] = jnp.zeros((wc.shape[0] - begin, 128), jnp.bfloat16)

    for step_d in range(3):
        for step_x in range(3):
            for odd in range(2):
                value = jnp.zeros((8, 128), jnp.float32)
                for step_y in range(3):
                    at = 9 * step_d + 3 * step_y + step_x
                    value = jnp.where(line[:8] == step_y + odd, agg[at : at + 1, :], value)
                band_w[(step_d * 3 + step_x) * 2 + odd] = value

    once = inner_pairs[::2] + outer_pairs
    at_x = lax.broadcasted_iota(jnp.int32, (D, cols), 1)
    at_i = lax.broadcasted_iota(jnp.int32, (D, cols), 0)
    low = at_x < D
    for j, apart in enumerate((jnp.where(low, at_x - at_i + D, at_x - at_i - D), at_x - at_i)):
        mask[j] = jnp.where((apart >= 1) & (apart <= D - 2), 0.0, -jnp.inf)

    base = 16 + D
    pt[:, base : base + cols, :] = tr_ref[...].astype(jnp.float32)
    ext[:, :, 12 * cin :] = jnp.zeros((2, span + 32, 128 - 12 * cin), jnp.float32)

    @pl.when(my_col == 0)
    def _():
        right_m[:, D + cols - 16 :, :] = jnp.zeros((pairs, 16, 640), jnp.bfloat16)

    left_ok = (my_col > 0).astype(jnp.float32)
    right_ok = (my_col < cols_axis - 1).astype(jnp.float32)
    top_ok = (my_row > 0) | (line[:1] > 0)
    end_ok = (my_row < rows_axis - 1) | (line[:1] < 3)
    base = 16 + D
    counts = (wide_l, span)
    origin = (8, lead)
    local = cols - 16

    def gather(image, first, count):
        begin = 8 + origin[1] - origin[image] + first
        for step_x in range(3):
            at = begin + step_x - 1
            lhs[image, first : first + count, step_x * main : (step_x + 1) * main] = (
                pt[image, at : at + count, :].astype(jnp.bfloat16)
            )

    def gather_lines(image, first, count):
        at = 16 + origin[1] - origin[image] + first
        lhs[image, first : first + count, 3 * main :] = ext[image, at : at + count, :].astype(jnp.bfloat16)

    def finish(total, j, k, image):
        value = total[:, j * 128 : (j + 1) * 128] + bias
        value = jnp.maximum(value, value * 0.1)
        value = value.astype(jnp.bfloat16).astype(jnp.float32)
        if image == 0 and k == 0:
            value = jnp.where(top_ok, value, 0.0)
        if image == 0 and k == pairs - 1:
            value = jnp.where(end_ok, value, 0.0)
        return value

    def convolve(rows_in, n, depth):
        return jnp.dot(
            rows_in, wc[:depth, n * 256 : (n + 1) * 256], preferred_element_type=jnp.float32
        )

    def put(image, k, begin, value):
        store = (lf, rf)[image]
        edge = origin[image]
        end = begin + value.shape[0]
        if begin < edge:
            store[k, begin:edge, :] = value[: edge - begin, :] * left_ok
            value, begin = value[edge - begin :, :], edge
        if image == 0 and end > 8 + cols:
            store[k, 8 + cols : end, :] = value[8 + cols - begin :, :] * right_ok
            value = value[: 8 + cols - begin, :]
        store[k, begin : begin + value.shape[0], :] = value

    def place_lines(image, place):
        half = 2 * cin
        block = jnp.concatenate(
            [
                lines[side, place, image * half : (image + 1) * half, :].astype(jnp.float32)
                for side in range(2)
            ]
            * 3
            + [jnp.zeros((128 - 6 * half, cols), jnp.float32)],
            axis=0,
        ).T
        at = 8 + base
        if place == 0:
            keep = reach if image else 16
            at, block = at - keep, block[cols - keep :, :]
        elif place == 2:
            at, block = at + cols, block[:16, :]
        for step_x in range(3):
            begin = at + 1 - step_x
            some = slice(step_x * 2 * half, (step_x + 1) * 2 * half)
            ext[image, begin : begin + block.shape[0], some] = block[:, some]

    def build_right(k, begin, count):
        for delta in range(-2, 3):
            at = lead - D + delta + begin
            right_m[k, begin : begin + count, (delta + 2) * 128 : (delta + 3) * 128] = (
                rf[k, at : at + count, :].astype(jnp.bfloat16)
            )

    def build_left(k, chunks):
        for chunk in chunks:
            at = 7 + chunk * 16
            shifted = [lf[k, at + c : at + c + 16, :].reshape(2, 8, 128) for c in range(3)]
            for odd in range(2):
                for delta in range(-2, 3):
                    value = None
                    for c in range(3):
                        a = c - delta
                        if 0 <= a < 3:
                            term = shifted[c] * band_w[(a * 3 + c) * 2 + odd]
                            value = term if value is None else value + term
                    left_m[
                        k,
                        odd * cols + chunk * 16 : odd * cols + chunk * 16 + 16,
                        (delta + 2) * 128 : (delta + 3) * 128,
                    ] = value.reshape(16, 128).astype(jnp.bfloat16)

    def end_product(k, d, x, count):
        return lf[k, 8 + x : 8 + x + count, :] * rf[k, lead + x - d : lead + x - d + count, :]

    def build_ends(where, k):
        if k not in once:
            return
        columns = slice(once.index(k) * 128, (once.index(k) + 1) * 128)
        gap = jnp.zeros((8, 128), jnp.float32)
        for j, d in enumerate((0, 1, D - 2, D - 1)):
            reached = 16 if j < 2 else D + 16
            if where == 2:
                x, count = reached, cols - 16 - reached
            elif where == 0:
                x, count = 0, reached
                block = jnp.concatenate([gap, end_product(k, d, -8, 8)], axis=0)
                end_in[j, 0:16, columns] = block.astype(jnp.bfloat16)
            else:
                x, count = cols - 16, 16
                block = jnp.concatenate([end_product(k, d, cols, 8), gap], axis=0)
                end_in[j, 16 + cols :, columns] = block.astype(jnp.bfloat16)
            end_in[j, 16 + x : 16 + x + count, columns] = end_product(k, d, x, count).astype(jnp.bfloat16)

    chunks = cols // 16
    inner = len(inner_pairs) // 2
    strips = (((1, 0, lead + 8), (0, 0, 16)), ((1, span - 16, 16), (0, wide_l - 16, 16)))

    def own_columns(pairs_in, n, depth):
        for image in range(2):
            first = origin[image] + 8
            total = convolve(lhs[image, first : first + local, :depth], n, depth)
            for j, k in enumerate(pairs_in):
                put(image, k, first, finish(total, j, k, image))
        for k in pairs_in:
            build_right(k, D + 16, cols - 32)
            build_left(k, range(1, chunks - 1))
            build_ends(2, k)

    def other_columns(sides, pairs_in, n, depth):
        some = [strip for side in sides for strip in strips[side]]
        rows_in = jnp.concatenate(
            [lhs[image, first : first + count, :depth] for image, first, count in some], axis=0
        )
        total = convolve(rows_in, n, depth)
        for j, k in enumerate(pairs_in):
            at = 0
            for image, first, count in some:
                put(image, k, first, finish(total[at : at + count, :], j, k, image))
                at += count
        for k in pairs_in:
            if 0 in sides:
                build_right(k, 0, D + 16)
                build_left(k, [0])
            if 1 in sides:
                build_right(k, D + cols - 16, 16)
                build_left(k, [chunks - 1])
            for side in sides:
                build_ends(side, k)

    def columns_in(side):
        if side == 0:
            pt[1, base - reach : base, :] = near1[...].astype(jnp.float32)
            pt[0, base - 16 : base, :] = near0[...].astype(jnp.float32)
        else:
            pt[:, base + cols : base + cols + 16, :] = far[...].astype(jnp.float32)
        for image, first, count in strips[side]:
            gather(image, first, count)

    def corners_in(side):
        for image in range(2):
            place_lines(image, 2 * side)
        for image, first, count in strips[side]:
            gather_lines(image, first, count)

    def inner_columns(sides):
        for n in range(inner):
            other_columns(sides, inner_pairs[2 * n : 2 * n + 2], n, 3 * main)

    def outer_columns(sides):
        other_columns(sides, outer_pairs, inner, 3 * main + 128)

    low_lane = lax.broadcasted_iota(jnp.int32, (D, cols), 1) < D
    lane8 = lax.broadcasted_iota(jnp.int32, (8, cols), 1)
    from_x = (lane8 - lax.broadcasted_iota(jnp.int32, (8, cols), 0)).astype(jnp.float32)
    jump = jnp.where(lane8 < D, float(D), -float(D))

    def attend(k):
        score = lax.dot_general(right_m[k], left_m[k], nt, preferred_element_type=jnp.float32)
        for odd in range(2):
            mine = slice(odd * cols, (odd + 1) * cols)
            outer = jnp.where(low_lane, score[:D, mine], score[2 * D :, mine]) + mask[0]
            inner = score[D : 2 * D, mine] + mask[1]
            outer = outer.reshape(D // 8, 8, cols)
            inner = inner.reshape(D // 8, 8, cols)
            best = jnp.maximum(jnp.max(outer, axis=0), jnp.max(inner, axis=0))
            outer = jnp.exp2(outer - best)
            both = outer + jnp.exp2(inner - best)
            tail, steps = both[D // 8 - 1], None
            for j in range(D // 8 - 2, -1, -1):
                steps = tail if steps is None else steps + tail
                tail = tail + both[j]
            moment = from_x * tail - 8.0 * steps + jump * jnp.sum(outer, axis=0)
            y = 2 * k + odd
            for j, value in enumerate((best, tail, moment)):
                part[j, y * 8 : (y + 1) * 8, :] = value

    strip_rows = D + 16
    lane_s = lax.broadcasted_iota(jnp.int32, (strip_rows, 32), 1) % 16
    apart_s = lane_s + D - lax.broadcasted_iota(jnp.int32, (strip_rows, 32), 0)
    within_s = (apart_s >= 1) & (apart_s <= D - 2)
    from_s = apart_s[:8].astype(jnp.float32)

    def attend_strip(k):
        columns = jnp.concatenate([left_m[k, cols - 16 : cols, :], left_m[k, 2 * cols - 16 :, :]], axis=0)
        score = lax.dot_general(
            right_m[k, D + cols - strip_rows :, :], columns, nt, preferred_element_type=jnp.float32
        )
        score = jnp.where(within_s, score, -jnp.inf).reshape(strip_rows // 8, 8, 32)
        best = jnp.max(score, axis=0)
        weight = jnp.exp2(score - best)
        tail, steps = weight[strip_rows // 8 - 1], None
        for j in range(strip_rows // 8 - 2, -1, -1):
            steps = tail if steps is None else steps + tail
            tail = tail + weight[j]
        moment = from_s * tail - 8.0 * steps
        for j, value in enumerate((best, tail, moment)):
            at = (j * pairs + k) * 8
            strip_out[at : at + 8, :32] = value
            value = strip_out[at : at + 8, :]
            part[j, 16 * k : 16 * k + 8, cols - 16 :] = pltpu.roll(value, cols - 16, 1)[:, cols - 16 :]
            part[j, 16 * k + 8 : 16 * k + 16, cols - 16 :] = pltpu.roll(value, cols - 32, 1)[:, cols - 16 :]

    def send_later(order):
        for step in order:
            n = later.index(step)

            @pl.when(exists(step))
            def _(n=n):
                pl.semaphore_wait(ready.at[(0, 2, 1)[n]], 1)

            send(lambda other: other == step)

    def send_beside():
        @pl.when(odd_row & (tall > 1))
        def _():
            pl.semaphore_wait(ready.at[3], tall - 1)

        @pl.when(odd_row)
        def _():
            send(lambda step: step in beside)

    def send_all_later():
        @pl.when(even_row)
        def _():
            send_later(later[1:] + later[:1])

        @pl.when(odd_row)
        def _():
            send_later(later)

    def send_rest():
        send_beside()
        send_all_later()

    root = (my_col == 0) & (my_row < 2) & (lax.axis_index("pairs") == 0)

    @pl.when(my_col > 0)
    def _():
        send_rest()

    for image in range(2):
        gather(image, origin[image] + 8, local)
    for n in range(inner):
        own_columns(inner_pairs[2 * n : 2 * n + 2], n, 3 * main)

    @pl.when((my_col == 0) & jnp.logical_not(root))
    def _():
        send_rest()

    @pl.when(my_col == 0)
    def _():
        columns_in(0)
        inner_columns([0])
        for k in inner_pairs:
            attend(k)

    @pl.when(root)
    def _():
        send_beside()

    half_lane = lax.broadcasted_iota(jnp.int32, (128, 128), 1) < 64
    behind = line - lax.broadcasted_iota(jnp.int32, tile, 0)
    for t, k in enumerate(once):
        hit = [behind == step_y - 2 * k for step_y in range(3)]
        if k == 0:
            hit = [h & (line < 2) for h in hit]
        taps = []
        for step_d in range(3):
            pieces = []
            for step_x in range(3):
                value = jnp.zeros(tile, jnp.float32)
                for step_y in range(3):
                    at = 9 * step_d + 3 * step_y + step_x
                    value = jnp.where(hit[step_y], agg[at : at + 1, :], value)
                pieces.append(value)
            taps.append(pieces)
        gap = [jnp.zeros(tile, jnp.float32)]
        for j, (low_d, high_d) in enumerate(((1, 1), (2, 0))):
            value = jnp.concatenate(taps[low_d] + gap + taps[high_d] + gap, axis=0).T
            for n, keep in ((j, half_lane), (3 - j, jnp.logical_not(half_lane))):
                end_w[n, t * 128 : (t + 1) * 128, :] = jnp.where(keep, value, 0.0).astype(jnp.bfloat16)

    @pl.when(root)
    def _():
        send_all_later()

    tiles = len(once) - len(outer_pairs)

    def sum_ends(columns, where=slice(None)):
        total = None
        for j in range(4):
            term = jnp.dot(
                end_in[j, where, columns], end_w[j, columns, :], preferred_element_type=jnp.float32
            )
            total = term if total is None else total + term
        return total

    def sum_inner_ends():
        end_sum[...] = sum_ends(slice(0, tiles * 128))

    def sum_outer_ends():
        end_sum[...] += sum_ends(slice(tiles * 128, len(once) * 128))
        spread_ends()

    def spread_ends():
        place = lax.broadcasted_iota(jnp.int32, (cols, 128), 1) % 64 // 16
        total = end_sum[15 : 15 + cols, :]
        for step_x in (1, 2):
            total = jnp.where(place == step_x, end_sum[15 + step_x : 15 + step_x + cols, :], total)
        total = total.T
        for n, j in enumerate((0, 64)):
            ends[n] = total[j : j + 16, :] + total[j + 16 : j + 32, :] + total[j + 32 : j + 48, :]

    @pl.when(my_col == 0)
    def _():
        sum_inner_ends()

    receive(lambda step: step[1] == 0)
    for image in range(2):
        place_lines(image, 1)
        gather_lines(image, origin[image] + 8, local)
    own_columns(outer_pairs, inner, 3 * main + 128)

    @pl.when(my_col == 0)
    def _():
        corners_in(0)
        outer_columns([0])

    def staged(sides, do):
        receive(lambda step: step[0] == 0)
        for side in sides:
            columns_in(side)
        inner_columns(sides)
        for k in inner_pairs:
            do(k)
        receive(lambda step: step[0] != 0 and step[1] != 0)
        for side in sides:
            corners_in(side)
        sum_inner_ends()
        outer_columns(sides)
        sum_outer_ends()
        for k in outer_pairs:
            do(k)

    @pl.when(my_col == 0)
    def _():
        receive(lambda step: step[1] != 0)
        columns_in(1)
        corners_in(1)
        inner_columns([1])
        outer_columns([1])
        end_sum[cols:, :] = sum_ends(slice(0, tiles * 128), slice(cols, cols + 32))
        sum_outer_ends()
        for k in inner_pairs:
            attend_strip(k)
        for k in outer_pairs:
            attend(k)

    @pl.when((my_col > 0) & odd_row)
    def _():
        staged([0, 1], attend)

    @pl.when((my_col > 0) & even_row)
    def _():
        receive(lambda step: step[1] != 0)
        for side in range(2):
            columns_in(side)
            corners_in(side)
        inner_columns([0, 1])
        outer_columns([0, 1])
        sum_inner_ends()
        sum_outer_ends()
        for k in range(pairs):
            attend(k)

    for h in range(rows // 8):
        first = ends[0, h * 8 : (h + 1) * 8, :]
        last = ends[1, h * 8 : (h + 1) * 8, :]
        tops = [part[0, pl.ds(h * 64 + j, 8, stride=8), :] for j in range(8)]
        best = jnp.maximum(first, last)
        for top in tops:
            best = jnp.maximum(best, top)
        last = jnp.exp2(last - best)
        total = jnp.exp2(first - best) + last
        moment = last * float(D - 1)
        for j in range(8):
            weight = jnp.exp2(tops[j] - best)
            total = total + weight * part[1, pl.ds(h * 64 + j, 8, stride=8), :]
            moment = moment + weight * part[2, pl.ds(h * 64 + j, 8, stride=8), :]
        out_ref[h * 8 : (h + 1) * 8, :] = moment / (total * D)

    for step, copy in copies:

        @pl.when(exists(step))
        def _(copy=copy):
            copy.wait_send()


def on_device(images, conv_weight, conv_bias, agg_weight):
    cin, rows, cols = images.shape[1:]
    groups = agg_weight.shape[0]
    per = conv_weight.shape[0] // groups
    main = rows * cin
    pairs = rows // 2
    span = cols + D + 16
    reach = -(-(D + 2) // 16) * 16
    return pl.pallas_call(
        functools.partial(body, (rows, cols, groups, per, cin)),
        out_shape=pltpu.VMEM((rows, cols), jnp.float32),
        in_specs=[pl.BlockSpec(memory_space=pl.ANY)] * 4,
        out_specs=pl.BlockSpec(memory_space=pltpu.VMEM),
        scratch_shapes=[
            pltpu.VMEM(images.shape, images.dtype),
            pltpu.VMEM(conv_weight.shape, conv_weight.dtype),
            pltpu.VMEM((1,) + conv_bias.shape, conv_bias.dtype),
            pltpu.VMEM(agg_weight.shape, agg_weight.dtype),
            pltpu.SemaphoreType.DMA((7,)),
            pltpu.VMEM((2, span + 16, main), jnp.float32),
            pltpu.VMEM((2, span + 32, 128), jnp.float32),
            pltpu.VMEM((2, span, 3 * main + 128), jnp.bfloat16),
            pltpu.VMEM((3 * main + 128, pairs * 128), jnp.bfloat16),
            pltpu.VMEM((4, (pairs // 2 + 1) * 128, 128), jnp.bfloat16),
            pltpu.VMEM((4, cols + 32, (pairs // 2 + 1) * 128), jnp.bfloat16),
            pltpu.VMEM((cols + 32, 128), jnp.float32),
            pltpu.VMEM((2, rows, cols), jnp.float32),
            pltpu.VMEM((9 * cin, 128), jnp.float32),
            pltpu.VMEM((18, 8, 128), jnp.float32),
            pltpu.VMEM((2, D, cols), jnp.float32),
            pltpu.VMEM((pairs, cols + 16, 128), jnp.float32),
            pltpu.VMEM((pairs, span, 128), jnp.float32),
            pltpu.VMEM((pairs, 2 * cols, 640), jnp.bfloat16),
            pltpu.VMEM((pairs, D + cols, 640), jnp.bfloat16),
            pltpu.VMEM((3, rows * 8, cols), jnp.float32),
            pltpu.VMEM((3 * pairs * 8, 128), jnp.float32),
            pltpu.VMEM((2, cols, main), jnp.bfloat16),
            pltpu.VMEM((2, 4 * cin, cols), jnp.bfloat16),
            pltpu.VMEM((16, main), jnp.bfloat16),
            pltpu.VMEM((reach, main), jnp.bfloat16),
            pltpu.VMEM((2, 16, main), jnp.bfloat16),
            pltpu.VMEM((2, 3, 4 * cin, cols), jnp.bfloat16),
            pltpu.SemaphoreType.DMA((9,)),
            pltpu.SemaphoreType.DMA((9,)),
            pltpu.SemaphoreType.REGULAR((4,)),
        ],
        compiler_params=pltpu.CompilerParams(collective_id=0, has_side_effects=True),
    )(images, conv_weight, conv_bias[None], agg_weight)


def solution(mesh):
    in_specs = (P("pairs", None, "row", "col"), P(), P(), P())
    out_specs = P(("pairs", "row"), "col")
    return jax.shard_map(
        on_device, mesh=mesh, in_specs=in_specs, out_specs=out_specs, check_vma=False
    )
```

```python
import functools

import jax
import jax.numpy as jnp
from jax import lax
from jax.experimental import pallas as pl
from jax.experimental.pallas import tpu as pltpu
from jax.sharding import PartitionSpec as P

D = 64
LOG2E = 1.4426950408889634


MESH = pl.DeviceIdType.MESH
STEPS = ((0, 1), (0, -1), (1, 0), (-1, 0), (1, 1), (1, -1), (-1, 1), (-1, -1))


def body(
    shape, images_hbm, weight_hbm, bias_hbm, agg_hbm, out_ref,
    images_ref, weight_ref, bias_in, agg_in, load_sem,
    pt, ext, lhs, wc, end_w, end_in, end_sum, ends, taps_ref, band_w, mask, lf, rf, left_m, right_m, part, strip_out,
    tr_ref, edge_ref, near0, near1, far, lines, send_sem, recv_sem, ready,
):
    rows, cols, groups, per, cin = shape
    feats = groups * per
    pairs = rows // 2
    lead = D + 8
    span = rf.shape[1]
    wide_l = lf.shape[1]
    rows_axis, cols_axis = lax.axis_size("row"), lax.axis_size("col")
    my_row, my_col = lax.axis_index("row"), lax.axis_index("col")
    reach = near1.shape[0]

    def exists(step):
        r, c = my_row + step[0], my_col + step[1]
        return (r >= 0) & (r < rows_axis) & (c >= 0) & (c < cols_axis)

    def device(step):
        return {"row": my_row + step[0], "col": my_col + step[1]}

    odd_row = lax.rem(my_row, 2) == 1
    even_row = jnp.logical_not(odd_row)
    beside, later, earlier = ((1, 0), (-1, 0)), ((0, 1), (1, 1), (-1, 1)), ((0, -1), (1, -1), (-1, -1))

    barrier = pltpu.get_barrier_semaphore()
    for step in later + beside:
        allowed = exists(step) if step in later else exists(step) & odd_row

        @pl.when(allowed)
        def _(step=step):
            pl.semaphore_signal(barrier, inc=1, device_id=device(step), device_id_type=MESH)

    quarter = cin // 2
    loads = [
        pltpu.make_async_copy(
            images_hbm.at[image, pl.ds(part_at, quarter)],
            images_ref.at[image, pl.ds(part_at, quarter)],
            load_sem.at[2 * image + part_at // quarter],
        )
        for image in range(2)
        for part_at in (0, quarter)
    ]
    small_loads = [
        pltpu.make_async_copy(source, target, load_sem.at[4 + k])
        for k, (source, target) in enumerate(
            ((weight_hbm, weight_ref), (bias_hbm, bias_in), (agg_hbm, agg_in))
        )
    ]
    for load in loads + small_loads:
        load.start()
    tall = 1 + (my_row > 0).astype(jnp.int32) + (my_row < rows_axis - 1).astype(jnp.int32)
    greeted = jnp.where(my_col > 0, tall, 0) + jnp.where(even_row, tall - 1, 0)

    @pl.when(greeted > 0)
    def _():
        pl.semaphore_wait(barrier, greeted)

    for n, step in enumerate(earlier):

        @pl.when(exists(step))
        def _(n=n, step=step):
            pl.semaphore_signal(ready.at[n], inc=1, device_id=device(step), device_id_type=MESH)

    for step in beside:

        @pl.when(exists(step) & even_row)
        def _(step=step):
            pl.semaphore_signal(ready.at[3], inc=1, device_id=device(step), device_id_type=MESH)

    for load in loads:
        load.wait()

    main = rows * cin
    for image in range(2):
        for side, first in ((0, 0), (1, rows - 2)):
            pair = [images_ref[image, :, first + y, :] for y in range(2)]
            edge_ref[side, image * 2 * cin : (image + 1) * 2 * cin, :] = jnp.concatenate(
                pair, axis=0
            ).astype(jnp.bfloat16)

    plan = [
        ((0, 1), tr_ref.at[1, pl.ds(cols - reach, reach), :], near1),
        ((0, 1), tr_ref.at[0, pl.ds(cols - 16, 16), :], near0),
        ((0, -1), tr_ref.at[:, pl.ds(0, 16), :], far),
    ]
    for r in (1, -1):
        side = 0 if r == 1 else 1
        for c in (0, 1, -1):
            plan.append(((r, c), edge_ref.at[1 - side], lines.at[side, 1 - c]))
    copies = []
    for k, (step, source, target) in enumerate(plan):
        copy = pltpu.make_async_remote_copy(
            src_ref=source,
            dst_ref=target,
            send_sem=send_sem.at[k],
            recv_sem=recv_sem.at[k],
            device_id=device(step),
            device_id_type=MESH,
        )
        copies.append((step, copy))

    def send(chosen):
        for step, copy in copies:
            if chosen(step):

                @pl.when(exists(step))
                def _(copy=copy):
                    copy.start()

    def receive(chosen):
        for step, copy in copies:
            if chosen(step):

                @pl.when(exists((-step[0], -step[1])))
                def _(copy=copy):
                    copy.wait_recv()

    send(lambda step: step in earlier[1:])
    for image in range(2):
        tr_ref[image] = images_ref[image].reshape(main, cols).T.astype(jnp.bfloat16)
    send(lambda step: step == earlier[0])

    @pl.when(even_row)
    def _():
        send(lambda step: step in beside)

    for k, (step, source, target) in enumerate(plan):

        @pl.when(jnp.logical_not(exists((-step[0], -step[1]))))
        def _(target=target):
            target[...] = jnp.zeros(target.shape, target.dtype)

    for load in small_loads:
        load.wait()


    tn = (((0,), (0,)), ((), ()))
    nt = (((1,), (1,)), ((), ()))
    tile = (rows, 128)
    lane = lax.broadcasted_iota(jnp.int32, tile, 1)
    line = lane // feats
    spread = (
        lax.broadcasted_iota(jnp.int32, (feats, 128), 1) % feats
        == lax.broadcasted_iota(jnp.int32, (feats, 128), 0)
    ).astype(jnp.float32)
    one = (
        lax.broadcasted_iota(jnp.int32, (groups, 128), 1) % feats // per
        == lax.broadcasted_iota(jnp.int32, (groups, 128), 0)
    ).astype(jnp.float32)
    exact = dict(precision=lax.Precision.HIGHEST, preferred_element_type=jnp.float32)
    bias = jnp.dot(bias_in[...], spread, **exact)
    taps_ref[...] = lax.dot_general(
        weight_ref[...].astype(jnp.float32), spread, tn, preferred_element_type=jnp.float32
    )
    agg = lax.dot_general(agg_in[...], one, tn, **exact) * (LOG2E / per)

    above = lax.broadcasted_iota(jnp.int32, tile, 0) - line + 2
    near_line = line[:cin]
    inner_pairs, outer_pairs = list(range(1, pairs - 1)), [0, pairs - 1]
    for n, k in enumerate(inner_pairs + outer_pairs):
        columns = slice(n * 128, (n + 1) * 128)
        hit = [above == step_y + 2 * k for step_y in range(3)]
        for step_x in range(3):
            for c in range(cin):
                value = jnp.zeros(tile, jnp.float32)
                for step_y in range(3):
                    at = (step_y * 3 + step_x) * cin + c
                    value = jnp.where(hit[step_y], taps_ref[at : at + 1, :], value)
                begin = step_x * main + c * rows
                wc[begin : begin + rows, columns] = value.astype(jnp.bfloat16)
        if k in outer_pairs:
            for step_x in range(3):
                for side in range(2):
                    halves = []
                    for y in range(2):
                        row = y - 2 if side == 0 else rows + y
                        value = jnp.zeros((cin, 128), jnp.float32)
                        for step_y in range(3):
                            at = (step_y * 3 + step_x) * cin
                            value = jnp.where(
                                near_line == row - 2 * k + 2 - step_y, taps_ref[at : at + cin, :], value
                            )
                        halves.append(value)
                    begin = 3 * main + (step_x * 2 + side) * 2 * cin
                    wc[begin : begin + 2 * cin, columns] = (
                        jnp.concatenate(halves, axis=0).astype(jnp.bfloat16)
                    )
            begin = 3 * main + 12 * cin
            wc[begin:, columns] = jnp.zeros((wc.shape[0] - begin, 128), jnp.bfloat16)

    for step_d in range(3):
        for step_x in range(3):
            for odd in range(2):
                value = jnp.zeros((8, 128), jnp.float32)
                for step_y in range(3):
                    at = 9 * step_d + 3 * step_y + step_x
                    value = jnp.where(line[:8] == step_y + odd, agg[at : at + 1, :], value)
                band_w[(step_d * 3 + step_x) * 2 + odd] = value

    once = inner_pairs[::2] + outer_pairs
    at_x = lax.broadcasted_iota(jnp.int32, (D, cols), 1)
    at_i = lax.broadcasted_iota(jnp.int32, (D, cols), 0)
    low = at_x < D
    for j, apart in enumerate((jnp.where(low, at_x - at_i + D, at_x - at_i - D), at_x - at_i)):
        mask[j] = jnp.where((apart >= 1) & (apart <= D - 2), 0.0, -jnp.inf)

    base = 16 + D
    pt[:, base : base + cols, :] = tr_ref[...].astype(jnp.float32)
    ext[:, :, 12 * cin :] = jnp.zeros((2, span + 32, 128 - 12 * cin), jnp.float32)

    @pl.when(my_col == 0)
    def _():
        right_m[:, D + cols - 16 :, :] = jnp.zeros((pairs, 16, 640), jnp.bfloat16)

    left_ok = (my_col > 0).astype(jnp.float32)
    right_ok = (my_col < cols_axis - 1).astype(jnp.float32)
    top_ok = (my_row > 0) | (line[:1] > 0)
    end_ok = (my_row < rows_axis - 1) | (line[:1] < 3)
    base = 16 + D
    counts = (wide_l, span)
    origin = (8, lead)
    local = cols - 16

    def gather(image, first, count):
        begin = 8 + origin[1] - origin[image] + first
        for step_x in range(3):
            at = begin + step_x - 1
            lhs[image, first : first + count, step_x * main : (step_x + 1) * main] = (
                pt[image, at : at + count, :].astype(jnp.bfloat16)
            )

    def gather_lines(image, first, count):
        at = 16 + origin[1] - origin[image] + first
        lhs[image, first : first + count, 3 * main :] = ext[image, at : at + count, :].astype(jnp.bfloat16)

    def finish(total, j, k, image):
        value = total[:, j * 128 : (j + 1) * 128] + bias
        value = jnp.maximum(value, value * 0.1)
        value = value.astype(jnp.bfloat16).astype(jnp.float32)
        if image == 0 and k == 0:
            value = jnp.where(top_ok, value, 0.0)
        if image == 0 and k == pairs - 1:
            value = jnp.where(end_ok, value, 0.0)
        return value

    def convolve(rows_in, n, depth):
        return jnp.dot(
            rows_in, wc[:depth, n * 256 : (n + 1) * 256], preferred_element_type=jnp.float32
        )

    def put(image, k, begin, value):
        store = (lf, rf)[image]
        edge = origin[image]
        end = begin + value.shape[0]
        if begin < edge:
            store[k, begin:edge, :] = value[: edge - begin, :] * left_ok
            value, begin = value[edge - begin :, :], edge
        if image == 0 and end > 8 + cols:
            store[k, 8 + cols : end, :] = value[8 + cols - begin :, :] * right_ok
            value = value[: 8 + cols - begin, :]
        store[k, begin : begin + value.shape[0], :] = value

    def place_lines(image, place):
        half = 2 * cin
        block = jnp.concatenate(
            [
                lines[side, place, image * half : (image + 1) * half, :].astype(jnp.float32)
                for side in range(2)
            ]
            * 3
            + [jnp.zeros((128 - 6 * half, cols), jnp.float32)],
            axis=0,
        ).T
        at = 8 + base
        if place == 0:
            keep = reach if image else 16
            at, block = at - keep, block[cols - keep :, :]
        elif place == 2:
            at, block = at + cols, block[:16, :]
        for step_x in range(3):
            begin = at + 1 - step_x
            some = slice(step_x * 2 * half, (step_x + 1) * 2 * half)
            ext[image, begin : begin + block.shape[0], some] = block[:, some]

    def build_right(k, begin, count):
        for delta in range(-2, 3):
            at = lead - D + delta + begin
            right_m[k, begin : begin + count, (delta + 2) * 128 : (delta + 3) * 128] = (
                rf[k, at : at + count, :].astype(jnp.bfloat16)
            )

    def build_left(k, chunks):
        for chunk in chunks:
            at = 7 + chunk * 16
            shifted = [lf[k, at + c : at + c + 16, :].reshape(2, 8, 128) for c in range(3)]
            for odd in range(2):
                for delta in range(-2, 3):
                    value = None
                    for c in range(3):
                        a = c - delta
                        if 0 <= a < 3:
                            term = shifted[c] * band_w[(a * 3 + c) * 2 + odd]
                            value = term if value is None else value + term
                    left_m[
                        k,
                        odd * cols + chunk * 16 : odd * cols + chunk * 16 + 16,
                        (delta + 2) * 128 : (delta + 3) * 128,
                    ] = value.reshape(16, 128).astype(jnp.bfloat16)

    def end_product(k, d, x, count):
        return lf[k, 8 + x : 8 + x + count, :] * rf[k, lead + x - d : lead + x - d + count, :]

    def build_ends(where, k):
        if k not in once:
            return
        columns = slice(once.index(k) * 128, (once.index(k) + 1) * 128)
        gap = jnp.zeros((8, 128), jnp.float32)
        for j, d in enumerate((0, 1, D - 2, D - 1)):
            reached = 16 if j < 2 else D + 16
            if where == 2:
                x, count = reached, cols - 16 - reached
            elif where == 0:
                x, count = 0, reached
                block = jnp.concatenate([gap, end_product(k, d, -8, 8)], axis=0)
                end_in[j, 0:16, columns] = block.astype(jnp.bfloat16)
            else:
                x, count = cols - 16, 16
                block = jnp.concatenate([end_product(k, d, cols, 8), gap], axis=0)
                end_in[j, 16 + cols :, columns] = block.astype(jnp.bfloat16)
            end_in[j, 16 + x : 16 + x + count, columns] = end_product(k, d, x, count).astype(jnp.bfloat16)

    chunks = cols // 16
    inner = len(inner_pairs) // 2
    strips = (((1, 0, lead + 8), (0, 0, 16)), ((1, span - 16, 16), (0, wide_l - 16, 16)))

    def own_columns(pairs_in, n, depth):
        for image in range(2):
            first = origin[image] + 8
            total = convolve(lhs[image, first : first + local, :depth], n, depth)
            for j, k in enumerate(pairs_in):
                put(image, k, first, finish(total, j, k, image))
        for k in pairs_in:
            build_right(k, D + 16, cols - 32)
            build_left(k, range(1, chunks - 1))
            build_ends(2, k)

    def other_columns(sides, pairs_in, n, depth):
        some = [strip for side in sides for strip in strips[side]]
        rows_in = jnp.concatenate(
            [lhs[image, first : first + count, :depth] for image, first, count in some], axis=0
        )
        total = convolve(rows_in, n, depth)
        for j, k in enumerate(pairs_in):
            at = 0
            for image, first, count in some:
                put(image, k, first, finish(total[at : at + count, :], j, k, image))
                at += count
        for k in pairs_in:
            if 0 in sides:
                build_right(k, 0, D + 16)
                build_left(k, [0])
            if 1 in sides:
                build_right(k, D + cols - 16, 16)
                build_left(k, [chunks - 1])
            for side in sides:
                build_ends(side, k)

    def columns_in(side):
        if side == 0:
            pt[1, base - reach : base, :] = near1[...].astype(jnp.float32)
            pt[0, base - 16 : base, :] = near0[...].astype(jnp.float32)
        else:
            pt[:, base + cols : base + cols + 16, :] = far[...].astype(jnp.float32)
        for image, first, count in strips[side]:
            gather(image, first, count)

    def corners_in(side):
        for image in range(2):
            place_lines(image, 2 * side)
        for image, first, count in strips[side]:
            gather_lines(image, first, count)

    def inner_columns(sides):
        for n in range(inner):
            other_columns(sides, inner_pairs[2 * n : 2 * n + 2], n, 3 * main)

    def outer_columns(sides):
        other_columns(sides, outer_pairs, inner, 3 * main + 128)

    low_lane = lax.broadcasted_iota(jnp.int32, (D, cols), 1) < D
    lane8 = lax.broadcasted_iota(jnp.int32, (8, cols), 1)
    from_x = (lane8 - lax.broadcasted_iota(jnp.int32, (8, cols), 0)).astype(jnp.float32)
    jump = jnp.where(lane8 < D, float(D), -float(D))

    def attend(k):
        score = lax.dot_general(right_m[k], left_m[k], nt, preferred_element_type=jnp.float32)
        for odd in range(2):
            mine = slice(odd * cols, (odd + 1) * cols)
            outer = jnp.where(low_lane, score[:D, mine], score[2 * D :, mine]) + mask[0]
            inner = score[D : 2 * D, mine] + mask[1]
            outer = outer.reshape(D // 8, 8, cols)
            inner = inner.reshape(D // 8, 8, cols)
            best = jnp.maximum(jnp.max(outer, axis=0), jnp.max(inner, axis=0))
            outer = jnp.exp2(outer - best)
            both = outer + jnp.exp2(inner - best)
            tail, steps = both[D // 8 - 1], None
            for j in range(D // 8 - 2, -1, -1):
                steps = tail if steps is None else steps + tail
                tail = tail + both[j]
            moment = from_x * tail - 8.0 * steps + jump * jnp.sum(outer, axis=0)
            y = 2 * k + odd
            for j, value in enumerate((best, tail, moment)):
                part[j, y * 8 : (y + 1) * 8, :] = value

    strip_rows = D + 16
    lane_s = lax.broadcasted_iota(jnp.int32, (strip_rows, 32), 1) % 16
    apart_s = lane_s + D - lax.broadcasted_iota(jnp.int32, (strip_rows, 32), 0)
    within_s = (apart_s >= 1) & (apart_s <= D - 2)
    from_s = apart_s[:8].astype(jnp.float32)

    def attend_strip(k):
        columns = jnp.concatenate([left_m[k, cols - 16 : cols, :], left_m[k, 2 * cols - 16 :, :]], axis=0)
        score = lax.dot_general(
            right_m[k, D + cols - strip_rows :, :], columns, nt, preferred_element_type=jnp.float32
        )
        score = jnp.where(within_s, score, -jnp.inf).reshape(strip_rows // 8, 8, 32)
        best = jnp.max(score, axis=0)
        weight = jnp.exp2(score - best)
        tail, steps = weight[strip_rows // 8 - 1], None
        for j in range(strip_rows // 8 - 2, -1, -1):
            steps = tail if steps is None else steps + tail
            tail = tail + weight[j]
        moment = from_s * tail - 8.0 * steps
        for j, value in enumerate((best, tail, moment)):
            at = (j * pairs + k) * 8
            strip_out[at : at + 8, :32] = value
            value = strip_out[at : at + 8, :]
            part[j, 16 * k : 16 * k + 8, cols - 16 :] = pltpu.roll(value, cols - 16, 1)[:, cols - 16 :]
            part[j, 16 * k + 8 : 16 * k + 16, cols - 16 :] = pltpu.roll(value, cols - 32, 1)[:, cols - 16 :]

    def send_later(order):
        for step in order:
            n = later.index(step)

            @pl.when(exists(step))
            def _(n=n):
                pl.semaphore_wait(ready.at[(0, 2, 1)[n]], 1)

            send(lambda other: other == step)

    def send_beside():
        @pl.when(odd_row & (tall > 1))
        def _():
            pl.semaphore_wait(ready.at[3], tall - 1)

        @pl.when(odd_row)
        def _():
            send(lambda step: step in beside)

    def send_all_later():
        @pl.when(even_row)
        def _():
            send_later(later[1:] + later[:1])

        @pl.when(odd_row)
        def _():
            send_later(later)

    def send_rest():
        send_beside()
        send_all_later()

    root = (my_col == 0) & (my_row < 2) & (lax.axis_index("pairs") == 0)

    @pl.when(my_col > 0)
    def _():
        send_rest()

    for image in range(2):
        gather(image, origin[image] + 8, local)
    for n in range(inner):
        own_columns(inner_pairs[2 * n : 2 * n + 2], n, 3 * main)

    @pl.when((my_col == 0) & jnp.logical_not(root))
    def _():
        send_rest()

    @pl.when(my_col == 0)
    def _():
        columns_in(0)
        inner_columns([0])
        for k in inner_pairs:
            attend(k)

    @pl.when(root)
    def _():
        send_beside()

    half_lane = lax.broadcasted_iota(jnp.int32, (128, 128), 1) < 64
    behind = line - lax.broadcasted_iota(jnp.int32, tile, 0)
    for t, k in enumerate(once):
        hit = [behind == step_y - 2 * k for step_y in range(3)]
        if k == 0:
            hit = [h & (line < 2) for h in hit]
        taps = []
        for step_d in range(3):
            pieces = []
            for step_x in range(3):
                value = jnp.zeros(tile, jnp.float32)
                for step_y in range(3):
                    at = 9 * step_d + 3 * step_y + step_x
                    value = jnp.where(hit[step_y], agg[at : at + 1, :], value)
                pieces.append(value)
            taps.append(pieces)
        gap = [jnp.zeros(tile, jnp.float32)]
        for j, (low_d, high_d) in enumerate(((1, 1), (2, 0))):
            value = jnp.concatenate(taps[low_d] + gap + taps[high_d] + gap, axis=0).T
            for n, keep in ((j, half_lane), (3 - j, jnp.logical_not(half_lane))):
                end_w[n, t * 128 : (t + 1) * 128, :] = jnp.where(keep, value, 0.0).astype(jnp.bfloat16)

    @pl.when(root)
    def _():
        send_all_later()

    tiles = len(once) - len(outer_pairs)

    def sum_ends(columns, where=slice(None)):
        total = None
        for j in range(4):
            term = jnp.dot(
                end_in[j, where, columns], end_w[j, columns, :], preferred_element_type=jnp.float32
            )
            total = term if total is None else total + term
        return total

    def sum_inner_ends():
        end_sum[...] = sum_ends(slice(0, tiles * 128))

    def sum_outer_ends():
        end_sum[...] += sum_ends(slice(tiles * 128, len(once) * 128))
        spread_ends()

    def spread_ends():
        place = lax.broadcasted_iota(jnp.int32, (cols, 128), 1) % 64 // 16
        total = end_sum[15 : 15 + cols, :]
        for step_x in (1, 2):
            total = jnp.where(place == step_x, end_sum[15 + step_x : 15 + step_x + cols, :], total)
        total = total.T
        for n, j in enumerate((0, 64)):
            ends[n] = total[j : j + 16, :] + total[j + 16 : j + 32, :] + total[j + 32 : j + 48, :]

    @pl.when(my_col == 0)
    def _():
        sum_inner_ends()

    receive(lambda step: step[1] == 0)
    for image in range(2):
        place_lines(image, 1)
        gather_lines(image, origin[image] + 8, local)
    own_columns(outer_pairs, inner, 3 * main + 128)

    @pl.when(my_col == 0)
    def _():
        corners_in(0)

    def staged(sides, do):
        receive(lambda step: step[0] == 0)
        for side in sides:
            columns_in(side)
        inner_columns(sides)
        sum_inner_ends()
        for k in inner_pairs:
            do(k)
        receive(lambda step: step[0] != 0 and step[1] != 0)
        for side in sides:
            corners_in(side)
        outer_columns(sides)
        sum_outer_ends()
        for k in outer_pairs:
            do(k)

    @pl.when(my_col == 0)
    def _():
        receive(lambda step: step[1] != 0)
        columns_in(1)
        corners_in(1)
        inner_columns([1])
        outer_columns([0, 1])
        end_sum[cols:, :] = sum_ends(slice(0, tiles * 128), slice(cols, cols + 32))
        sum_outer_ends()
        for k in inner_pairs:
            attend_strip(k)
        for k in outer_pairs:
            attend(k)

    @pl.when((my_col > 0) & odd_row)
    def _():
        staged([0, 1], attend)

    @pl.when((my_col > 0) & even_row)
    def _():
        receive(lambda step: step[1] == -1)
        columns_in(1)
        corners_in(1)
        inner_columns([1])
        outer_columns([1])
        receive(lambda step: step[1] == 1)
        columns_in(0)
        corners_in(0)
        inner_columns([0])
        outer_columns([0])
        sum_inner_ends()
        sum_outer_ends()
        for k in range(pairs):
            attend(k)

    for h in range(rows // 8):
        first = ends[0, h * 8 : (h + 1) * 8, :]
        last = ends[1, h * 8 : (h + 1) * 8, :]
        tops = [part[0, pl.ds(h * 64 + j, 8, stride=8), :] for j in range(8)]
        best = jnp.maximum(first, last)
        for top in tops:
            best = jnp.maximum(best, top)
        last = jnp.exp2(last - best)
        total = jnp.exp2(first - best) + last
        moment = last * float(D - 1)
        for j in range(8):
            weight = jnp.exp2(tops[j] - best)
            total = total + weight * part[1, pl.ds(h * 64 + j, 8, stride=8), :]
            moment = moment + weight * part[2, pl.ds(h * 64 + j, 8, stride=8), :]
        out_ref[h * 8 : (h + 1) * 8, :] = moment / total / D

    for step, copy in copies:

        @pl.when(exists(step))
        def _(copy=copy):
            copy.wait_send()


def on_device(images, conv_weight, conv_bias, agg_weight):
    cin, rows, cols = images.shape[1:]
    groups = agg_weight.shape[0]
    per = conv_weight.shape[0] // groups
    main = rows * cin
    pairs = rows // 2
    span = cols + D + 16
    reach = -(-(D + 2) // 16) * 16
    return pl.pallas_call(
        functools.partial(body, (rows, cols, groups, per, cin)),
        out_shape=pltpu.VMEM((rows, cols), jnp.float32),
        in_specs=[pl.BlockSpec(memory_space=pl.ANY)] * 4,
        out_specs=pl.BlockSpec(memory_space=pltpu.VMEM),
        scratch_shapes=[
            pltpu.VMEM(images.shape, images.dtype),
            pltpu.VMEM(conv_weight.shape, conv_weight.dtype),
            pltpu.VMEM((1,) + conv_bias.shape, conv_bias.dtype),
            pltpu.VMEM(agg_weight.shape, agg_weight.dtype),
            pltpu.SemaphoreType.DMA((7,)),
            pltpu.VMEM((2, span + 16, main), jnp.float32),
            pltpu.VMEM((2, span + 32, 128), jnp.float32),
            pltpu.VMEM((2, span, 3 * main + 128), jnp.bfloat16),
            pltpu.VMEM((3 * main + 128, pairs * 128), jnp.bfloat16),
            pltpu.VMEM((4, (pairs // 2 + 1) * 128, 128), jnp.bfloat16),
            pltpu.VMEM((4, cols + 32, (pairs // 2 + 1) * 128), jnp.bfloat16),
            pltpu.VMEM((cols + 32, 128), jnp.float32),
            pltpu.VMEM((2, rows, cols), jnp.float32),
            pltpu.VMEM((9 * cin, 128), jnp.float32),
            pltpu.VMEM((18, 8, 128), jnp.float32),
            pltpu.VMEM((2, D, cols), jnp.float32),
            pltpu.VMEM((pairs, cols + 16, 128), jnp.float32),
            pltpu.VMEM((pairs, span, 128), jnp.float32),
            pltpu.VMEM((pairs, 2 * cols, 640), jnp.bfloat16),
            pltpu.VMEM((pairs, D + cols, 640), jnp.bfloat16),
            pltpu.VMEM((3, rows * 8, cols), jnp.float32),
            pltpu.VMEM((3 * pairs * 8, 128), jnp.float32),
            pltpu.VMEM((2, cols, main), jnp.bfloat16),
            pltpu.VMEM((2, 4 * cin, cols), jnp.bfloat16),
            pltpu.VMEM((16, main), jnp.bfloat16),
            pltpu.VMEM((reach, main), jnp.bfloat16),
            pltpu.VMEM((2, 16, main), jnp.bfloat16),
            pltpu.VMEM((2, 3, 4 * cin, cols), jnp.bfloat16),
            pltpu.SemaphoreType.DMA((9,)),
            pltpu.SemaphoreType.DMA((9,)),
            pltpu.SemaphoreType.REGULAR((4,)),
        ],
        compiler_params=pltpu.CompilerParams(collective_id=0, has_side_effects=True),
    )(images, conv_weight, conv_bias[None], agg_weight)


def solution(mesh):
    in_specs = (P("pairs", None, "row", "col"), P(), P(), P())
    out_specs = P(("pairs", "row"), "col")
    return jax.shard_map(
        on_device, mesh=mesh, in_specs=in_specs, out_specs=out_specs, check_vma=False
    )
```
